32 devices in a mesh: strip: 2 (over x), ra: 16 (over z, y, core).
Axes of the slice: x: 2, y: 2, z: 4, core: 2. Of those that a mesh axis runs over, the one named last changes fastest.
Arguments:
- vis: bfloat16 [4, 32, 2048, 512], P(None, 'strip', 'ra'), parts along dimension 1, may hold values from -16 to 16
- beams: bfloat16 [4, 32, 16, 128], P(None, 'strip'), parts along dimension 1, may hold values from 0.19921875 to 1
- m_ra: bfloat16 [128, 512], replicated, may hold values from -0.25 to 0.25
- m_dec: bfloat16 [16, 16], replicated, may hold values from -0.75 to 0.75
- facet_of: int32 [4096, 1], P(('strip', 'ra')), parts along dimension 0, may hold values from 0 to 15; in each aligned block of 128 rows (0 to 127, 128 to 255, ...) at most 16 rows name the same one
- tile_of: int32 [4096], P(('strip', 'ra')), parts along dimension 0, may hold values from 0 to 1
- beam_of: int32 [4096], P(('strip', 'ra')), parts along dimension 0, may hold values from 0 to 15
- step_size: float32 [4], replicated, may hold values from 0.05 to 0.2
- thresholds: float32 [4, 4], replicated, may hold values from 0.5 to 5
Outputs:
- image: float32 [4, 32, 4096], P(None, 'strip', 'ra'), parts along dimension 1
The draws below stay inside these ranges and needn't reach their ends.
There are 2 independent parts, one for each index of `strip`. The reference program is written for one: setup_inputs(seed, part) draws one part's arguments, and reference() takes and returns one part's arrays. A program takes and returns all parts, laid end to end along the dimension named above; an argument that names none is the same for every part. Nothing has to cross between parts.
Inputs may be any that keep to these rules, and one draw needn't show every extreme that they name: `facet_of`: among the pointings of one device (aligned blocks of 128 rows) no facet is named more than 16 times, a bound that some block reaches.
All inputs are finite; a program needn't handle non-finite values.
Results may differ from the reference program's by a relative error of at most 0.0058.
The reference program's roundings to bfloat16 on the way (of `first_residual`, `dec_back`, `patch_grad`, `image_tiles`, `weighted`, `along_ra` and `second_residual`) count: a program that leaves them out, or rounds other values in their place, can miss the bound.
Values may be sent and summed in bfloat16 or wider, within the bound.
No kernel may reach another device: no remote copies, remote signals or barrier semaphores. Data moves between devices by JAX's collectives and lax.ppermute only.
A program may use at most 128 MiB of HBM per device.

```python
import math
import jax
import jax.numpy as jnp
import numpy as np
from jax import lax

C = 4
BASES = 4
TW = 128
NB = 16
DEC = 16
RA_DEV = 256
PNT_DEV = 128
K = 512
TILES_DEV = 2
CAP = 16
POINTINGS = 2048
N_RA = 16


def set_ends(values, stream_key, smallest, top_value):
    longest = values.shape.index(max(values.shape))
    spots = []
    for shift in (0, 1):
        where = [jax.random.randint(jax.random.fold_in(stream_key, axis), (), 0, length) for axis, length in enumerate(values.shape)]
        where[longest] = (where[longest] + shift) % values.shape[longest]
        spots.append(tuple(where))
    return values.at[spots[0]].set(smallest).at[spots[1]].set(top_value)


def block_scale(stream_key, shape, cuts, smallest, high):
    level = 1.0
    for dim, shards_of in cuts:
        heights = jax.random.uniform(jax.random.fold_in(jax.random.fold_in(stream_key, 6), dim), (shards_of,), jnp.float32, smallest / len(cuts), high / len(cuts))
        level = level * jnp.repeat(jnp.exp(heights), shape[dim] // shards_of).reshape((-1,) + (1,) * (len(shape) - 1 - dim))
    return level


def deal_out(stream_key, own, number, rows, number_of, top, reach, skew):
    sequence = jax.random.permutation(stream_key, number_of)
    crowded, usual = load_shares(number_of, rows * top, reach, skew, True), load_shares(number_of, rows * top, reach, skew, False)
    places = jnp.arange(number_of)

    def named(sizes, turn):
        used = int((sizes > 0).sum())
        fixed = max(1, used // 4)
        passed = fixed + (places - fixed + turn * (used - fixed)) % max(1, number_of - fixed)
        return jnp.zeros((number_of,), jnp.int32).at[sequence[jnp.where(places < fixed, places, passed)]].set(jnp.asarray(sizes, jnp.int32))

    sizes = jnp.where(number % 4 == 0, named(crowded, number // 4), named(usual, number - number // 4 - 1))
    mixed = jax.random.permutation(jax.random.fold_in(own, 3), number_of)
    giver, receiver = mixed[0:number_of // 2 * 2:2], mixed[1:number_of // 2 * 2:2]
    slack = jnp.minimum(sizes[giver] - 1, reach - sizes[receiver]) // 2
    slack = jnp.where((giver == sequence[0]) | (receiver == sequence[0]) | (sizes[receiver] == 0), 0, jnp.maximum(slack, 0))
    passed = jax.random.randint(jax.random.fold_in(own, 4), (number_of // 2,), 0, 1 << 20) % (slack + 1)
    sizes = sizes.at[giver].add(-passed).at[receiver].add(passed)
    labels = jnp.searchsorted(jnp.cumsum(sizes), jnp.arange(rows * top), side="right").astype(jnp.int32)
    grid = labels.reshape(top, rows).T
    grid = grid[jax.random.permutation(jax.random.fold_in(own, 1), rows)]
    turn = jax.random.randint(jax.random.fold_in(own, 2), (rows, 1), 0, top)
    return jnp.take_along_axis(grid, (jnp.arange(top)[None, :] + turn) % top, axis=1)


def load_shares(number_of, total, most, lean, full):
    loads = [(1 << 20) // math.isqrt(rank ** lean) + 1 for rank in range(1, number_of + 1)]
    largest = most if full else min(most, max(-(-total // number_of), total * loads[0] // sum(loads)))
    least = 1 if total - largest >= number_of - 1 else 0
    given, spare = [largest] + [least] * (number_of - 1), total - largest - least * (number_of - 1)
    while spare > 0:
        free = [i for i in range(1, number_of) if given[i] < largest] or [i for i in range(1, number_of) if given[i] < most]
        whole, left = sum([loads[i] for i in free]), spare
        for i in free:
            extra = min(most - given[i], max(1, left * loads[i] // whole), spare)
            given[i] = given[i] + extra
            spare = spare - extra
    return np.array(given)


def centred(own_key, shape, width, most, pieces=(), dtype=jnp.bfloat16):
    array = jax.random.normal(own_key, shape, jnp.float32) * width
    if len(pieces) > 0:
        array = block_scale(own_key, shape, pieces, -0.22, 0.18) * array
    return jnp.clip(array, min=-most, max=most).astype(dtype)


def setup_inputs(seed: int = 0, part: int = 0) -> dict:
    seeds = jax.random.split(jax.random.key(seed), 10)
    own_keys = jax.random.split(jax.random.fold_in(seeds[9], part), 10)
    vis = centred(own_keys[0], (C, DEC, POINTINGS, K), 4.0, 16.0, ((2, 16),))
    beams = jnp.clip(jax.random.uniform(own_keys[1], (C, DEC, NB, TW), jnp.float32, 0.19921875, 1.0), 0.19921875, 1.0).astype(jnp.bfloat16)
    m_ra = centred(seeds[2], (TW, K), K ** -0.5, 0.25)
    m_dec = centred(seeds[3], (DEC, DEC), (4 * DEC) ** -0.5, 0.75)
    facet_of_keys = jax.random.split(jax.random.fold_in(own_keys[4], 1), POINTINGS // PNT_DEV)
    facet_of_turns = jax.random.permutation(jax.random.fold_in(own_keys[4], 3), POINTINGS // PNT_DEV)
    facet_of = jax.vmap(lambda own, number: deal_out(jax.random.fold_in(own_keys[4], 2), own, number, PNT_DEV, N_RA, 1, CAP, 2))(facet_of_keys, facet_of_turns).reshape((POINTINGS, 1))
    tile_of = set_ends(jax.random.randint(own_keys[5], (POINTINGS,), 0, TILES_DEV), jax.random.fold_in(own_keys[5], 1), 0, TILES_DEV - 1).astype(jnp.int32)
    beam_of = set_ends(jax.random.randint(own_keys[6], (POINTINGS,), 0, NB), jax.random.fold_in(own_keys[6], 1), 0, NB - 1).astype(jnp.int32)
    step_size = jnp.clip(jnp.exp(jax.random.uniform(seeds[7], (C,), jnp.float32, math.log(0.05), math.log(0.2))), 0.05, 0.2)
    thresholds = jnp.clip(jnp.exp(jax.random.uniform(seeds[8], (BASES, C), jnp.float32, math.log(0.5), math.log(5.0))), 0.5, 5.0)
    return dict(vis=vis, beams=beams, m_ra=m_ra, m_dec=m_dec, facet_of=facet_of, tile_of=tile_of, beam_of=beam_of, step_size=step_size, thresholds=thresholds)


daub_coeffs = (
    (0.7071067811865476, 0.7071067811865476),
    (0.48296291314453416, 0.8365163037378079, 0.22414386804201339, -0.12940952255126037),
    (0.3326705529500825, 0.8068915093110924, 0.4598775021184914, -0.1350110200102546, -0.0854412738820267, 0.0352262918857095),
    (0.2303778133088964, 0.7148465705529154, 0.6308807679298587, -0.0279837694168599, -0.1870348117190931, 0.0308413818355607, 0.0328830116668852, -0.0105974017850690),
)


def filter_table(basis_count):
    low_pass = np.zeros((basis_count, 8))
    for basis_id in range(basis_count):
        coeffs = daub_coeffs[basis_id]
        low_pass[basis_id, :len(coeffs)] = coeffs
    high_pass = np.zeros((basis_count, 8))
    for column in range(8):
        high_pass[:, column] = ((-1.0) ** column) * low_pass[:, 7 - column]
    return jnp.asarray(low_pass, jnp.float32), jnp.asarray(high_pass, jnp.float32), low_pass, high_pass


def dec_table(low_pass, high_pass, length):
    basis_count = low_pass.shape[0]
    half_size = length // 2
    matrix = np.zeros((basis_count, length, length))
    for basis_id in range(basis_count):
        for row_index in range(half_size):
            for column in range(8):
                target = (2 * row_index + column) % length
                matrix[basis_id, row_index, target] += low_pass[basis_id, column]
                matrix[basis_id, half_size + row_index, target] += high_pass[basis_id, column]
    return jnp.asarray(matrix, jnp.float32)


def taps(table, column):
    return table[:, column].reshape(-1, 1, 1, 1)


def ra_analysis(signal, tail, low_pass, high_pass):
    extended = jnp.concatenate([signal, tail], axis=-1)
    evens = extended[..., 0::2]
    odds = extended[..., 1::2]
    length = signal.shape[-1] // 2
    lower = jnp.float32(0.0)
    upper = jnp.float32(0.0)
    for tap_pair in range(4):
        even_part = evens[..., tap_pair:tap_pair + length]
        odd_part = odds[..., tap_pair:tap_pair + length]
        lower = lower + taps(low_pass, 2 * tap_pair) * even_part + taps(low_pass, 2 * tap_pair + 1) * odd_part
        upper = upper + taps(high_pass, 2 * tap_pair) * even_part + taps(high_pass, 2 * tap_pair + 1) * odd_part
    return lower, upper


def ra_synthesis(lower, upper, head_low, head_high, low_pass, high_pass):
    ext_low = jnp.concatenate([head_low, lower], axis=-1)
    ext_high = jnp.concatenate([head_high, upper], axis=-1)
    length = lower.shape[-1]
    evens = jnp.float32(0.0)
    odds = jnp.float32(0.0)
    for tap_pair in range(4):
        low_slice = ext_low[..., 3 - tap_pair:3 - tap_pair + length]
        high_slice = ext_high[..., 3 - tap_pair:3 - tap_pair + length]
        evens = evens + taps(low_pass, 2 * tap_pair) * low_slice + taps(high_pass, 2 * tap_pair) * high_slice
        odds = odds + taps(low_pass, 2 * tap_pair + 1) * low_slice + taps(high_pass, 2 * tap_pair + 1) * high_slice
    return jnp.stack([evens, odds], axis=-1).reshape(lower.shape[:-1] + (2 * length,))


def dec_apply(matrix, values):
    return jnp.einsum("qed,qcdn->qcen", matrix, values, precision=lax.Precision.HIGHEST)


def dec_adjoint(matrix, values):
    return jnp.einsum("qde,qcdn->qcen", matrix, values, precision=lax.Precision.HIGHEST)


def shrink(values, limits):
    return jnp.sign(values) * jnp.maximum(jnp.abs(values) - limits, 0.0)


def prox_image(field, limits, low_pass, high_pass, first_table, second_table):
    half_rows = field.shape[1] // 2
    bound = limits[:, :, None, None]
    low_one, high_one = ra_analysis(field[None], field[None, :, :, :6], low_pass, high_pass)
    coarse_a = dec_apply(first_table, low_one)
    coarse_b = shrink(dec_apply(first_table, high_one), bound)
    smooth = coarse_a[:, :, :half_rows]
    detail = shrink(coarse_a[:, :, half_rows:], bound)
    low_two, high_two = ra_analysis(smooth, smooth[..., :6], low_pass, high_pass)
    fine_a = shrink(dec_apply(second_table, low_two), bound)
    fine_b = shrink(dec_apply(second_table, high_two), bound)
    back_low = dec_adjoint(second_table, fine_a)
    back_high = dec_adjoint(second_table, fine_b)
    smooth_new = ra_synthesis(back_low, back_high, back_low[..., -3:], back_high[..., -3:], low_pass, high_pass)
    merged = jnp.concatenate([smooth_new, detail], axis=2)
    top_low = dec_adjoint(first_table, merged)
    top_high = dec_adjoint(first_table, coarse_b)
    rebuilt = ra_synthesis(top_low, top_high, top_low[..., -3:], top_high[..., -3:], low_pass, high_pass)
    return jnp.maximum(jnp.mean(rebuilt, axis=0), 0.0)


def reference(vis, beams, m_ra, m_dec, facet_of, tile_of, beam_of, step_size, thresholds):
    channels, dec_rows, total_points, samples = vis.shape
    patch_width = m_ra.shape[0]
    tile_count = RA_DEV // patch_width
    all_tiles = tile_count * N_RA
    patch_of = (facet_of[:, 0] * tile_count + tile_of).astype(jnp.int32)
    low_pass, high_pass, low_np, high_np = filter_table(BASES)
    first_table = dec_table(low_np, high_np, dec_rows)
    second_table = dec_table(low_np, high_np, dec_rows // 2)
    limits = thresholds * step_size[None, :]
    ra_mat = m_ra.astype(jnp.float32)
    dec_mat = m_dec.astype(jnp.float32)

    def gradient_from(make_residual):
        def one_block(block_id, total):
            first = (block_id * PNT_DEV).astype(jnp.int32)
            tile_ids = lax.dynamic_slice_in_dim(patch_of, first, PNT_DEV)
            beam_ids = lax.dynamic_slice_in_dim(beam_of, first, PNT_DEV)
            beam_block = jnp.take(beams, beam_ids, axis=2).astype(jnp.float32)
            vis_block = lax.dynamic_slice_in_dim(vis, first, PNT_DEV, axis=2)
            residual = make_residual(vis_block, tile_ids, beam_block)
            dec_back = jnp.einsum("ed,cepk->cdpk", dec_mat, residual.astype(jnp.float32)).astype(jnp.bfloat16)
            patches = jnp.einsum("cdpk,tk->cdpt", dec_back.astype(jnp.float32), ra_mat)
            patch_grad = (beam_block * patches).astype(jnp.bfloat16)
            return total.at[:, :, tile_ids, :].add(patch_grad.astype(jnp.float32))

        blank = jnp.zeros((channels, dec_rows, all_tiles, patch_width), jnp.float32)
        total = lax.fori_loop(0, N_RA, one_block, blank)
        return total.reshape(channels, dec_rows, all_tiles * patch_width)

    def first_residual(vis_block, tile_ids, beam_block):
        return -vis_block

    gradient = gradient_from(first_residual)
    first_image = prox_image(-step_size[:, None, None] * gradient, limits, low_pass, high_pass, first_table, second_table)
    image_tiles = first_image.astype(jnp.bfloat16).reshape(channels, dec_rows, all_tiles, patch_width)

    def second_residual(vis_block, tile_ids, beam_block):
        tiles = jnp.take(image_tiles, tile_ids, axis=2).astype(jnp.float32)
        weighted = (beam_block * tiles).astype(jnp.bfloat16)
        along_ra = jnp.einsum("cdpt,tk->cdpk", weighted.astype(jnp.float32), ra_mat).astype(jnp.bfloat16)
        predicted = jnp.einsum("ed,cdpk->cepk", dec_mat, along_ra.astype(jnp.float32))
        return (predicted - vis_block.astype(jnp.float32)).astype(jnp.bfloat16)

    gradient_two = gradient_from(second_residual)
    return prox_image(first_image - step_size[:, None, None] * gradient_two, limits, low_pass, high_pass, first_table, second_table)
```

```python
import functools

import jax
import jax.numpy as jnp
import numpy as np
from jax import lax
from jax.experimental import pallas as pl
from jax.experimental.pallas import tpu as pltpu
from jax.sharding import PartitionSpec as P

BASES = 4
RA_DEV = 256
GROUP = 16
PHASES = 4
LANES = 128
SPAN = LANES // PHASES
SLOTS = 3

daub_coeffs = (
    (0.7071067811865476, 0.7071067811865476),
    (0.48296291314453416, 0.8365163037378079, 0.2241438680420134, -0.12940952255126037),
    (
        0.3326705529500825,
        0.8068915093110924,
        0.4598775021184914,
        -0.1350110200102546,
        -0.0854412738820267,
        0.0352262918857095,
    ),
    (
        0.2303778133088964,
        0.7148465705529155,
        0.6308807679298587,
        -0.0279837694168599,
        -0.1870348117190931,
        0.0308413818355607,
        0.0328830116668852,
        -0.010597401785069,
    ),
)


def filter_table(basis_count):
    low_pass = np.zeros((basis_count, 8))
    for basis_id in range(basis_count):
        coeffs = daub_coeffs[basis_id]
        low_pass[basis_id, : len(coeffs)] = coeffs
    high_pass = np.zeros((basis_count, 8))
    for column in range(8):
        high_pass[:, column] = (-1.0) ** column * low_pass[:, 7 - column]
    return low_pass.astype(np.float32), high_pass.astype(np.float32)


def iota(shape, axis):
    return lax.broadcasted_iota(jnp.int32, shape, axis)


def where_equal(left, right):
    return jnp.where(left == right, 1.0, 0.0)


def dot(left, right, contract=((1,), (0,))):
    return lax.dot_general(left, right, (contract, ((), ())), preferred_element_type=jnp.float32)


def phase_rows(width):
    row, column = iota((width, width), 0), iota((width, width), 1)
    span = width // PHASES
    return where_equal(column, PHASES * (row % span) + row // span).astype(jnp.bfloat16)


def back_matrix(m_dec):
    size = GROUP * GROUP
    pick = where_equal(iota((size, GROUP), 0) % GROUP, iota((size, GROUP), 1)).astype(jnp.bfloat16)
    place = where_equal(iota((GROUP, size), 0), iota((GROUP, size), 1) // GROUP).astype(jnp.bfloat16)
    wide = dot(dot(pick, m_dec, ((1,), (1,))).astype(jnp.bfloat16), place)
    return (wide * where_equal(iota((size, size), 0) // GROUP, iota((size, size), 1) % GROUP)).astype(jnp.bfloat16)


def forward_matrix(m_dec):
    size = GROUP * GROUP
    pick = where_equal(iota((size, GROUP), 0) // GROUP, iota((size, GROUP), 1)).astype(jnp.bfloat16)
    place = where_equal(iota((GROUP, size), 0), iota((GROUP, size), 1) % GROUP).astype(jnp.bfloat16)
    wide = dot(dot(pick, m_dec).astype(jnp.bfloat16), place)
    return (wide * where_equal(iota((size, size), 0) % GROUP, iota((size, size), 1) // GROUP)).astype(jnp.bfloat16)


def swap_rows(size_a, size_b):
    size = size_a * size_b
    row, column = iota((size, size), 0), iota((size, size), 1)
    return where_equal((row % size_a) * size_b + row // size_a, column).astype(jnp.bfloat16)


def gradient_kernel(second, patch_ref, beam_ref, vis_ref, beams_ref, m_ra_ref, m_dec_ref, *refs):
    if second:
        tiles_ref, out_ref, back, forward, ra_out, ra_in, table, total = refs
    else:
        out_ref, back, ra_out, table, total = refs
    channel = pl.program_id(0)
    channels = pl.num_programs(0)
    dec_rows, owned = vis_ref.shape[1], vis_ref.shape[2]
    width = m_ra_ref.shape[0]
    beam_count = beams_ref.shape[2]
    facets = out_ref.shape[0]

    @pl.when(channel == 0)
    def _():
        back[...] = back_matrix(m_dec_ref[...])
        order = phase_rows(width)
        ra_out[...] = dot(m_ra_ref[...], order, ((0,), (1,))).astype(jnp.bfloat16)
        if second:
            forward[...] = forward_matrix(m_dec_ref[...])
            ra_in[...] = dot(order, m_ra_ref[...]).astype(jnp.bfloat16)

    rows = beams_ref[0].reshape(dec_rows * beam_count, width)
    swapped = dot(swap_rows(dec_rows, beam_count), rows).astype(jnp.bfloat16)
    table[...] = (
        dot(swapped, phase_rows(width), ((1,), (1,)))
        .astype(jnp.bfloat16)
        .reshape(beam_count, dec_rows, width)
    )
    total[...] = jnp.zeros_like(total)

    def one_group(group, carry):
        first = pl.multiple_of(group * GROUP, GROUP)
        data = vis_ref[0, :, pl.ds(first, GROUP), :].reshape(dec_rows * GROUP, vis_ref.shape[3])
        patch_ids = [patch_ref[first + p] for p in range(GROUP)]
        slabs = [table[beam_ref[first + p]].astype(jnp.float32) for p in range(GROUP)]
        if second:
            weighted = jnp.concatenate(
                [
                    (slabs[p] * tiles_ref[patch_ids[p] * channels + channel].astype(jnp.float32)).astype(
                        jnp.bfloat16
                    )
                    for p in range(GROUP)
                ],
                axis=0,
            )
            along_ra = dot(weighted, ra_in[...]).astype(jnp.bfloat16)
            predicted = dot(forward[...], along_ra)
            data = (predicted - data.astype(jnp.float32)).astype(jnp.bfloat16)
        dec_back = dot(back[...], data).astype(jnp.bfloat16)
        patches = dot(dec_back, ra_out[...])
        for p in range(GROUP):
            patch = patches[p * dec_rows : (p + 1) * dec_rows]
            patch_grad = (slabs[p] * patch).astype(jnp.bfloat16).astype(jnp.float32)
            total[patch_ids[p]] = total[patch_ids[p]] + patch_grad
        return carry

    lax.fori_loop(0, owned // GROUP, one_group, 0)
    from_left = iota((dec_rows, width), 1) % SPAN >= SPAN // 2
    tiles = total.shape[0]

    def one_facet(facet, carry):
        own = 2 * facet
        left, right = lax.rem(own + tiles - 1, tiles), lax.rem(own + 2, tiles)
        out_ref[facet, 0, 0] = total[own].astype(jnp.bfloat16)
        out_ref[facet, 1, 0] = total[own + 1].astype(jnp.bfloat16)
        out_ref[facet, 2, 0] = jnp.where(from_left, total[left], total[right]).astype(jnp.bfloat16)
        return carry

    lax.fori_loop(0, facets, one_facet, 0)


def gradient_call(patch_of, beam_of, vis, beams, m_ra, m_dec, facets, tiles=None):
    channels, dec_rows, owned, samples = vis.shape
    width = m_ra.shape[0]
    beam_count = beams.shape[2]
    second = tiles is not None
    whole = lambda c, *_: (0, 0)
    in_specs = [
        pl.BlockSpec((1, dec_rows, owned, samples), lambda c, *_: (c, 0, 0, 0)),
        pl.BlockSpec((1, dec_rows, beam_count, width), lambda c, *_: (c, 0, 0, 0)),
        pl.BlockSpec(m_ra.shape, whole),
        pl.BlockSpec(m_dec.shape, whole),
    ]
    operands = [vis, beams, m_ra, m_dec]
    size = GROUP * GROUP
    back = pltpu.VMEM((size, size), jnp.bfloat16)
    ra_out = pltpu.VMEM((samples, width), jnp.bfloat16)
    ra_in = pltpu.VMEM((width, samples), jnp.bfloat16)
    tail = [
        pltpu.VMEM((beam_count, dec_rows, width), jnp.bfloat16),
        pltpu.VMEM((2 * facets, dec_rows, width), jnp.float32),
    ]
    if second:
        in_specs.append(pl.BlockSpec(tiles.shape, lambda c, *_: (0, 0, 0)))
        operands.append(tiles)
        scratch = [back, back, ra_out, ra_in] + tail
    else:
        scratch = [back, ra_out] + tail
    work = channels * owned * samples * dec_rows
    return pl.pallas_call(
        functools.partial(gradient_kernel, second),
        out_shape=jax.ShapeDtypeStruct((facets, SLOTS, channels, dec_rows, width), jnp.bfloat16),
        grid_spec=pltpu.PrefetchScalarGridSpec(
            num_scalar_prefetch=2,
            grid=(channels,),
            in_specs=in_specs,
            out_specs=pl.BlockSpec((facets, SLOTS, 1, dec_rows, width), lambda c, *_: (0, 0, c, 0, 0)),
            scratch_shapes=scratch,
        ),
        compiler_params=pltpu.CompilerParams(vmem_limit_bytes=48 << 20),
        cost_estimate=pl.CostEstimate(
            flops=(4 if second else 2) * 256 * work, bytes_accessed=2 * work, transcendentals=0
        ),
        name="second_gradient" if second else "first_gradient",
    )(patch_of, beam_of, *operands)


def shrink(values, bound):
    return values - jnp.clip(values, -bound, bound)


def combine(terms):
    total = None
    for factor, value in terms:
        if factor == 0.0:
            continue
        term = value * jnp.float32(factor)
        total = term if total is None else total + term
    return total


def dec_analysis(rows, low, high):
    count = len(rows)
    half = count // 2
    lows = [combine([(low[j], rows[(2 * k + j) % count]) for j in range(8)]) for k in range(half)]
    highs = [combine([(high[j], rows[(2 * k + j) % count]) for j in range(8)]) for k in range(half)]
    return lows + highs


def dec_synthesis(rows, low, high):
    count = len(rows)
    half = count // 2
    gathered = [[] for _ in range(count)]
    for k in range(half):
        for j in range(8):
            gathered[(2 * k + j) % count].append((low[j], rows[k]))
            gathered[(2 * k + j) % count].append((high[j], rows[half + k]))
    return [combine(terms) for terms in gathered]


def prox_kernel(second, recv_ref, thresholds_ref, step_ref, *refs):
    if second:
        first_ref, out_ref, summed, columns, natural = refs
    else:
        first_ref, out_ref, summed, columns, natural = refs
    sources, rows = recv_ref.shape[0], recv_ref.shape[1]
    dec_rows = first_ref.shape[1]
    channels = step_ref.shape[0]
    half = 4
    shape = (8, LANES)
    upper = iota(shape, 0) >= half
    channel = iota(shape, 0) % half
    lane = iota(shape, 1)
    block = lane // SPAN

    def add_source(source, total):
        return total + recv_ref[source].astype(jnp.float32)

    total = lax.fori_loop(1, sources, add_source, recv_ref[0].astype(jnp.float32))
    summed[:rows] = total
    summed[rows:] = total[rows - channels * dec_rows :]

    def spread(scalars):
        value = jnp.full(shape, scalars[channels - 1], jnp.float32)
        for c in range(channels - 1):
            value = jnp.where(channel == c, scalars[c], value)
        return value

    step = spread([step_ref[c] for c in range(channels)])
    roll = lambda value, shift: pltpu.roll(value, shift % LANES, 1)
    swap = lambda value: pltpu.roll(value, half, 0)
    halves = lambda low, high: jnp.where(upper, high, low)

    for d in range(dec_rows):
        own = summed[pl.ds(d, 8, stride=dec_rows), :]
        edge = summed[pl.ds(8 * dec_rows + d, 8, stride=dec_rows), :]
        other = swap(own)
        own_32, own_64 = roll(own, -32), roll(own, -64)
        other_up, other_64 = roll(other, 32), roll(other, -64)
        edge_32, edge_64, edge_96 = roll(edge, 32), roll(edge, 64), roll(edge, 96)
        evens = jnp.where(
            block == 0,
            halves(own, other_64),
            jnp.where(
                block == 1,
                halves(other_up, own_32),
                jnp.where(block == 2, halves(edge_64, edge), halves(edge_96, edge_32)),
            ),
        )
        odds = jnp.where(
            block == 0,
            halves(own_32, other_up),
            jnp.where(
                block == 1,
                halves(other, own_64),
                jnp.where(block == 2, halves(edge_32, edge_96), halves(edge_64, edge)),
            ),
        )
        evens, odds = step * evens, step * odds
        if second:
            evens, odds = first_ref[0, d] - evens, first_ref[1, d] - odds
        columns[0, d], columns[1, d] = evens, odds
        for e, value in enumerate((evens, odds)):
            later = roll(value, -1)
            middle = swap(halves(later, value))
            columns[2 + e, d] = middle
            columns[4 + e, d] = later
            columns[6 + e, d] = roll(middle, -1)

    low_pass, high_pass = filter_table(BASES)
    result = [[None] * dec_rows for _ in range(2)]
    for b in range(BASES):
        low, high = [float(v) for v in low_pass[b]], [float(v) for v in high_pass[b]]
        bound = spread([thresholds_ref[b, c] for c in range(channels)]) * step
        ra_low = [combine([(low[j], columns[j, d]) for j in range(8)]) for d in range(dec_rows)]
        ra_high = [combine([(high[j], columns[j, d]) for j in range(8)]) for d in range(dec_rows)]
        coarse_a = dec_analysis(ra_low, low, high)
        coarse_b = [shrink(v, bound) for v in dec_analysis(ra_high, low, high)]
        smooth, detail = coarse_a[: dec_rows // 2], [shrink(v, bound) for v in coarse_a[dec_rows // 2 :]]
        pair = lambda even, odd: jnp.where(upper, jnp.float32(odd), jnp.float32(even))
        fine = []
        for value in smooth:
            moved = [value] + [roll(value, -i) for i in (1, 2, 3)]
            lows = sum(pair(low[2 * i], low[2 * i + 1]) * moved[i] for i in range(4))
            highs = sum(pair(high[2 * i], high[2 * i + 1]) * moved[i] for i in range(4))
            fine.append(halves(lows, highs) + swap(halves(highs, lows)))
        fine = [shrink(v, bound) for v in dec_analysis(fine, low, high)]
        fine = dec_synthesis(fine, low, high)
        smooth = []
        for value in fine:
            moved = [value] + [roll(value, i) for i in (1, 2, 3)]
            evens = sum(pair(low[2 * i], high[2 * i]) * moved[i] for i in range(4))
            odds = sum(pair(low[2 * i + 1], high[2 * i + 1]) * moved[i] for i in range(4))
            smooth.append(halves(evens, odds) + swap(halves(odds, evens)))
        top_low = dec_synthesis(smooth + detail, low, high)
        top_high = dec_synthesis(coarse_b, low, high)
        for d in range(dec_rows):
            shifted = []
            for value in (top_low[d], top_high[d]):
                other = swap(value)
                before = halves(roll(other, 1), other)
                shifted.append([value, before, roll(value, 1), roll(before, 1)])
            for e in range(2):
                terms = []
                for i in range(4):
                    terms.append((low[2 * i + e], shifted[0][i]))
                    terms.append((high[2 * i + e], shifted[1][i]))
                value = combine(terms)
                result[e][d] = value if b == 0 else result[e][d] + value

    for d in range(dec_rows):
        evens = jnp.maximum(result[0][d] * (1.0 / BASES), 0.0)
        odds = jnp.maximum(result[1][d] * (1.0 / BASES), 0.0)
        if not second:
            first_ref[0, d], first_ref[1, d] = evens, odds
        even_other, odd_other = swap(evens), swap(odds)
        value = jnp.where(
            block == 0,
            halves(evens, roll(even_other, -32)),
            jnp.where(
                block == 1,
                halves(roll(odds, 32), odd_other),
                jnp.where(
                    block == 2,
                    halves(roll(even_other, 64), roll(evens, 32)),
                    halves(roll(odd_other, 96), roll(odds, 64)),
                ),
            ),
        )
        natural[pl.ds(d, 8, stride=dec_rows), :] = value
    if second:
        order = phase_rows(LANES).astype(jnp.float32)
        image = lax.dot_general(
            natural[...],
            order,
            (((1,), (0,)), ((), ())),
            precision=lax.Precision.HIGHEST,
            preferred_element_type=jnp.float32,
        )
        for tile in range(2):
            for c in range(channels):
                start = (tile * channels + c) * dec_rows
                out_ref[c, :, tile * LANES : (tile + 1) * LANES] = image[start : start + dec_rows]
    else:
        out_ref[...] = natural[...].astype(jnp.bfloat16)


def prox_call(received, thresholds, step_size, dec_rows, first=None):
    second = first is not None
    sources = received.shape[0]
    channels = step_size.shape[0]
    received = received.reshape(sources, SLOTS * channels * dec_rows, LANES)
    vmem = pl.BlockSpec(memory_space=pltpu.VMEM)
    smem = pl.BlockSpec(memory_space=pltpu.SMEM)
    held = jax.ShapeDtypeStruct((2, dec_rows, 8, LANES), jnp.float32)
    if second:
        out_shape = jax.ShapeDtypeStruct((channels, dec_rows, RA_DEV), jnp.float32)
        out_specs = vmem
    else:
        out_shape = (held, jax.ShapeDtypeStruct((2 * channels * dec_rows, LANES), jnp.bfloat16))
        out_specs = (vmem, vmem)
    return pl.pallas_call(
        functools.partial(prox_kernel, second),
        out_shape=out_shape,
        in_specs=[vmem, smem, smem] + ([vmem] if second else []),
        out_specs=out_specs,
        scratch_shapes=[
            pltpu.VMEM((4 * channels * dec_rows, LANES), jnp.float32),
            pltpu.VMEM((8, dec_rows, 8, LANES), jnp.float32),
            pltpu.VMEM((2 * channels * dec_rows, LANES), jnp.float32),
        ],
        compiler_params=pltpu.CompilerParams(vmem_limit_bytes=32 << 20),
        name="second_prox" if second else "first_prox",
    )(received, thresholds, step_size, *([first] if second else []))


def local(vis, beams, m_ra, m_dec, facet_of, tile_of, beam_of, step_size, thresholds):
    facets = lax.axis_size("ra")
    channels, dec_rows, owned, samples = vis.shape
    width = m_ra.shape[0]
    patch_of = facet_of[:, 0] * (RA_DEV // width) + tile_of

    def exchange(sums):
        return lax.all_to_all(sums, "ra", split_axis=0, concat_axis=0, tiled=True)

    sums = gradient_call(patch_of, beam_of, vis, beams, m_ra, m_dec, facets)
    first, tiles = prox_call(exchange(sums), thresholds, step_size, dec_rows)
    tiles = lax.all_gather(tiles, "ra", axis=0, tiled=True)
    tiles = tiles.reshape(facets * 2 * channels, dec_rows, width)
    sums = gradient_call(patch_of, beam_of, vis, beams, m_ra, m_dec, facets, tiles)
    return prox_call(exchange(sums), thresholds, step_size, dec_rows, first)


def solution(mesh):
    in_specs = (
        P(None, "strip", "ra", None),
        P(None, "strip", None, None),
        P(),
        P(),
        P(("strip", "ra"), None),
        P(("strip", "ra")),
        P(("strip", "ra")),
        P(),
        P(),
    )
    out_specs = P(None, "strip", "ra")
    return jax.shard_map(local, mesh=mesh, in_specs=in_specs, out_specs=out_specs, check_vma=False)
```

```python
import functools

import jax
import jax.numpy as jnp
import numpy as np
from jax import lax
from jax.experimental import pallas as pl
from jax.experimental.pallas import tpu as pltpu
from jax.sharding import PartitionSpec as P

BASES = 4
RA_DEV = 256
GROUP = 16
PHASES = 4
LANES = 128
SPAN = LANES // PHASES
SLOTS = 3
CHUNK = 256

daub_coeffs = (
    (0.7071067811865476, 0.7071067811865476),
    (0.48296291314453416, 0.8365163037378079, 0.2241438680420134, -0.12940952255126037),
    (
        0.3326705529500825,
        0.8068915093110924,
        0.4598775021184914,
        -0.1350110200102546,
        -0.0854412738820267,
        0.0352262918857095,
    ),
    (
        0.2303778133088964,
        0.7148465705529155,
        0.6308807679298587,
        -0.0279837694168599,
        -0.1870348117190931,
        0.0308413818355607,
        0.0328830116668852,
        -0.010597401785069,
    ),
)


def filter_table(basis_count):
    low_pass = np.zeros((basis_count, 8))
    for basis_id in range(basis_count):
        coeffs = daub_coeffs[basis_id]
        low_pass[basis_id, : len(coeffs)] = coeffs
    high_pass = np.zeros((basis_count, 8))
    for column in range(8):
        high_pass[:, column] = (-1.0) ** column * low_pass[:, 7 - column]
    return low_pass.astype(np.float32), high_pass.astype(np.float32)


def iota(shape, axis):
    return lax.broadcasted_iota(jnp.int32, shape, axis)


def where_equal(left, right):
    return jnp.where(left == right, 1.0, 0.0)


def dot(left, right, contract=((1,), (0,))):
    return lax.dot_general(left, right, (contract, ((), ())), preferred_element_type=jnp.float32)


def phase_rows(width):
    row, column = iota((width, width), 0), iota((width, width), 1)
    span = width // PHASES
    return where_equal(column, PHASES * (row % span) + row // span).astype(jnp.bfloat16)


def back_matrix(m_dec):
    size = GROUP * GROUP
    pick = where_equal(iota((size, GROUP), 0) % GROUP, iota((size, GROUP), 1)).astype(jnp.bfloat16)
    place = where_equal(iota((GROUP, size), 0), iota((GROUP, size), 1) // GROUP).astype(jnp.bfloat16)
    wide = dot(dot(pick, m_dec, ((1,), (1,))).astype(jnp.bfloat16), place)
    return (wide * where_equal(iota((size, size), 0) // GROUP, iota((size, size), 1) % GROUP)).astype(jnp.bfloat16)


def forward_matrix(m_dec):
    size = GROUP * GROUP
    pick = where_equal(iota((size, GROUP), 0) // GROUP, iota((size, GROUP), 1)).astype(jnp.bfloat16)
    place = where_equal(iota((GROUP, size), 0), iota((GROUP, size), 1) % GROUP).astype(jnp.bfloat16)
    wide = dot(dot(pick, m_dec).astype(jnp.bfloat16), place)
    return (wide * where_equal(iota((size, size), 0) % GROUP, iota((size, size), 1) // GROUP)).astype(jnp.bfloat16)


def swap_rows(size_a, size_b):
    size = size_a * size_b
    row, column = iota((size, size), 0), iota((size, size), 1)
    return where_equal((row % size_a) * size_b + row // size_a, column).astype(jnp.bfloat16)


def gradient_kernel(second, patch_ref, beam_ref, vis_ref, beams_ref, m_ra_ref, m_dec_ref, *refs):
    if second:
        tiles_ref, out_ref, back, forward, ra_out, ra_in, table, total, along, weighted = refs
    else:
        out_ref, back, ra_out, table, total, along, weighted = refs
    channel = pl.program_id(0)
    channels = pl.num_programs(0)
    dec_rows, owned = vis_ref.shape[1], vis_ref.shape[2]
    width = m_ra_ref.shape[0]
    beam_count = beams_ref.shape[2]
    facets = out_ref.shape[0]

    @pl.when(channel == 0)
    def _():
        back[...] = back_matrix(m_dec_ref[...])
        order = phase_rows(width)
        ra_out[...] = dot(m_ra_ref[...], order, ((0,), (1,))).astype(jnp.bfloat16)
        if second:
            forward[...] = forward_matrix(m_dec_ref[...])
            ra_in[...] = dot(order, m_ra_ref[...]).astype(jnp.bfloat16)

    rows = beams_ref[0].reshape(dec_rows * beam_count, width)
    swapped = dot(swap_rows(dec_rows, beam_count), rows).astype(jnp.bfloat16)
    table[...] = (
        dot(swapped, phase_rows(width), ((1,), (1,)))
        .astype(jnp.bfloat16)
        .reshape(beam_count, dec_rows, width)
    )
    total[...] = jnp.zeros_like(total)

    samples = vis_ref.shape[3]
    size = GROUP * dec_rows
    groups = owned // GROUP

    if second:
        for p in range(owned):
            weighted[p * dec_rows : (p + 1) * dec_rows] = (
                table[beam_ref[p]].astype(jnp.float32)
                * tiles_ref[patch_ref[p] * channels + channel].astype(jnp.float32)
            ).astype(jnp.bfloat16)
        for m in range(0, owned * dec_rows, CHUNK):
            along[m : m + CHUNK] = dot(weighted[m : m + CHUNK], ra_in[...]).astype(jnp.bfloat16)
    for group in range(groups):
        rows = slice(group * size, (group + 1) * size)
        data = vis_ref[0, :, group * GROUP : (group + 1) * GROUP, :].reshape(size, samples)
        if second:
            predicted = dot(forward[...], along[rows])
            data = (predicted - data.astype(jnp.float32)).astype(jnp.bfloat16)
        along[rows] = dot(back[...], data).astype(jnp.bfloat16)
    for m in range(0, owned * dec_rows, CHUNK):
        patches = dot(along[m : m + CHUNK], ra_out[...])
        for i in range(CHUNK // dec_rows):
            p = m // dec_rows + i
            patch = patches[i * dec_rows : (i + 1) * dec_rows]
            patch_grad = (table[beam_ref[p]].astype(jnp.float32) * patch).astype(jnp.bfloat16).astype(jnp.float32)
            total[patch_ref[p]] = total[patch_ref[p]] + patch_grad
    from_left = iota((dec_rows, width), 1) % SPAN >= SPAN // 2
    tiles = total.shape[0]

    def one_facet(facet, carry):
        own = 2 * facet
        left, right = lax.rem(own + tiles - 1, tiles), lax.rem(own + 2, tiles)
        out_ref[facet, 0, 0] = total[own].astype(jnp.bfloat16)
        out_ref[facet, 1, 0] = total[own + 1].astype(jnp.bfloat16)
        out_ref[facet, 2, 0] = jnp.where(from_left, total[left], total[right]).astype(jnp.bfloat16)
        return carry

    lax.fori_loop(0, facets, one_facet, 0, unroll=4)


def gradient_call(patch_of, beam_of, vis, beams, m_ra, m_dec, facets, tiles=None):
    channels, dec_rows, owned, samples = vis.shape
    width = m_ra.shape[0]
    beam_count = beams.shape[2]
    second = tiles is not None
    whole = lambda c, *_: (0, 0)
    in_specs = [
        pl.BlockSpec((1, dec_rows, owned, samples), lambda c, *_: (c, 0, 0, 0)),
        pl.BlockSpec((1, dec_rows, beam_count, width), lambda c, *_: (c, 0, 0, 0)),
        pl.BlockSpec(m_ra.shape, whole),
        pl.BlockSpec(m_dec.shape, whole),
    ]
    operands = [vis, beams, m_ra, m_dec]
    size = GROUP * GROUP
    back = pltpu.VMEM((size, size), jnp.bfloat16)
    ra_out = pltpu.VMEM((samples, width), jnp.bfloat16)
    ra_in = pltpu.VMEM((width, samples), jnp.bfloat16)
    tail = [
        pltpu.VMEM((beam_count, dec_rows, width), jnp.bfloat16),
        pltpu.VMEM((2 * facets, dec_rows, width), jnp.float32),
        pltpu.VMEM((owned * dec_rows, samples), jnp.bfloat16),
        pltpu.VMEM((owned * dec_rows, width), jnp.bfloat16),
    ]
    if second:
        in_specs.append(pl.BlockSpec(tiles.shape, lambda c, *_: (0, 0, 0)))
        operands.append(tiles)
        scratch = [back, back, ra_out, ra_in] + tail
    else:
        scratch = [back, ra_out] + tail
    work = channels * owned * samples * dec_rows
    return pl.pallas_call(
        functools.partial(gradient_kernel, second),
        out_shape=jax.ShapeDtypeStruct((facets, SLOTS, channels, dec_rows, width), jnp.bfloat16),
        grid_spec=pltpu.PrefetchScalarGridSpec(
            num_scalar_prefetch=2,
            grid=(channels,),
            in_specs=in_specs,
            out_specs=pl.BlockSpec((facets, SLOTS, 1, dec_rows, width), lambda c, *_: (0, 0, c, 0, 0)),
            scratch_shapes=scratch,
        ),
        compiler_params=pltpu.CompilerParams(vmem_limit_bytes=48 << 20),
        cost_estimate=pl.CostEstimate(
            flops=(4 if second else 2) * 256 * work, bytes_accessed=2 * work, transcendentals=0
        ),
        name="second_gradient" if second else "first_gradient",
    )(patch_of, beam_of, *operands)


def shrink(values, bound):
    return values - jnp.clip(values, -bound, bound)


def combine(terms):
    total = None
    for factor, value in terms:
        if factor == 0.0:
            continue
        term = value * jnp.float32(factor)
        total = term if total is None else total + term
    return total


def dec_analysis(rows, low, high):
    count = len(rows)
    half = count // 2
    lows = [combine([(low[j], rows[(2 * k + j) % count]) for j in range(8)]) for k in range(half)]
    highs = [combine([(high[j], rows[(2 * k + j) % count]) for j in range(8)]) for k in range(half)]
    return lows + highs


def dec_synthesis(rows, low, high):
    count = len(rows)
    half = count // 2
    gathered = [[] for _ in range(count)]
    for k in range(half):
        for j in range(8):
            gathered[(2 * k + j) % count].append((low[j], rows[k]))
            gathered[(2 * k + j) % count].append((high[j], rows[half + k]))
    return [combine(terms) for terms in gathered]


def prox_kernel(second, recv_ref, thresholds_ref, step_ref, *refs):
    if second:
        first_ref, out_ref, summed, columns, natural = refs
    else:
        first_ref, out_ref, summed, columns, natural = refs
    sources, rows = recv_ref.shape[0], recv_ref.shape[1]
    dec_rows = first_ref.shape[1]
    channels = step_ref.shape[0]
    half = 4
    shape = (8, LANES)
    upper = iota(shape, 0) >= half
    channel = iota(shape, 0) % half
    lane = iota(shape, 1)
    block = lane // SPAN

    def add_source(source, total):
        return total + recv_ref[source].astype(jnp.float32)

    total = lax.fori_loop(1, sources, add_source, recv_ref[0].astype(jnp.float32))
    summed[:rows] = total
    summed[rows:] = total[rows - channels * dec_rows :]

    def spread(scalars):
        value = jnp.full(shape, scalars[channels - 1], jnp.float32)
        for c in range(channels - 1):
            value = jnp.where(channel == c, scalars[c], value)
        return value

    step = spread([step_ref[c] for c in range(channels)])
    roll = lambda value, shift: pltpu.roll(value, shift % LANES, 1)
    swap = lambda value: pltpu.roll(value, half, 0)
    halves = lambda low, high: jnp.where(upper, high, low)

    for d in range(dec_rows):
        own = summed[pl.ds(d, 8, stride=dec_rows), :]
        edge = summed[pl.ds(8 * dec_rows + d, 8, stride=dec_rows), :]
        other = swap(own)
        own_32, own_64 = roll(own, -32), roll(own, -64)
        other_up, other_64 = roll(other, 32), roll(other, -64)
        edge_32, edge_64, edge_96 = roll(edge, 32), roll(edge, 64), roll(edge, 96)
        evens = jnp.where(
            block == 0,
            halves(own, other_64),
            jnp.where(
                block == 1,
                halves(other_up, own_32),
                jnp.where(block == 2, halves(edge_64, edge), halves(edge_96, edge_32)),
            ),
        )
        odds = jnp.where(
            block == 0,
            halves(own_32, other_up),
            jnp.where(
                block == 1,
                halves(other, own_64),
                jnp.where(block == 2, halves(edge_32, edge_96), halves(edge_64, edge)),
            ),
        )
        evens, odds = step * evens, step * odds
        if second:
            evens, odds = first_ref[0, d] - evens, first_ref[1, d] - odds
        columns[0, d], columns[1, d] = evens, odds
        for e, value in enumerate((evens, odds)):
            later = roll(value, -1)
            middle = swap(halves(later, value))
            columns[2 + e, d] = middle
            columns[4 + e, d] = later
            columns[6 + e, d] = roll(middle, -1)

    low_pass, high_pass = filter_table(BASES)
    result = [[None] * dec_rows for _ in range(2)]
    for b in range(BASES):
        low, high = [float(v) for v in low_pass[b]], [float(v) for v in high_pass[b]]
        bound = spread([thresholds_ref[b, c] for c in range(channels)]) * step
        ra_low = [combine([(low[j], columns[j, d]) for j in range(8)]) for d in range(dec_rows)]
        ra_high = [combine([(high[j], columns[j, d]) for j in range(8)]) for d in range(dec_rows)]
        coarse_a = dec_analysis(ra_low, low, high)
        coarse_b = [shrink(v, bound) for v in dec_analysis(ra_high, low, high)]
        smooth, detail = coarse_a[: dec_rows // 2], [shrink(v, bound) for v in coarse_a[dec_rows // 2 :]]
        pair = lambda even, odd: jnp.where(upper, jnp.float32(odd), jnp.float32(even))
        fine = []
        for value in smooth:
            moved = [value] + [roll(value, -i) for i in (1, 2, 3)]
            lows = sum(pair(low[2 * i], low[2 * i + 1]) * moved[i] for i in range(4))
            highs = sum(pair(high[2 * i], high[2 * i + 1]) * moved[i] for i in range(4))
            fine.append(halves(lows, highs) + swap(halves(highs, lows)))
        fine = [shrink(v, bound) for v in dec_analysis(fine, low, high)]
        fine = dec_synthesis(fine, low, high)
        smooth = []
        for value in fine:
            moved = [value] + [roll(value, i) for i in (1, 2, 3)]
            evens = sum(pair(low[2 * i], high[2 * i]) * moved[i] for i in range(4))
            odds = sum(pair(low[2 * i + 1], high[2 * i + 1]) * moved[i] for i in range(4))
            smooth.append(halves(evens, odds) + swap(halves(odds, evens)))
        top_low = dec_synthesis(smooth + detail, low, high)
        top_high = dec_synthesis(coarse_b, low, high)
        for d in range(dec_rows):
            shifted = []
            for value in (top_low[d], top_high[d]):
                other = swap(value)
                before = halves(roll(other, 1), other)
                shifted.append([value, before, roll(value, 1), roll(before, 1)])
            for e in range(2):
                terms = []
                for i in range(4):
                    terms.append((low[2 * i + e], shifted[0][i]))
                    terms.append((high[2 * i + e], shifted[1][i]))
                value = combine(terms)
                result[e][d] = value if b == 0 else result[e][d] + value

    for d in range(dec_rows):
        evens = jnp.maximum(result[0][d] * (1.0 / BASES), 0.0)
        odds = jnp.maximum(result[1][d] * (1.0 / BASES), 0.0)
        if not second:
            first_ref[0, d], first_ref[1, d] = evens, odds
        even_other, odd_other = swap(evens), swap(odds)
        value = jnp.where(
            block == 0,
            halves(evens, roll(even_other, -32)),
            jnp.where(
                block == 1,
                halves(roll(odds, 32), odd_other),
                jnp.where(
                    block == 2,
                    halves(roll(even_other, 64), roll(evens, 32)),
                    halves(roll(odd_other, 96), roll(odds, 64)),
                ),
            ),
        )
        natural[pl.ds(d, 8, stride=dec_rows), :] = value
    if second:
        order = phase_rows(LANES).astype(jnp.float32)
        image = lax.dot_general(
            natural[...],
            order,
            (((1,), (0,)), ((), ())),
            precision=lax.Precision.HIGHEST,
            preferred_element_type=jnp.float32,
        )
        for tile in range(2):
            for c in range(channels):
                start = (tile * channels + c) * dec_rows
                out_ref[c, :, tile * LANES : (tile + 1) * LANES] = image[start : start + dec_rows]
    else:
        out_ref[...] = natural[...].astype(jnp.bfloat16)


def prox_call(received, thresholds, step_size, dec_rows, first=None):
    second = first is not None
    sources = received.shape[0]
    channels = step_size.shape[0]
    received = received.reshape(sources, SLOTS * channels * dec_rows, LANES)
    vmem = pl.BlockSpec(memory_space=pltpu.VMEM)
    smem = pl.BlockSpec(memory_space=pltpu.SMEM)
    held = jax.ShapeDtypeStruct((2, dec_rows, 8, LANES), jnp.float32)
    if second:
        out_shape = jax.ShapeDtypeStruct((channels, dec_rows, RA_DEV), jnp.float32)
        out_specs = vmem
    else:
        out_shape = (held, jax.ShapeDtypeStruct((2 * channels * dec_rows, LANES), jnp.bfloat16))
        out_specs = (vmem, vmem)
    return pl.pallas_call(
        functools.partial(prox_kernel, second),
        out_shape=out_shape,
        in_specs=[vmem, smem, smem] + ([vmem] if second else []),
        out_specs=out_specs,
        scratch_shapes=[
            pltpu.VMEM((4 * channels * dec_rows, LANES), jnp.float32),
            pltpu.VMEM((8, dec_rows, 8, LANES), jnp.float32),
            pltpu.VMEM((2 * channels * dec_rows, LANES), jnp.float32),
        ],
        compiler_params=pltpu.CompilerParams(vmem_limit_bytes=32 << 20),
        name="second_prox" if second else "first_prox",
    )(received, thresholds, step_size, *([first] if second else []))


def local(vis, beams, m_ra, m_dec, facet_of, tile_of, beam_of, step_size, thresholds):
    facets = lax.axis_size("ra")
    channels, dec_rows, owned, samples = vis.shape
    width = m_ra.shape[0]
    beams, m_ra, m_dec, beam_of = (
        pltpu.with_memory_space_constraint(x, pltpu.HBM) for x in (beams, m_ra, m_dec, beam_of)
    )
    patch_of = facet_of[:, 0] * (RA_DEV // width) + tile_of

    def exchange(sums):
        return lax.all_to_all(sums, "ra", split_axis=0, concat_axis=0, tiled=True)

    sums = gradient_call(patch_of, beam_of, vis, beams, m_ra, m_dec, facets)
    first, tiles = prox_call(exchange(sums), thresholds, step_size, dec_rows)
    tiles = lax.all_gather(tiles, "ra", axis=0, tiled=True)
    tiles = tiles.reshape(facets * 2 * channels, dec_rows, width)
    sums = gradient_call(patch_of, beam_of, vis, beams, m_ra, m_dec, facets, tiles)
    return prox_call(exchange(sums), thresholds, step_size, dec_rows, first)


def solution(mesh):
    in_specs = (
        P(None, "strip", "ra", None),
        P(None, "strip", None, None),
        P(),
        P(),
        P(("strip", "ra"), None),
        P(("strip", "ra")),
        P(("strip", "ra")),
        P(),
        P(),
    )
    out_specs = P(None, "strip", "ra")
    return jax.shard_map(local, mesh=mesh, in_specs=in_specs, out_specs=out_specs, check_vma=False)
```

```python
import functools

import jax
import jax.numpy as jnp
import numpy as np
from jax import lax
from jax.experimental import pallas as pl
from jax.experimental.pallas import tpu as pltpu
from jax.sharding import PartitionSpec as P

BASES = 4
RA_DEV = 256
GROUP = 16
PHASES = 4
LANES = 128
SPAN = LANES // PHASES
SLOTS = 3
CHUNK = 256

daub_coeffs = (
    (0.7071067811865476, 0.7071067811865476),
    (0.48296291314453416, 0.8365163037378079, 0.2241438680420134, -0.12940952255126037),
    (
        0.3326705529500825,
        0.8068915093110924,
        0.4598775021184914,
        -0.1350110200102546,
        -0.0854412738820267,
        0.0352262918857095,
    ),
    (
        0.2303778133088964,
        0.7148465705529155,
        0.6308807679298587,
        -0.0279837694168599,
        -0.1870348117190931,
        0.0308413818355607,
        0.0328830116668852,
        -0.010597401785069,
    ),
)


def filter_table(basis_count):
    low_pass = np.zeros((basis_count, 8))
    for basis_id in range(basis_count):
        coeffs = daub_coeffs[basis_id]
        low_pass[basis_id, : len(coeffs)] = coeffs
    high_pass = np.zeros((basis_count, 8))
    for column in range(8):
        high_pass[:, column] = (-1.0) ** column * low_pass[:, 7 - column]
    return low_pass.astype(np.float32), high_pass.astype(np.float32)


def iota(shape, axis):
    return lax.broadcasted_iota(jnp.int32, shape, axis)


def where_equal(left, right):
    return jnp.where(left == right, 1.0, 0.0)


def dot(left, right, contract=((1,), (0,))):
    return lax.dot_general(left, right, (contract, ((), ())), preferred_element_type=jnp.float32)


def phase_rows(width):
    row, column = iota((width, width), 0), iota((width, width), 1)
    span = width // PHASES
    return where_equal(column, PHASES * (row % span) + row // span).astype(jnp.bfloat16)


def back_matrix(m_dec):
    size = GROUP * GROUP
    pick = where_equal(iota((size, GROUP), 0) % GROUP, iota((size, GROUP), 1)).astype(jnp.bfloat16)
    place = where_equal(iota((GROUP, size), 0), iota((GROUP, size), 1) // GROUP).astype(jnp.bfloat16)
    wide = dot(dot(pick, m_dec, ((1,), (1,))).astype(jnp.bfloat16), place)
    return (wide * where_equal(iota((size, size), 0) // GROUP, iota((size, size), 1) % GROUP)).astype(jnp.bfloat16)


def forward_matrix(m_dec):
    size = GROUP * GROUP
    pick = where_equal(iota((size, GROUP), 0) // GROUP, iota((size, GROUP), 1)).astype(jnp.bfloat16)
    place = where_equal(iota((GROUP, size), 0), iota((GROUP, size), 1) % GROUP).astype(jnp.bfloat16)
    wide = dot(dot(pick, m_dec).astype(jnp.bfloat16), place)
    return (wide * where_equal(iota((size, size), 0) % GROUP, iota((size, size), 1) // GROUP)).astype(jnp.bfloat16)


def swap_rows(size_a, size_b):
    size = size_a * size_b
    row, column = iota((size, size), 0), iota((size, size), 1)
    return where_equal((row % size_a) * size_b + row // size_a, column).astype(jnp.bfloat16)


def gradient_kernel(second, paired, patch_ref, beam_ref, *refs):
    if paired:
        me_ref, *refs = refs
    if second:
        slot_ref, *refs = refs
    vis_ref, beams_ref, m_ra_ref, m_dec_ref, *refs = refs
    if second:
        tiles_ref, *refs = refs
    outs, refs = refs[: 1 + paired], refs[1 + paired :]
    if second:
        back, forward, ra_out, ra_in, table, total, along, weighted = refs
    else:
        back, ra_out, table, total, along, weighted = refs
    channel = pl.program_id(0)
    channels = pl.num_programs(0)
    dec_rows, owned = vis_ref.shape[1], vis_ref.shape[2]
    width = m_ra_ref.shape[0]
    beam_count = beams_ref.shape[2]
    facets = outs[0].shape[0]

    @pl.when(channel == 0)
    def _():
        back[...] = back_matrix(m_dec_ref[...])
        order = phase_rows(width)
        ra_out[...] = dot(m_ra_ref[...], order, ((0,), (1,))).astype(jnp.bfloat16)
        if second:
            forward[...] = forward_matrix(m_dec_ref[...])
            ra_in[...] = dot(order, m_ra_ref[...]).astype(jnp.bfloat16)

    rows = beams_ref[0].reshape(dec_rows * beam_count, width)
    swapped = dot(swap_rows(dec_rows, beam_count), rows).astype(jnp.bfloat16)
    table[...] = (
        dot(swapped, phase_rows(width), ((1,), (1,)))
        .astype(jnp.bfloat16)
        .reshape(beam_count, dec_rows, width)
    )
    total[...] = jnp.zeros_like(total)

    samples = vis_ref.shape[3]
    size = GROUP * dec_rows
    groups = owned // GROUP

    if second:
        for p in range(owned):
            weighted[p * dec_rows : (p + 1) * dec_rows] = (
                table[beam_ref[p]].astype(jnp.float32)
                * tiles_ref[slot_ref[p] * channels + channel].astype(jnp.float32)
            ).astype(jnp.bfloat16)
        for m in range(0, owned * dec_rows, CHUNK):
            along[m : m + CHUNK] = dot(weighted[m : m + CHUNK], ra_in[...]).astype(jnp.bfloat16)
    for group in range(groups):
        rows = slice(group * size, (group + 1) * size)
        data = vis_ref[0, :, group * GROUP : (group + 1) * GROUP, :].reshape(size, samples)
        if second:
            predicted = dot(forward[...], along[rows])
            data = (predicted - data.astype(jnp.float32)).astype(jnp.bfloat16)
        along[rows] = dot(back[...], data).astype(jnp.bfloat16)
    for m in range(0, owned * dec_rows, CHUNK):
        patches = dot(along[m : m + CHUNK], ra_out[...])
        for i in range(CHUNK // dec_rows):
            p = m // dec_rows + i
            patch = patches[i * dec_rows : (i + 1) * dec_rows]
            patch_grad = (table[beam_ref[p]].astype(jnp.float32) * patch).astype(jnp.bfloat16).astype(jnp.float32)
            total[patch_ref[p]] = total[patch_ref[p]] + patch_grad
    from_left = iota((dec_rows, width), 1) % SPAN >= SPAN // 2
    tiles = total.shape[0]

    def one_facet(index, carry):
        for side, out_ref in enumerate(outs):
            facet = (2 * index + side) ^ me_ref[0] if paired else index
            own = 2 * facet
            left, right = lax.rem(own + tiles - 1, tiles), lax.rem(own + 2, tiles)
            out_ref[index, 0, 0] = total[own].astype(out_ref.dtype)
            out_ref[index, 1, 0] = total[own + 1].astype(out_ref.dtype)
            out_ref[index, 2, 0] = jnp.where(from_left, total[left], total[right]).astype(out_ref.dtype)
        return carry

    lax.fori_loop(0, facets, one_facet, 0, unroll=4)


def gradient_call(patch_of, beam_of, vis, beams, m_ra, m_dec, facets, me=None, slot_of=None, tiles=None):
    channels, dec_rows, owned, samples = vis.shape
    width = m_ra.shape[0]
    beam_count = beams.shape[2]
    second, paired = tiles is not None, me is not None
    scalars = [patch_of, beam_of] + [me] * paired + [slot_of] * second
    whole = lambda c, *_: (0, 0)
    in_specs = [
        pl.BlockSpec((1, dec_rows, owned, samples), lambda c, *_: (c, 0, 0, 0)),
        pl.BlockSpec((1, dec_rows, beam_count, width), lambda c, *_: (c, 0, 0, 0)),
        pl.BlockSpec(m_ra.shape, whole),
        pl.BlockSpec(m_dec.shape, whole),
    ]
    operands = [vis, beams, m_ra, m_dec]
    size = GROUP * GROUP
    back = pltpu.VMEM((size, size), jnp.bfloat16)
    ra_out = pltpu.VMEM((samples, width), jnp.bfloat16)
    ra_in = pltpu.VMEM((width, samples), jnp.bfloat16)
    tail = [
        pltpu.VMEM((beam_count, dec_rows, width), jnp.bfloat16),
        pltpu.VMEM((2 * facets, dec_rows, width), jnp.float32),
        pltpu.VMEM((owned * dec_rows, samples), jnp.bfloat16),
        pltpu.VMEM((owned * dec_rows, width), jnp.bfloat16),
    ]
    if second:
        in_specs.append(pl.BlockSpec(tiles.shape, lambda c, *_: (0, 0, 0)))
        operands.append(tiles)
        scratch = [back, back, ra_out, ra_in] + tail
    else:
        scratch = [back, ra_out] + tail
    work = channels * owned * samples * dec_rows
    kept, sum_type = (facets // 2, jnp.float32) if paired else (facets, jnp.bfloat16)
    out_shape = jax.ShapeDtypeStruct((kept, SLOTS, channels, dec_rows, width), sum_type)
    return pl.pallas_call(
        functools.partial(gradient_kernel, second, paired),
        out_shape=[out_shape] * (1 + paired),
        grid_spec=pltpu.PrefetchScalarGridSpec(
            num_scalar_prefetch=len(scalars),
            grid=(channels,),
            in_specs=in_specs,
            out_specs=[pl.BlockSpec((kept, SLOTS, 1, dec_rows, width), lambda c, *_: (0, 0, c, 0, 0))] * (1 + paired),
            scratch_shapes=scratch,
        ),
        compiler_params=pltpu.CompilerParams(vmem_limit_bytes=48 << 20),
        cost_estimate=pl.CostEstimate(
            flops=(4 if second else 2) * 256 * work, bytes_accessed=2 * work, transcendentals=0
        ),
        name="second_gradient" if second else "first_gradient",
    )(*scalars, *operands)


def shrink(values, bound):
    return values - jnp.clip(values, -bound, bound)


def combine(terms):
    total = None
    for factor, value in terms:
        if factor == 0.0:
            continue
        term = value * jnp.float32(factor)
        total = term if total is None else total + term
    return total


def dec_analysis(rows, low, high):
    count = len(rows)
    half = count // 2
    lows = [combine([(low[j], rows[(2 * k + j) % count]) for j in range(8)]) for k in range(half)]
    highs = [combine([(high[j], rows[(2 * k + j) % count]) for j in range(8)]) for k in range(half)]
    return lows + highs


def dec_synthesis(rows, low, high):
    count = len(rows)
    half = count // 2
    gathered = [[] for _ in range(count)]
    for k in range(half):
        for j in range(8):
            gathered[(2 * k + j) % count].append((low[j], rows[k]))
            gathered[(2 * k + j) % count].append((high[j], rows[half + k]))
    return [combine(terms) for terms in gathered]


def prox_kernel(second, parts, *refs):
    part_refs, (thresholds_ref, step_ref, *refs) = refs[:parts], refs[parts:]
    first_ref, out_ref, summed, columns, natural = refs
    rows = part_refs[0].shape[1]
    dec_rows = first_ref.shape[1]
    channels = step_ref.shape[0]
    half = 4
    shape = (8, LANES)
    upper = iota(shape, 0) >= half
    channel = iota(shape, 0) % half
    lane = iota(shape, 1)
    block = lane // SPAN

    total = part_refs[0][0].astype(jnp.float32)
    for part_ref in part_refs[1:]:
        total = total + part_ref[0].astype(jnp.float32)
    for index in range(1, part_refs[0].shape[0]):
        total = total + part_refs[0][index].astype(jnp.float32)
    summed[:rows] = total
    summed[rows:] = total[rows - channels * dec_rows :]

    def spread(scalars):
        value = jnp.full(shape, scalars[channels - 1], jnp.float32)
        for c in range(channels - 1):
            value = jnp.where(channel == c, scalars[c], value)
        return value

    step = spread([step_ref[c] for c in range(channels)])
    roll = lambda value, shift: pltpu.roll(value, shift % LANES, 1)
    swap = lambda value: pltpu.roll(value, half, 0)
    halves = lambda low, high: jnp.where(upper, high, low)

    for d in range(dec_rows):
        own = summed[pl.ds(d, 8, stride=dec_rows), :]
        edge = summed[pl.ds(8 * dec_rows + d, 8, stride=dec_rows), :]
        other = swap(own)
        own_32, own_64 = roll(own, -32), roll(own, -64)
        other_up, other_64 = roll(other, 32), roll(other, -64)
        edge_32, edge_64, edge_96 = roll(edge, 32), roll(edge, 64), roll(edge, 96)
        evens = jnp.where(
            block == 0,
            halves(own, other_64),
            jnp.where(
                block == 1,
                halves(other_up, own_32),
                jnp.where(block == 2, halves(edge_64, edge), halves(edge_96, edge_32)),
            ),
        )
        odds = jnp.where(
            block == 0,
            halves(own_32, other_up),
            jnp.where(
                block == 1,
                halves(other, own_64),
                jnp.where(block == 2, halves(edge_32, edge_96), halves(edge_64, edge)),
            ),
        )
        evens, odds = step * evens, step * odds
        if second:
            evens, odds = first_ref[0, d] - evens, first_ref[1, d] - odds
        columns[0, d], columns[1, d] = evens, odds
        for e, value in enumerate((evens, odds)):
            later = roll(value, -1)
            middle = swap(halves(later, value))
            columns[2 + e, d] = middle
            columns[4 + e, d] = later
            columns[6 + e, d] = roll(middle, -1)

    low_pass, high_pass = filter_table(BASES)
    result = [[None] * dec_rows for _ in range(2)]
    for b in range(BASES):
        low, high = [float(v) for v in low_pass[b]], [float(v) for v in high_pass[b]]
        bound = spread([thresholds_ref[b, c] for c in range(channels)]) * step
        ra_low = [combine([(low[j], columns[j, d]) for j in range(8)]) for d in range(dec_rows)]
        ra_high = [combine([(high[j], columns[j, d]) for j in range(8)]) for d in range(dec_rows)]
        coarse_a = dec_analysis(ra_low, low, high)
        coarse_b = [shrink(v, bound) for v in dec_analysis(ra_high, low, high)]
        smooth, detail = coarse_a[: dec_rows // 2], [shrink(v, bound) for v in coarse_a[dec_rows // 2 :]]
        pair = lambda even, odd: jnp.where(upper, jnp.float32(odd), jnp.float32(even))
        fine = []
        for value in smooth:
            moved = [value] + [roll(value, -i) for i in (1, 2, 3)]
            lows = sum(pair(low[2 * i], low[2 * i + 1]) * moved[i] for i in range(4))
            highs = sum(pair(high[2 * i], high[2 * i + 1]) * moved[i] for i in range(4))
            fine.append(halves(lows, highs) + swap(halves(highs, lows)))
        fine = [shrink(v, bound) for v in dec_analysis(fine, low, high)]
        fine = dec_synthesis(fine, low, high)
        smooth = []
        for value in fine:
            moved = [value] + [roll(value, i) for i in (1, 2, 3)]
            evens = sum(pair(low[2 * i], high[2 * i]) * moved[i] for i in range(4))
            odds = sum(pair(low[2 * i + 1], high[2 * i + 1]) * moved[i] for i in range(4))
            smooth.append(halves(evens, odds) + swap(halves(odds, evens)))
        top_low = dec_synthesis(smooth + detail, low, high)
        top_high = dec_synthesis(coarse_b, low, high)
        for d in range(dec_rows):
            shifted = []
            for value in (top_low[d], top_high[d]):
                other = swap(value)
                before = halves(roll(other, 1), other)
                shifted.append([value, before, roll(value, 1), roll(before, 1)])
            for e in range(2):
                terms = []
                for i in range(4):
                    terms.append((low[2 * i + e], shifted[0][i]))
                    terms.append((high[2 * i + e], shifted[1][i]))
                value = combine(terms)
                result[e][d] = value if b == 0 else result[e][d] + value

    for d in range(dec_rows):
        evens = jnp.maximum(result[0][d] * (1.0 / BASES), 0.0)
        odds = jnp.maximum(result[1][d] * (1.0 / BASES), 0.0)
        if not second:
            first_ref[0, d], first_ref[1, d] = evens, odds
        even_other, odd_other = swap(evens), swap(odds)
        value = jnp.where(
            block == 0,
            halves(evens, roll(even_other, -32)),
            jnp.where(
                block == 1,
                halves(roll(odds, 32), odd_other),
                jnp.where(
                    block == 2,
                    halves(roll(even_other, 64), roll(evens, 32)),
                    halves(roll(odd_other, 96), roll(odds, 64)),
                ),
            ),
        )
        natural[pl.ds(d, 8, stride=dec_rows), :] = value
    if second:
        order = phase_rows(LANES).astype(jnp.float32)
        image = lax.dot_general(
            natural[...],
            order,
            (((1,), (0,)), ((), ())),
            precision=lax.Precision.HIGHEST,
            preferred_element_type=jnp.float32,
        )
        for tile in range(2):
            for c in range(channels):
                start = (tile * channels + c) * dec_rows
                out_ref[c, :, tile * LANES : (tile + 1) * LANES] = image[start : start + dec_rows]
    else:
        out_ref[...] = natural[...].astype(jnp.bfloat16)


def prox_call(received, thresholds, step_size, dec_rows, first=None):
    second = first is not None
    channels = step_size.shape[0]
    received = [part.reshape(-1, SLOTS * channels * dec_rows, LANES) for part in received]
    vmem = pl.BlockSpec(memory_space=pltpu.VMEM)
    smem = pl.BlockSpec(memory_space=pltpu.SMEM)
    held = jax.ShapeDtypeStruct((2, dec_rows, 8, LANES), jnp.float32)
    if second:
        out_shape = jax.ShapeDtypeStruct((channels, dec_rows, RA_DEV), jnp.float32)
        out_specs = vmem
    else:
        out_shape = (held, jax.ShapeDtypeStruct((2 * channels * dec_rows, LANES), jnp.bfloat16))
        out_specs = (vmem, vmem)
    return pl.pallas_call(
        functools.partial(prox_kernel, second, len(received)),
        out_shape=out_shape,
        in_specs=[vmem] * len(received) + [smem, smem] + ([vmem] if second else []),
        out_specs=out_specs,
        scratch_shapes=[
            pltpu.VMEM((4 * channels * dec_rows, LANES), jnp.float32),
            pltpu.VMEM((8, dec_rows, 8, LANES), jnp.float32),
            pltpu.VMEM((2 * channels * dec_rows, LANES), jnp.float32),
        ],
        compiler_params=pltpu.CompilerParams(vmem_limit_bytes=32 << 20),
        name="second_prox" if second else "first_prox",
    )(*received, thresholds, step_size, *([first] if second else []))


def fold_kernel(keep_ref, got_ref, *outs):
    for index, out_ref in enumerate(outs):
        out_ref[0] = (keep_ref[index] + got_ref[index]).astype(out_ref.dtype)


def join_kernel(*refs):
    *parts, out_ref = refs
    start = 0
    for part_ref in parts:
        out_ref[start : start + part_ref.shape[0]] = part_ref[...]
        start += part_ref.shape[0]


def small_call(kernel, name, out_shape, *operands):
    vmem = pl.BlockSpec(memory_space=pltpu.VMEM)
    return pl.pallas_call(
        kernel,
        out_shape=out_shape,
        in_specs=[vmem] * len(operands),
        out_specs=jax.tree.map(lambda _: vmem, out_shape),
        compiler_params=pltpu.CompilerParams(vmem_limit_bytes=16 << 20),
        name=name,
    )(*operands)


def join(*parts):
    rows = sum(part.shape[0] for part in parts)
    shape = jax.ShapeDtypeStruct((rows,) + parts[0].shape[1:], parts[0].dtype)
    return small_call(join_kernel, "join", shape, *parts)


def across(value, difference):
    count = lax.axis_size("ra")
    return lax.ppermute(value, "ra", [(source, source ^ difference) for source in range(count)])


def pair_exchange(keep, send):
    got = across(send, 1)
    shape = (1,) + keep.shape[1:]
    kinds = [jnp.float32] + [jnp.bfloat16] * (keep.shape[0] - 1)
    parts = small_call(fold_kernel, "fold", [jax.ShapeDtypeStruct(shape, kind) for kind in kinds], keep, got)
    far = [across(parts[index], 2 * index) for index in reversed(range(1, len(parts)))]
    return [parts[0]] + far


def pair_gather(tiles):
    tiles = join(tiles, across(tiles, 2))
    far = [across(tiles, difference) for difference in (12, 8, 4)]
    tiles = join(tiles, *reversed(far))
    return join(tiles, across(tiles, 1))


def local(vis, beams, m_ra, m_dec, facet_of, tile_of, beam_of, step_size, thresholds):
    facets = lax.axis_size("ra")
    channels, dec_rows, owned, samples = vis.shape
    width = m_ra.shape[0]
    per_facet = RA_DEV // width
    beams, m_ra, m_dec, beam_of = (
        pltpu.with_memory_space_constraint(x, pltpu.HBM) for x in (beams, m_ra, m_dec, beam_of)
    )
    patch_of = facet_of[:, 0] * per_facet + tile_of
    paired = facets == 16
    if paired:
        me = lax.axis_index("ra").astype(jnp.int32)
        apart = facet_of[:, 0] ^ me
        slot_of = ((apart & 1) * (facets // 2) + (apart >> 1)) * per_facet + tile_of
        me = me.reshape(1)
        exchange, gather = pair_exchange, pair_gather
    else:
        me, slot_of = None, patch_of
        exchange = lambda sums: [lax.all_to_all(sums, "ra", split_axis=0, concat_axis=0, tiled=True)]
        gather = lambda tiles: lax.all_gather(tiles, "ra", axis=0, tiled=True)

    sums = gradient_call(patch_of, beam_of, vis, beams, m_ra, m_dec, facets, me)
    first, tiles = prox_call(exchange(*sums), thresholds, step_size, dec_rows)
    tiles = gather(tiles).reshape(facets * per_facet * channels, dec_rows, width)
    sums = gradient_call(patch_of, beam_of, vis, beams, m_ra, m_dec, facets, me, slot_of, tiles)
    return prox_call(exchange(*sums), thresholds, step_size, dec_rows, first)


def solution(mesh):
    in_specs = (
        P(None, "strip", "ra", None),
        P(None, "strip", None, None),
        P(),
        P(),
        P(("strip", "ra"), None),
        P(("strip", "ra")),
        P(("strip", "ra")),
        P(),
        P(),
    )
    out_specs = P(None, "strip", "ra")
    return jax.shard_map(local, mesh=mesh, in_specs=in_specs, out_specs=out_specs, check_vma=False)
```

```python
import functools

import jax
import jax.numpy as jnp
import numpy as np
from jax import lax
from jax.experimental import pallas as pl
from jax.experimental.pallas import tpu as pltpu
from jax.sharding import PartitionSpec as P

BASES = 4
RA_DEV = 256
GROUP = 16
PHASES = 4
LANES = 128
SPAN = LANES // PHASES
SLOTS = 3
CHUNK = 256
COLUMNS = 256

daub_coeffs = (
    (0.7071067811865476, 0.7071067811865476),
    (0.48296291314453416, 0.8365163037378079, 0.2241438680420134, -0.12940952255126037),
    (
        0.3326705529500825,
        0.8068915093110924,
        0.4598775021184914,
        -0.1350110200102546,
        -0.0854412738820267,
        0.0352262918857095,
    ),
    (
        0.2303778133088964,
        0.7148465705529155,
        0.6308807679298587,
        -0.0279837694168599,
        -0.1870348117190931,
        0.0308413818355607,
        0.0328830116668852,
        -0.010597401785069,
    ),
)


def filter_table(basis_count):
    low_pass = np.zeros((basis_count, 8))
    for basis_id in range(basis_count):
        coeffs = daub_coeffs[basis_id]
        low_pass[basis_id, : len(coeffs)] = coeffs
    high_pass = np.zeros((basis_count, 8))
    for column in range(8):
        high_pass[:, column] = (-1.0) ** column * low_pass[:, 7 - column]
    return low_pass.astype(np.float32), high_pass.astype(np.float32)


def iota(shape, axis):
    return lax.broadcasted_iota(jnp.int32, shape, axis)


def where_equal(left, right):
    return jnp.where(left == right, 1.0, 0.0)


def dot(left, right, contract=((1,), (0,))):
    return lax.dot_general(left, right, (contract, ((), ())), preferred_element_type=jnp.float32)


def phase_rows(width):
    row, column = iota((width, width), 0), iota((width, width), 1)
    span = width // PHASES
    return where_equal(column, PHASES * (row % span) + row // span).astype(jnp.bfloat16)


def back_matrix(m_dec):
    size = GROUP * GROUP
    pick = where_equal(iota((size, GROUP), 0) % GROUP, iota((size, GROUP), 1)).astype(jnp.bfloat16)
    place = where_equal(iota((GROUP, size), 0), iota((GROUP, size), 1) // GROUP).astype(jnp.bfloat16)
    wide = dot(dot(pick, m_dec, ((1,), (1,))).astype(jnp.bfloat16), place)
    return (wide * where_equal(iota((size, size), 0) // GROUP, iota((size, size), 1) % GROUP)).astype(jnp.bfloat16)


def forward_matrix(m_dec):
    size = GROUP * GROUP
    pick = where_equal(iota((size, GROUP), 0) // GROUP, iota((size, GROUP), 1)).astype(jnp.bfloat16)
    place = where_equal(iota((GROUP, size), 0), iota((GROUP, size), 1) % GROUP).astype(jnp.bfloat16)
    wide = dot(dot(pick, m_dec).astype(jnp.bfloat16), place)
    return (wide * where_equal(iota((size, size), 0) % GROUP, iota((size, size), 1) // GROUP)).astype(jnp.bfloat16)


def swap_rows(size_a, size_b):
    size = size_a * size_b
    row, column = iota((size, size), 0), iota((size, size), 1)
    return where_equal((row % size_a) * size_b + row // size_a, column).astype(jnp.bfloat16)


def accumulate(patch_ref, beam_ref, table, dec_back, ra_out, total):
    dec_rows = total.shape[1]
    for m in range(0, dec_back.shape[0], CHUNK):
        patches = dot(dec_back[m : m + CHUNK], ra_out[...])
        for i in range(CHUNK // dec_rows):
            p = m // dec_rows + i
            patch = patches[i * dec_rows : (i + 1) * dec_rows]
            patch_grad = (table[beam_ref[p]].astype(jnp.float32) * patch).astype(jnp.bfloat16).astype(jnp.float32)
            total[patch_ref[p]] = total[patch_ref[p]] + patch_grad


def write_sums(total, me_ref, outs):
    tiles, dec_rows, width = total.shape
    from_left = iota((dec_rows, width), 1) % SPAN >= SPAN // 2
    paired = me_ref is not None

    def one_facet(index, carry):
        for side, out_ref in enumerate(outs):
            facet = (2 * index + side) ^ me_ref[0] if paired else index
            own = 2 * facet
            left, right = lax.rem(own + tiles - 1, tiles), lax.rem(own + 2, tiles)
            out_ref[index, 0, 0] = total[own].astype(out_ref.dtype)
            out_ref[index, 1, 0] = total[own + 1].astype(out_ref.dtype)
            out_ref[index, 2, 0] = jnp.where(from_left, total[left], total[right]).astype(out_ref.dtype)
        return carry

    lax.fori_loop(0, outs[0].shape[0], one_facet, 0, unroll=4)


def vis_copy(vis_ref, held, arrived, channel):
    return pltpu.make_async_copy(vis_ref.at[channel], held.at[channel], arrived.at[channel])


def wait_and_start_next(vis_ref, held, arrived, channel):
    vis_copy(vis_ref, held, arrived, channel).wait()

    @pl.when(channel + 1 < held.shape[0])
    def _():
        vis_copy(vis_ref, held, arrived, channel + 1).start()


def group_data(held, channel, group, columns):
    data = held[channel, :, group * GROUP : (group + 1) * GROUP, columns]
    return data.reshape(-1, data.shape[-1])


def blocks(owned, samples):
    groups = owned // GROUP
    for group in range(groups):
        for k in range(0, samples, COLUMNS):
            yield group, slice(k, k + COLUMNS)


def first_gradient_kernel(paired, patch_ref, beam_ref, *refs):
    me_ref, refs = (refs[0], refs[1:]) if paired else (None, refs)
    vis_ref, beams_ref, m_ra_ref, m_dec_ref, *refs = refs
    outs, refs = refs[: 1 + paired], refs[1 + paired :]
    table, back, forward, ra_out, ra_in, total, dec_back, swap, order, held, arrived = refs
    channel = pl.program_id(0)
    channels, dec_rows, owned, samples = held.shape
    width = m_ra_ref.shape[0]
    beam_count = beams_ref.shape[2]
    size = GROUP * dec_rows

    @pl.when(channel == 0)
    def _():
        vis_copy(vis_ref, held, arrived, 0).start()
        back[...] = back_matrix(m_dec_ref[...])
        forward[...] = forward_matrix(m_dec_ref[...])
        order[...] = phase_rows(width)
        swap[...] = swap_rows(dec_rows, beam_count)
        ra_out[...] = dot(m_ra_ref[...], order[...], ((0,), (1,))).astype(jnp.bfloat16)
        ra_in[...] = dot(order[...], m_ra_ref[...]).astype(jnp.bfloat16)

    swapped = dot(swap[...], beams_ref[0].reshape(dec_rows * beam_count, width)).astype(jnp.bfloat16)
    ordered = dot(swapped, order[...], ((1,), (1,))).astype(jnp.bfloat16)
    table[0] = ordered.reshape(beam_count, dec_rows, width)
    total[...] = jnp.zeros_like(total)
    wait_and_start_next(vis_ref, held, arrived, channel)
    for group, columns in blocks(owned, samples):
        rows = slice(group * size, (group + 1) * size)
        dec_back[rows, columns] = dot(back[...], group_data(held, channel, group, columns)).astype(jnp.bfloat16)
    accumulate(patch_ref, beam_ref, table.at[0], dec_back, ra_out, total)
    write_sums(total, me_ref, outs)


def second_gradient_kernel(paired, patch_ref, beam_ref, slot_ref, *refs):
    me_ref, refs = (refs[0], refs[1:]) if paired else (None, refs)
    vis_ref, table, back, forward, ra_out, ra_in, tiles_ref, *refs = refs
    outs, refs = refs[: 1 + paired], refs[1 + paired :]
    total, rows_k, weighted, held, arrived = refs
    channel = pl.program_id(0)
    channels, dec_rows, owned, samples = held.shape
    size = GROUP * dec_rows

    @pl.when(channel == 0)
    def _():
        vis_copy(vis_ref, held, arrived, 0).start()

    total[...] = jnp.zeros_like(total)
    for p in range(owned):
        weighted[p * dec_rows : (p + 1) * dec_rows] = (
            table[0, beam_ref[p]].astype(jnp.float32)
            * tiles_ref[slot_ref[p] * channels + channel].astype(jnp.float32)
        ).astype(jnp.bfloat16)
    for m in range(0, owned * dec_rows, CHUNK):
        rows_k[m : m + CHUNK] = dot(weighted[m : m + CHUNK], ra_in[...]).astype(jnp.bfloat16)
    wait_and_start_next(vis_ref, held, arrived, channel)
    for group, columns in blocks(owned, samples):
        rows = slice(group * size, (group + 1) * size)
        predicted = dot(forward[...], rows_k[rows, columns])
        data = group_data(held, channel, group, columns).astype(jnp.float32)
        rows_k[rows, columns] = (predicted - data).astype(jnp.bfloat16)
    for group, columns in blocks(owned, samples):
        rows = slice(group * size, (group + 1) * size)
        rows_k[rows, columns] = dot(back[...], rows_k[rows, columns]).astype(jnp.bfloat16)
    accumulate(patch_ref, beam_ref, table.at[0], rows_k, ra_out, total)
    write_sums(total, me_ref, outs)


def gradient_call(scalars, vis, operands, facets, paired, second):
    channels, dec_rows, owned, samples = vis.shape
    width = LANES
    beam_count = operands[0].shape[2] if not second else operands[0].shape[1]
    size = GROUP * dec_rows
    whole = lambda shape: pl.BlockSpec(shape, lambda c, *_: (0,) * len(shape))
    channel_block = lambda *shape: pl.BlockSpec((1,) + shape, lambda c, *_: (c,) + (0,) * len(shape))
    kept, sum_type = (facets // 2, jnp.float32) if paired else (facets, jnp.bfloat16)
    out_shapes = [jax.ShapeDtypeStruct((kept, SLOTS, channels, dec_rows, width), sum_type)] * (1 + paired)
    out_specs = [pl.BlockSpec((kept, SLOTS, 1, dec_rows, width), lambda c, *_: (0, 0, c, 0, 0))] * (1 + paired)
    in_specs = [pl.BlockSpec(memory_space=pltpu.HBM)]
    in_specs.append(channel_block(*operands[0].shape[1:]))
    if not second:
        shared = [(size, size), (size, size), (samples, width), (width, samples)]
        out_shapes.append(jax.ShapeDtypeStruct((channels, beam_count, dec_rows, width), jnp.bfloat16))
        out_specs.append(channel_block(beam_count, dec_rows, width))
        out_shapes += [jax.ShapeDtypeStruct(shape, jnp.bfloat16) for shape in shared]
        out_specs += [whole(shape) for shape in shared]
    in_specs += [whole(operand.shape) for operand in operands[1:]]
    scratch = [
        pltpu.VMEM((2 * facets, dec_rows, width), jnp.float32),
        pltpu.VMEM((owned * dec_rows, samples), jnp.bfloat16),
    ]
    if second:
        scratch.append(pltpu.VMEM((owned * dec_rows, width), jnp.bfloat16))
    else:
        scratch += [pltpu.VMEM((size, size), jnp.bfloat16), pltpu.VMEM((width, width), jnp.bfloat16)]
    scratch += [pltpu.VMEM(vis.shape, jnp.bfloat16), pltpu.SemaphoreType.DMA((channels,))]
    work = channels * owned * samples * dec_rows
    return pl.pallas_call(
        functools.partial(second_gradient_kernel if second else first_gradient_kernel, paired),
        out_shape=out_shapes,
        grid_spec=pltpu.PrefetchScalarGridSpec(
            num_scalar_prefetch=len(scalars),
            grid=(channels,),
            in_specs=in_specs,
            out_specs=out_specs,
            scratch_shapes=scratch,
        ),
        compiler_params=pltpu.CompilerParams(vmem_limit_bytes=48 << 20),
        cost_estimate=pl.CostEstimate(
            flops=(4 if second else 2) * 256 * work, bytes_accessed=2 * work, transcendentals=0
        ),
        name="second_gradient" if second else "first_gradient",
    )(*scalars, vis, *operands)


def shrink(values, bound):
    return values - jnp.clip(values, -bound, bound)


def combine(terms):
    total = None
    for factor, value in terms:
        if factor == 0.0:
            continue
        term = value * jnp.float32(factor)
        total = term if total is None else total + term
    return total


def dec_analysis(rows, low, high):
    count = len(rows)
    half = count // 2
    lows = [combine([(low[j], rows[(2 * k + j) % count]) for j in range(8)]) for k in range(half)]
    highs = [combine([(high[j], rows[(2 * k + j) % count]) for j in range(8)]) for k in range(half)]
    return lows + highs


def dec_synthesis(rows, low, high):
    count = len(rows)
    half = count // 2
    gathered = [[] for _ in range(count)]
    for k in range(half):
        for j in range(8):
            gathered[(2 * k + j) % count].append((low[j], rows[k]))
            gathered[(2 * k + j) % count].append((high[j], rows[half + k]))
    return [combine(terms) for terms in gathered]


def prox_kernel(second, parts, *refs):
    part_refs, (thresholds_ref, step_ref, *refs) = refs[:parts], refs[parts:]
    first_ref, out_ref, summed, columns, natural, tops = refs
    rows = part_refs[0].shape[1]
    dec_rows = first_ref.shape[1]
    channels = step_ref.shape[0]
    half = 4
    shape = (8, LANES)
    upper = iota(shape, 0) >= half
    channel = iota(shape, 0) % half
    lane = iota(shape, 1)
    block = lane // SPAN

    total = part_refs[0][0].astype(jnp.float32)
    for part_ref in part_refs[1:]:
        total = total + part_ref[0].astype(jnp.float32)
    for index in range(1, part_refs[0].shape[0]):
        total = total + part_refs[0][index].astype(jnp.float32)
    summed[:rows] = total
    summed[rows:] = total[rows - channels * dec_rows :]

    def spread(scalars):
        value = jnp.full(shape, scalars[channels - 1], jnp.float32)
        for c in range(channels - 1):
            value = jnp.where(channel == c, scalars[c], value)
        return value

    step = spread([step_ref[c] for c in range(channels)])
    roll = lambda value, shift: pltpu.roll(value, shift % LANES, 1)
    swap = lambda value: pltpu.roll(value, half, 0)
    halves = lambda low, high: jnp.where(upper, high, low)

    for d in range(dec_rows):
        own = summed[pl.ds(d, 8, stride=dec_rows), :]
        edge = summed[pl.ds(8 * dec_rows + d, 8, stride=dec_rows), :]
        other = swap(own)
        own_32, own_64 = roll(own, -32), roll(own, -64)
        other_up, other_64 = roll(other, 32), roll(other, -64)
        edge_32, edge_64, edge_96 = roll(edge, 32), roll(edge, 64), roll(edge, 96)
        evens = jnp.where(
            block == 0,
            halves(own, other_64),
            jnp.where(
                block == 1,
                halves(other_up, own_32),
                jnp.where(block == 2, halves(edge_64, edge), halves(edge_96, edge_32)),
            ),
        )
        odds = jnp.where(
            block == 0,
            halves(own_32, other_up),
            jnp.where(
                block == 1,
                halves(other, own_64),
                jnp.where(block == 2, halves(edge_32, edge_96), halves(edge_64, edge)),
            ),
        )
        evens, odds = step * evens, step * odds
        if second:
            evens, odds = first_ref[0, d] - evens, first_ref[1, d] - odds
        columns[0, d], columns[1, d] = evens, odds
        for e, value in enumerate((evens, odds)):
            later = roll(value, -1)
            middle = swap(halves(later, value))
            columns[2 + e, d] = middle
            columns[4 + e, d] = later
            columns[6 + e, d] = roll(middle, -1)

    low_pass, high_pass = filter_table(BASES)
    for b in range(BASES):
        low, high = [float(v) for v in low_pass[b]], [float(v) for v in high_pass[b]]
        bound = spread([thresholds_ref[b, c] for c in range(channels)]) * step
        ra_low = [combine([(low[j], columns[j, d]) for j in range(8)]) for d in range(dec_rows)]
        ra_high = [combine([(high[j], columns[j, d]) for j in range(8)]) for d in range(dec_rows)]
        coarse_a = dec_analysis(ra_low, low, high)
        coarse_b = [shrink(v, bound) for v in dec_analysis(ra_high, low, high)]
        smooth, detail = coarse_a[: dec_rows // 2], [shrink(v, bound) for v in coarse_a[dec_rows // 2 :]]
        pair = lambda even, odd: jnp.where(upper, jnp.float32(odd), jnp.float32(even))
        pair_sum = lambda values, factors: sum(pair(*f) * v for f, v in zip(factors, values) if f != (0.0, 0.0))
        fine = []
        for value in smooth:
            moved = [value] + [roll(value, -i) for i in (1, 2, 3)]
            lows = pair_sum(moved, [(low[2 * i], low[2 * i + 1]) for i in range(4)])
            highs = pair_sum(moved, [(high[2 * i], high[2 * i + 1]) for i in range(4)])
            fine.append(halves(lows, highs) + swap(halves(highs, lows)))
        fine = [shrink(v, bound) for v in dec_analysis(fine, low, high)]
        fine = dec_synthesis(fine, low, high)
        smooth = []
        for value in fine:
            moved = [value] + [roll(value, i) for i in (1, 2, 3)]
            evens = pair_sum(moved, [(low[2 * i], high[2 * i]) for i in range(4)])
            odds = pair_sum(moved, [(low[2 * i + 1], high[2 * i + 1]) for i in range(4)])
            smooth.append(halves(evens, odds) + swap(halves(odds, evens)))
        top_low = dec_synthesis(smooth + detail, low, high)
        top_high = dec_synthesis(coarse_b, low, high)
        for d in range(dec_rows):
            tops[b, 0, d], tops[b, 1, d] = top_low[d], top_high[d]

    for d in range(dec_rows):
        images = []
        for e in range(2):
            parts = [
                combine(
                    [(float(low_pass[b, 2 * i + e]), tops[b, 0, d]) for b in range(BASES)]
                    + [(float(high_pass[b, 2 * i + e]), tops[b, 1, d]) for b in range(BASES)]
                )
                for i in range(4)
            ]
            other = swap(parts[1] + roll(parts[3], 1))
            value = parts[0] + roll(parts[2], 1) + halves(roll(other, 1), other)
            images.append(jnp.maximum(value * (1.0 / BASES), 0.0))
        evens, odds = images
        if not second:
            first_ref[0, d], first_ref[1, d] = evens, odds
        even_other, odd_other = swap(evens), swap(odds)
        value = jnp.where(
            block == 0,
            halves(evens, roll(even_other, -32)),
            jnp.where(
                block == 1,
                halves(roll(odds, 32), odd_other),
                jnp.where(
                    block == 2,
                    halves(roll(even_other, 64), roll(evens, 32)),
                    halves(roll(odd_other, 96), roll(odds, 64)),
                ),
            ),
        )
        natural[pl.ds(d, 8, stride=dec_rows), :] = value
    if second:
        order = phase_rows(LANES).astype(jnp.float32)
        image = lax.dot_general(
            natural[...],
            order,
            (((1,), (0,)), ((), ())),
            precision=lax.Precision.HIGHEST,
            preferred_element_type=jnp.float32,
        )
        for tile in range(2):
            for c in range(channels):
                start = (tile * channels + c) * dec_rows
                out_ref[c, :, tile * LANES : (tile + 1) * LANES] = image[start : start + dec_rows]
    else:
        out_ref[...] = natural[...].astype(jnp.bfloat16)


def prox_call(received, thresholds, step_size, dec_rows, first=None):
    second = first is not None
    channels = step_size.shape[0]
    received = [part.reshape(-1, SLOTS * channels * dec_rows, LANES) for part in received]
    vmem = pl.BlockSpec(memory_space=pltpu.VMEM)
    smem = pl.BlockSpec(memory_space=pltpu.SMEM)
    held = jax.ShapeDtypeStruct((2, dec_rows, 8, LANES), jnp.float32)
    if second:
        out_shape = jax.ShapeDtypeStruct((channels, dec_rows, RA_DEV), jnp.float32)
        out_specs = vmem
    else:
        out_shape = (held, jax.ShapeDtypeStruct((2 * channels * dec_rows, LANES), jnp.bfloat16))
        out_specs = (vmem, vmem)
    return pl.pallas_call(
        functools.partial(prox_kernel, second, len(received)),
        out_shape=out_shape,
        in_specs=[vmem] * len(received) + [smem, smem] + ([vmem] if second else []),
        out_specs=out_specs,
        scratch_shapes=[
            pltpu.VMEM((4 * channels * dec_rows, LANES), jnp.float32),
            pltpu.VMEM((8, dec_rows, 8, LANES), jnp.float32),
            pltpu.VMEM((2 * channels * dec_rows, LANES), jnp.float32),
            pltpu.VMEM((BASES, 2, dec_rows, 8, LANES), jnp.float32),
        ],
        compiler_params=pltpu.CompilerParams(vmem_limit_bytes=32 << 20),
        name="second_prox" if second else "first_prox",
    )(*received, thresholds, step_size, *([first] if second else []))


def fold_kernel(keep_ref, got_ref, *outs):
    for index, out_ref in enumerate(outs):
        out_ref[0] = (keep_ref[index] + got_ref[index]).astype(out_ref.dtype)


def join_kernel(*refs):
    *parts, out_ref = refs
    start = 0
    for part_ref in parts:
        out_ref[start : start + part_ref.shape[0]] = part_ref[...]
        start += part_ref.shape[0]


def small_call(kernel, name, out_shape, *operands):
    vmem = pl.BlockSpec(memory_space=pltpu.VMEM)
    return pl.pallas_call(
        kernel,
        out_shape=out_shape,
        in_specs=[vmem] * len(operands),
        out_specs=jax.tree.map(lambda _: vmem, out_shape),
        compiler_params=pltpu.CompilerParams(vmem_limit_bytes=16 << 20),
        name=name,
    )(*operands)


def join(*parts):
    rows = sum(part.shape[0] for part in parts)
    shape = jax.ShapeDtypeStruct((rows,) + parts[0].shape[1:], parts[0].dtype)
    return small_call(join_kernel, "join", shape, *parts)


def across(value, difference):
    count = lax.axis_size("ra")
    return lax.ppermute(value, "ra", [(source, source ^ difference) for source in range(count)])


def pair_exchange(keep, send):
    got = across(send, 1)
    shape = (1,) + keep.shape[1:]
    kinds = [jnp.float32] + [jnp.bfloat16] * (keep.shape[0] - 1)
    parts = small_call(fold_kernel, "fold", [jax.ShapeDtypeStruct(shape, kind) for kind in kinds], keep, got)
    far = [across(parts[index], 2 * index) for index in reversed(range(1, len(parts)))]
    return [parts[0]] + far


def pair_gather(tiles):
    tiles = join(tiles, across(tiles, 2))
    far = [across(tiles, difference) for difference in (12, 8, 4)]
    tiles = join(tiles, *reversed(far))
    return join(tiles, across(tiles, 1))


def local(vis, beams, m_ra, m_dec, facet_of, tile_of, beam_of, step_size, thresholds):
    facets = lax.axis_size("ra")
    channels, dec_rows, owned, samples = vis.shape
    width = m_ra.shape[0]
    per_facet = RA_DEV // width
    beams, m_ra, m_dec, beam_of = (
        pltpu.with_memory_space_constraint(x, pltpu.HBM) for x in (beams, m_ra, m_dec, beam_of)
    )
    patch_of = facet_of[:, 0] * per_facet + tile_of
    paired = facets == 16
    if paired:
        me = lax.axis_index("ra").astype(jnp.int32)
        apart = facet_of[:, 0] ^ me
        slot_of = ((apart & 1) * (facets // 2) + (apart >> 1)) * per_facet + tile_of
        me = me.reshape(1)
        exchange, gather = pair_exchange, pair_gather
    else:
        me, slot_of = None, patch_of
        exchange = lambda sums: [lax.all_to_all(sums, "ra", split_axis=0, concat_axis=0, tiled=True)]
        gather = lambda tiles: lax.all_gather(tiles, "ra", axis=0, tiled=True)

    base = [me] if paired else []
    sent = 1 + paired
    sums = gradient_call([patch_of, beam_of] + base, vis, [beams, m_ra, m_dec], facets, paired, False)
    sums, shared = sums[:sent], sums[sent:]
    first, tiles = prox_call(exchange(*sums), thresholds, step_size, dec_rows)
    tiles = gather(tiles).reshape(facets * per_facet * channels, dec_rows, width)
    sums = gradient_call([patch_of, beam_of, slot_of] + base, vis, [*shared, tiles], facets, paired, True)
    return prox_call(exchange(*sums), thresholds, step_size, dec_rows, first)


def solution(mesh):
    in_specs = (
        P(None, "strip", "ra", None),
        P(None, "strip", None, None),
        P(),
        P(),
        P(("strip", "ra"), None),
        P(("strip", "ra")),
        P(("strip", "ra")),
        P(),
        P(),
    )
    out_specs = P(None, "strip", "ra")
    return jax.shard_map(local, mesh=mesh, in_specs=in_specs, out_specs=out_specs, check_vma=False)
```

```python
import functools

import jax
import jax.numpy as jnp
import numpy as np
from jax import lax
from jax.experimental import pallas as pl
from jax.experimental.pallas import tpu as pltpu
from jax.sharding import PartitionSpec as P

BASES = 4
RA_DEV = 256
GROUP = 16
PHASES = 4
LANES = 128
SPAN = LANES // PHASES
SLOTS = 3
COLUMNS = 256

daub_coeffs = (
    (0.7071067811865476, 0.7071067811865476),
    (0.48296291314453416, 0.8365163037378079, 0.2241438680420134, -0.12940952255126037),
    (
        0.3326705529500825,
        0.8068915093110924,
        0.4598775021184914,
        -0.1350110200102546,
        -0.0854412738820267,
        0.0352262918857095,
    ),
    (
        0.2303778133088964,
        0.7148465705529155,
        0.6308807679298587,
        -0.0279837694168599,
        -0.1870348117190931,
        0.0308413818355607,
        0.0328830116668852,
        -0.010597401785069,
    ),
)


def filter_table(basis_count):
    low_pass = np.zeros((basis_count, 8))
    for basis_id in range(basis_count):
        coeffs = daub_coeffs[basis_id]
        low_pass[basis_id, : len(coeffs)] = coeffs
    high_pass = np.zeros((basis_count, 8))
    for column in range(8):
        high_pass[:, column] = (-1.0) ** column * low_pass[:, 7 - column]
    return low_pass.astype(np.float32), high_pass.astype(np.float32)


def iota(shape, axis):
    return lax.broadcasted_iota(jnp.int32, shape, axis)


def where_equal(left, right):
    return jnp.where(left == right, 1.0, 0.0)


def dot(left, right, contract=((1,), (0,))):
    return lax.dot_general(left, right, (contract, ((), ())), preferred_element_type=jnp.float32)


def phase_rows(width):
    row, column = iota((width, width), 0), iota((width, width), 1)
    span = width // PHASES
    return where_equal(column, PHASES * (row % span) + row // span).astype(jnp.bfloat16)


def back_matrix(m_dec):
    size = GROUP * GROUP
    pick = where_equal(iota((size, GROUP), 0) % GROUP, iota((size, GROUP), 1)).astype(jnp.bfloat16)
    place = where_equal(iota((GROUP, size), 0), iota((GROUP, size), 1) // GROUP).astype(jnp.bfloat16)
    wide = dot(dot(pick, m_dec, ((1,), (1,))).astype(jnp.bfloat16), place)
    return (wide * where_equal(iota((size, size), 0) // GROUP, iota((size, size), 1) % GROUP)).astype(jnp.bfloat16)


def forward_matrix(m_dec):
    size = GROUP * GROUP
    pick = where_equal(iota((size, GROUP), 0) // GROUP, iota((size, GROUP), 1)).astype(jnp.bfloat16)
    place = where_equal(iota((GROUP, size), 0), iota((GROUP, size), 1) % GROUP).astype(jnp.bfloat16)
    wide = dot(dot(pick, m_dec).astype(jnp.bfloat16), place)
    return (wide * where_equal(iota((size, size), 0) % GROUP, iota((size, size), 1) // GROUP)).astype(jnp.bfloat16)


def swap_rows(size_a, size_b):
    size = size_a * size_b
    row, column = iota((size, size), 0), iota((size, size), 1)
    return where_equal((row % size_a) * size_b + row // size_a, column).astype(jnp.bfloat16)


def accumulate(facet_ref, tile_ref, beam_ref, table, dec_back, ra_out, total, group):
    dec_rows = total.shape[1]
    patches = dot(dec_back[group * GROUP * dec_rows : (group + 1) * GROUP * dec_rows], ra_out[...])
    for i in range(GROUP):
        p = group * GROUP + i
        patch = patches[i * dec_rows : (i + 1) * dec_rows]
        patch_grad = (table[beam_ref[p]].astype(jnp.float32) * patch).astype(jnp.bfloat16).astype(jnp.float32)
        tile = 2 * facet_ref[p] + tile_ref[p]
        total[tile] = total[tile] + patch_grad


def run_steps(groups, steps):
    for turn in range(groups + 2*len(steps) - 2):
        for behind, step in reversed(list(enumerate(steps))):
            if 0 <= turn - 2*behind < groups:
                step(turn - 2*behind)


def write_sums(total, me_ref, outs, channel):
    tiles, dec_rows, width = total.shape
    from_left = iota((dec_rows, width), 1) % SPAN >= SPAN // 2
    paired = me_ref is not None

    def one_facet(index, carry):
        for side, out_ref in enumerate(outs):
            facet = (2 * index + side) ^ me_ref[0] if paired else index
            own = 2 * facet
            left, right = lax.rem(own + tiles - 1, tiles), lax.rem(own + 2, tiles)
            out_ref[index, 0, channel] = total[own].astype(out_ref.dtype)
            out_ref[index, 1, channel] = total[own + 1].astype(out_ref.dtype)
            out_ref[index, 2, channel] = jnp.where(from_left, total[left], total[right]).astype(out_ref.dtype)
        return carry

    lax.fori_loop(0, outs[0].shape[0], one_facet, 0, unroll=4)


def vis_copy(vis_ref, held, arrived, channel):
    return pltpu.make_async_copy(vis_ref.at[channel], held.at[channel], arrived.at[channel])


def wait_and_start_next(vis_ref, held, arrived, channel):
    vis_copy(vis_ref, held, arrived, channel).wait()

    @pl.when(channel + 1 < held.shape[0])
    def _():
        vis_copy(vis_ref, held, arrived, channel + 1).start()


def group_data(held, channel, group, columns):
    data = held[channel, :, group * GROUP : (group + 1) * GROUP, columns]
    return data.reshape(-1, data.shape[-1])


def column_blocks(samples):
    return [slice(k, k + COLUMNS) for k in range(0, samples, COLUMNS)]


def first_gradient_kernel(paired, facet_ref, tile_ref, beam_ref, *refs):
    me_ref, refs = (refs[0], refs[1:]) if paired else (None, refs)
    vis_ref, *small_refs = refs[:4]
    outs, refs = refs[4 : 5 + paired], refs[5 + paired :]
    table, back, forward, ra_out, ra_in, total, dec_back, swap, order, beams, m_ra, m_dec, held, arrived, came = refs
    channels, dec_rows, owned, samples = held.shape
    width = m_ra.shape[0]
    beam_count = beams.shape[2]
    size = GROUP * dec_rows
    copies = [
        pltpu.make_async_copy(source, target, came.at[index])
        for index, (source, target) in enumerate(zip(small_refs, (beams, m_ra, m_dec)))
    ]
    for copy in reversed(copies):
        copy.start()
    vis_copy(vis_ref, held, arrived, 0).start()
    order[...] = phase_rows(width)
    swap[...] = swap_rows(dec_rows, beam_count)
    for copy in copies:
        copy.wait()
    back[...] = back_matrix(m_dec[...])
    forward[...] = forward_matrix(m_dec[...])
    ra_out[...] = dot(m_ra[...], order[...], ((0,), (1,))).astype(jnp.bfloat16)
    ra_in[...] = dot(order[...], m_ra[...]).astype(jnp.bfloat16)

    def one_channel(channel, carry):
        swapped = dot(swap[...], beams[channel].reshape(dec_rows * beam_count, width)).astype(jnp.bfloat16)
        ordered = dot(swapped, order[...], ((1,), (1,))).astype(jnp.bfloat16)
        table[channel] = ordered.reshape(beam_count, dec_rows, width)
        total[...] = jnp.zeros_like(total)
        wait_and_start_next(vis_ref, held, arrived, channel)

        def go_back(group):
            rows = slice(group * size, (group + 1) * size)
            for columns in column_blocks(samples):
                data = group_data(held, channel, group, columns)
                dec_back[rows, columns] = dot(back[...], data).astype(jnp.bfloat16)

        gather = functools.partial(
            accumulate, facet_ref, tile_ref, beam_ref, table.at[channel], dec_back, ra_out, total
        )
        run_steps(owned // GROUP, [go_back, gather])
        write_sums(total, me_ref, outs, channel)
        return carry

    lax.fori_loop(0, channels, one_channel, 0)


def second_gradient_kernel(paired, facet_ref, tile_ref, beam_ref, *refs):
    me_ref, refs = (refs[0], refs[1:]) if paired else (None, refs)
    vis_ref, table, back, forward, ra_out, ra_in, tiles_ref, *refs = refs
    outs, refs = refs[: 1 + paired], refs[1 + paired :]
    total, rows_k, held, arrived = refs
    channels, dec_rows, owned, samples = held.shape
    size = GROUP * dec_rows
    vis_copy(vis_ref, held, arrived, 0).start()

    def one_channel(channel, carry):
        total[...] = jnp.zeros_like(total)

        def go_in(group):
            weighted = []
            for p in range(group * GROUP, (group + 1) * GROUP):
                facet = facet_ref[p] ^ me_ref[0] if paired else facet_ref[p]
                tile = tiles_ref[(2 * facet + tile_ref[p]) * channels + channel].astype(jnp.float32)
                weighted.append((table[channel, beam_ref[p]].astype(jnp.float32) * tile).astype(jnp.bfloat16))
            weighted = jnp.concatenate(weighted, axis=0)
            for columns in column_blocks(samples):
                along = dot(weighted, ra_in[:, columns]).astype(jnp.bfloat16)
                rows_k[group * size : (group + 1) * size, columns] = along

        def go_forward(group):
            if group == 0:
                wait_and_start_next(vis_ref, held, arrived, channel)
            rows = slice(group * size, (group + 1) * size)
            for columns in column_blocks(samples):
                predicted = dot(forward[...], rows_k[rows, columns])
                data = group_data(held, channel, group, columns).astype(jnp.float32)
                rows_k[rows, columns] = (predicted - data).astype(jnp.bfloat16)

        def go_back(group):
            rows = slice(group * size, (group + 1) * size)
            for columns in column_blocks(samples):
                rows_k[rows, columns] = dot(back[...], rows_k[rows, columns]).astype(jnp.bfloat16)

        gather = functools.partial(
            accumulate, facet_ref, tile_ref, beam_ref, table.at[channel], rows_k, ra_out, total
        )
        run_steps(owned // GROUP, [go_in, go_forward, go_back, gather])
        write_sums(total, me_ref, outs, channel)
        return carry

    lax.fori_loop(0, channels, one_channel, 0)


def gradient_call(scalars, vis, operands, facets, paired, second):
    channels, dec_rows, owned, samples = vis.shape
    width = LANES
    size = GROUP * dec_rows
    bf16 = jnp.bfloat16
    vmem, hbm = pl.BlockSpec(memory_space=pltpu.VMEM), pl.BlockSpec(memory_space=pltpu.HBM)
    kept, sum_type = (facets // 2, jnp.float32) if paired else (facets, bf16)
    out_shapes = [jax.ShapeDtypeStruct((kept, SLOTS, channels, dec_rows, width), sum_type)] * (1 + paired)
    scratch = [
        pltpu.VMEM((2 * facets, dec_rows, width), jnp.float32),
        pltpu.VMEM((owned * dec_rows, samples), bf16),
    ]
    if second:
        in_specs = [hbm] + [vmem] * len(operands)
    else:
        in_specs = [hbm] * (1 + len(operands))
        beam_count = operands[0].shape[2]
        shared = [(channels, beam_count, dec_rows, width), (size, size), (size, size), (samples, width), (width, samples)]
        out_shapes += [jax.ShapeDtypeStruct(shape, bf16) for shape in shared]
        scratch += [pltpu.VMEM((size, size), bf16), pltpu.VMEM((width, width), bf16)]
        scratch += [pltpu.VMEM(operand.shape, bf16) for operand in operands]
    scratch += [pltpu.VMEM(vis.shape, bf16), pltpu.SemaphoreType.DMA((channels,))]
    if not second:
        scratch.append(pltpu.SemaphoreType.DMA((len(operands),)))
    work = channels * owned * samples * dec_rows
    return pl.pallas_call(
        functools.partial(second_gradient_kernel if second else first_gradient_kernel, paired),
        out_shape=out_shapes,
        grid_spec=pltpu.PrefetchScalarGridSpec(
            num_scalar_prefetch=len(scalars),
            grid=(),
            in_specs=in_specs,
            out_specs=[vmem] * len(out_shapes),
            scratch_shapes=scratch,
        ),
        compiler_params=pltpu.CompilerParams(vmem_limit_bytes=40 << 20),
        cost_estimate=pl.CostEstimate(
            flops=(4 if second else 2) * 256 * work, bytes_accessed=2 * work, transcendentals=0
        ),
        name="second_gradient" if second else "first_gradient",
    )(*scalars, vis, *operands)


def shrink(values, bound):
    return values - jnp.clip(values, -bound, bound)


def combine(terms):
    total = None
    for factor, value in terms:
        if factor == 0.0:
            continue
        term = value * jnp.float32(factor)
        total = term if total is None else total + term
    return total


def dec_analysis(rows, low, high):
    count = len(rows)
    half = count // 2
    lows = [combine([(low[j], rows[(2 * k + j) % count]) for j in range(8)]) for k in range(half)]
    highs = [combine([(high[j], rows[(2 * k + j) % count]) for j in range(8)]) for k in range(half)]
    return lows + highs


def dec_synthesis(rows, low, high):
    count = len(rows)
    half = count // 2
    gathered = [[] for _ in range(count)]
    for k in range(half):
        for j in range(8):
            gathered[(2 * k + j) % count].append((low[j], rows[k]))
            gathered[(2 * k + j) % count].append((high[j], rows[half + k]))
    return [combine(terms) for terms in gathered]


def prox_kernel(second, parts, *refs):
    part_refs, (thresholds_ref, step_ref, *refs) = refs[:parts], refs[parts:]
    first_ref, out_ref, summed, columns, natural, tops = refs
    rows = part_refs[0].shape[1]
    dec_rows = first_ref.shape[1]
    channels = step_ref.shape[0]
    half = 4
    shape = (8, LANES)
    upper = iota(shape, 0) >= half
    channel = iota(shape, 0) % half
    lane = iota(shape, 1)
    block = lane // SPAN

    total = part_refs[0][0].astype(jnp.float32)
    for part_ref in part_refs[1:]:
        total = total + part_ref[0].astype(jnp.float32)
    for index in range(1, part_refs[0].shape[0]):
        total = total + part_refs[0][index].astype(jnp.float32)
    summed[:rows] = total
    summed[rows:] = total[rows - channels * dec_rows :]

    def spread(scalars):
        value = jnp.full(shape, scalars[channels - 1], jnp.float32)
        for c in range(channels - 1):
            value = jnp.where(channel == c, scalars[c], value)
        return value

    step = spread([step_ref[c] for c in range(channels)])
    roll = lambda value, shift: pltpu.roll(value, shift % LANES, 1)
    swap = lambda value: pltpu.roll(value, half, 0)
    halves = lambda low, high: jnp.where(upper, high, low)

    for d in range(dec_rows):
        own = summed[pl.ds(d, 8, stride=dec_rows), :]
        edge = summed[pl.ds(8 * dec_rows + d, 8, stride=dec_rows), :]
        other = swap(own)
        own_32, own_64 = roll(own, -32), roll(own, -64)
        other_up, other_64 = roll(other, 32), roll(other, -64)
        edge_32, edge_64, edge_96 = roll(edge, 32), roll(edge, 64), roll(edge, 96)
        evens = jnp.where(
            block == 0,
            halves(own, other_64),
            jnp.where(
                block == 1,
                halves(other_up, own_32),
                jnp.where(block == 2, halves(edge_64, edge), halves(edge_96, edge_32)),
            ),
        )
        odds = jnp.where(
            block == 0,
            halves(own_32, other_up),
            jnp.where(
                block == 1,
                halves(other, own_64),
                jnp.where(block == 2, halves(edge_32, edge_96), halves(edge_64, edge)),
            ),
        )
        evens, odds = step * evens, step * odds
        if second:
            evens, odds = first_ref[0, d] - evens, first_ref[1, d] - odds
        columns[0, d], columns[1, d] = evens, odds
        for e, value in enumerate((evens, odds)):
            later = roll(value, -1)
            middle = swap(halves(later, value))
            columns[2 + e, d] = middle
            columns[4 + e, d] = later
            columns[6 + e, d] = roll(middle, -1)

    low_pass, high_pass = filter_table(BASES)
    for b in range(BASES):
        low, high = [float(v) for v in low_pass[b]], [float(v) for v in high_pass[b]]
        bound = spread([thresholds_ref[b, c] for c in range(channels)]) * step
        ra_low = [combine([(low[j], columns[j, d]) for j in range(8)]) for d in range(dec_rows)]
        ra_high = [combine([(high[j], columns[j, d]) for j in range(8)]) for d in range(dec_rows)]
        coarse_a = dec_analysis(ra_low, low, high)
        coarse_b = [shrink(v, bound) for v in dec_analysis(ra_high, low, high)]
        smooth, detail = coarse_a[: dec_rows // 2], [shrink(v, bound) for v in coarse_a[dec_rows // 2 :]]
        pair = lambda even, odd: jnp.where(upper, jnp.float32(odd), jnp.float32(even))
        pair_sum = lambda values, factors: sum(pair(*f) * v for f, v in zip(factors, values) if f != (0.0, 0.0))
        fine = []
        for value in smooth:
            moved = [value] + [roll(value, -i) for i in (1, 2, 3)]
            lows = pair_sum(moved, [(low[2 * i], low[2 * i + 1]) for i in range(4)])
            highs = pair_sum(moved, [(high[2 * i], high[2 * i + 1]) for i in range(4)])
            fine.append(halves(lows, highs) + swap(halves(highs, lows)))
        fine = [shrink(v, bound) for v in dec_analysis(fine, low, high)]
        fine = dec_synthesis(fine, low, high)
        smooth = []
        for value in fine:
            moved = [value] + [roll(value, i) for i in (1, 2, 3)]
            evens = pair_sum(moved, [(low[2 * i], high[2 * i]) for i in range(4)])
            odds = pair_sum(moved, [(low[2 * i + 1], high[2 * i + 1]) for i in range(4)])
            smooth.append(halves(evens, odds) + swap(halves(odds, evens)))
        top_low = dec_synthesis(smooth + detail, low, high)
        top_high = dec_synthesis(coarse_b, low, high)
        for d in range(dec_rows):
            tops[b, 0, d], tops[b, 1, d] = top_low[d], top_high[d]

    for d in range(dec_rows):
        images = []
        for e in range(2):
            parts = [
                combine(
                    [(float(low_pass[b, 2 * i + e]), tops[b, 0, d]) for b in range(BASES)]
                    + [(float(high_pass[b, 2 * i + e]), tops[b, 1, d]) for b in range(BASES)]
                )
                for i in range(4)
            ]
            other = swap(parts[1] + roll(parts[3], 1))
            value = parts[0] + roll(parts[2], 1) + halves(roll(other, 1), other)
            images.append(jnp.maximum(value * (1.0 / BASES), 0.0))
        evens, odds = images
        if not second:
            first_ref[0, d], first_ref[1, d] = evens, odds
        even_other, odd_other = swap(evens), swap(odds)
        value = jnp.where(
            block == 0,
            halves(evens, roll(even_other, -32)),
            jnp.where(
                block == 1,
                halves(roll(odds, 32), odd_other),
                jnp.where(
                    block == 2,
                    halves(roll(even_other, 64), roll(evens, 32)),
                    halves(roll(odd_other, 96), roll(odds, 64)),
                ),
            ),
        )
        natural[pl.ds(d, 8, stride=dec_rows), :] = value
    if second:
        order = phase_rows(LANES).astype(jnp.float32)
        image = lax.dot_general(
            natural[...],
            order,
            (((1,), (0,)), ((), ())),
            precision=lax.Precision.HIGHEST,
            preferred_element_type=jnp.float32,
        )
        for tile in range(2):
            for c in range(channels):
                start = (tile * channels + c) * dec_rows
                out_ref[c, :, tile * LANES : (tile + 1) * LANES] = image[start : start + dec_rows]
    else:
        out_ref[...] = natural[...].astype(jnp.bfloat16)


def prox_call(received, thresholds, step_size, dec_rows, first=None):
    second = first is not None
    channels = step_size.shape[0]
    received = [part.reshape(-1, SLOTS * channels * dec_rows, LANES) for part in received]
    vmem = pl.BlockSpec(memory_space=pltpu.VMEM)
    smem = pl.BlockSpec(memory_space=pltpu.SMEM)
    held = jax.ShapeDtypeStruct((2, dec_rows, 8, LANES), jnp.float32)
    if second:
        out_shape = jax.ShapeDtypeStruct((channels, dec_rows, RA_DEV), jnp.float32)
        out_specs = vmem
    else:
        out_shape = (held, jax.ShapeDtypeStruct((2 * channels * dec_rows, LANES), jnp.bfloat16))
        out_specs = (vmem, vmem)
    return pl.pallas_call(
        functools.partial(prox_kernel, second, len(received)),
        out_shape=out_shape,
        in_specs=[vmem] * len(received) + [smem, smem] + ([vmem] if second else []),
        out_specs=out_specs,
        scratch_shapes=[
            pltpu.VMEM((4 * channels * dec_rows, LANES), jnp.float32),
            pltpu.VMEM((8, dec_rows, 8, LANES), jnp.float32),
            pltpu.VMEM((2 * channels * dec_rows, LANES), jnp.float32),
            pltpu.VMEM((BASES, 2, dec_rows, 8, LANES), jnp.float32),
        ],
        compiler_params=pltpu.CompilerParams(vmem_limit_bytes=32 << 20),
        name="second_prox" if second else "first_prox",
    )(*received, thresholds, step_size, *([first] if second else []))


def fold_kernel(keep_ref, got_ref, *outs):
    for index, out_ref in enumerate(outs):
        out_ref[0] = (keep_ref[index] + got_ref[index]).astype(out_ref.dtype)


def join_kernel(*refs):
    *parts, out_ref = refs
    start = 0
    for part_ref in parts:
        out_ref[start : start + part_ref.shape[0]] = part_ref[...]
        start += part_ref.shape[0]


def weave_kernel(rows, *refs):
    *parts, out_ref = refs
    for index in range(parts[0].shape[0] // rows):
        for side, part_ref in enumerate(parts):
            start = (2 * index + side) * rows
            out_ref[start : start + rows] = part_ref[index * rows : (index + 1) * rows]


def small_call(kernel, name, out_shape, *operands):
    vmem = pl.BlockSpec(memory_space=pltpu.VMEM)
    return pl.pallas_call(
        kernel,
        out_shape=out_shape,
        in_specs=[vmem] * len(operands),
        out_specs=jax.tree.map(lambda _: vmem, out_shape),
        compiler_params=pltpu.CompilerParams(vmem_limit_bytes=16 << 20),
        name=name,
    )(*operands)


def join(*parts):
    rows = sum(part.shape[0] for part in parts)
    shape = jax.ShapeDtypeStruct((rows,) + parts[0].shape[1:], parts[0].dtype)
    return small_call(join_kernel, "join", shape, *parts)


def across(value, difference):
    count = lax.axis_size("ra")
    return lax.ppermute(value, "ra", [(source, source ^ difference) for source in range(count)])


def pair_exchange(keep, send):
    got = across(send, 1)
    shape = (1,) + keep.shape[1:]
    kinds = [jnp.float32] + [jnp.bfloat16] * (keep.shape[0] - 1)
    parts = small_call(fold_kernel, "fold", [jax.ShapeDtypeStruct(shape, kind) for kind in kinds], keep, got)
    far = [across(parts[index], 2 * index) for index in reversed(range(1, len(parts)))]
    return [parts[0]] + far


def pair_gather(tiles):
    rows = tiles.shape[0]
    tiles = join(tiles, across(tiles, 2))
    far = [across(tiles, difference) for difference in (12, 8, 4)]
    tiles = join(tiles, *reversed(far))
    shape = jax.ShapeDtypeStruct((2 * tiles.shape[0],) + tiles.shape[1:], tiles.dtype)
    return small_call(functools.partial(weave_kernel, rows), "weave", shape, tiles, across(tiles, 1))


def local(vis, beams, m_ra, m_dec, facet_of, tile_of, beam_of, step_size, thresholds):
    facets = lax.axis_size("ra")
    channels, dec_rows, owned, samples = vis.shape
    width = m_ra.shape[0]
    per_facet = RA_DEV // width
    facet_of = facet_of.reshape(owned)
    held = [vis, beams, m_ra, m_dec, facet_of, tile_of, beam_of]
    held = [pltpu.with_memory_space_constraint(array, pltpu.HBM) for array in held]
    vis, beams, m_ra, m_dec, facet_of, tile_of, beam_of = held
    paired = facets == 16
    if paired:
        base = [lax.axis_index("ra").astype(jnp.int32).reshape(1)]
        exchange, gather = pair_exchange, pair_gather
    else:
        base = []
        exchange = lambda sums: [lax.all_to_all(sums, "ra", split_axis=0, concat_axis=0, tiled=True)]
        gather = lambda tiles: lax.all_gather(tiles, "ra", axis=0, tiled=True)

    scalars = [facet_of, tile_of, beam_of] + base
    sent = 1 + paired
    sums = gradient_call(scalars, vis, [beams, m_ra, m_dec], facets, paired, False)
    sums, shared = sums[:sent], sums[sent:]
    first, tiles = prox_call(exchange(*sums), thresholds, step_size, dec_rows)
    tiles = gather(tiles).reshape(facets * per_facet * channels, dec_rows, width)
    sums = gradient_call(scalars, vis, [*shared, tiles], facets, paired, True)
    return prox_call(exchange(*sums), thresholds, step_size, dec_rows, first)


def solution(mesh):
    in_specs = (
        P(None, "strip", "ra", None),
        P(None, "strip", None, None),
        P(),
        P(),
        P(("strip", "ra"), None),
        P(("strip", "ra")),
        P(("strip", "ra")),
        P(),
        P(),
    )
    out_specs = P(None, "strip", "ra")
    return jax.shard_map(local, mesh=mesh, in_specs=in_specs, out_specs=out_specs, check_vma=False)
```

```python
import functools

import jax
import jax.numpy as jnp
import numpy as np
from jax import lax
from jax.experimental import pallas as pl
from jax.experimental.pallas import tpu as pltpu
from jax.sharding import PartitionSpec as P

BASES = 4
RA_DEV = 256
GROUP = 16
PHASES = 4
LANES = 128
SPAN = LANES // PHASES
SLOTS = 3
COLUMNS = 256

daub_coeffs = (
    (0.7071067811865476, 0.7071067811865476),
    (0.48296291314453416, 0.8365163037378079, 0.2241438680420134, -0.12940952255126037),
    (
        0.3326705529500825,
        0.8068915093110924,
        0.4598775021184914,
        -0.1350110200102546,
        -0.0854412738820267,
        0.0352262918857095,
    ),
    (
        0.2303778133088964,
        0.7148465705529155,
        0.6308807679298587,
        -0.0279837694168599,
        -0.1870348117190931,
        0.0308413818355607,
        0.0328830116668852,
        -0.010597401785069,
    ),
)


def filter_table(basis_count):
    low_pass = np.zeros((basis_count, 8))
    for basis_id in range(basis_count):
        coeffs = daub_coeffs[basis_id]
        low_pass[basis_id, : len(coeffs)] = coeffs
    high_pass = np.zeros((basis_count, 8))
    for column in range(8):
        high_pass[:, column] = (-1.0) ** column * low_pass[:, 7 - column]
    return low_pass.astype(np.float32), high_pass.astype(np.float32)


def iota(shape, axis):
    return lax.broadcasted_iota(jnp.int32, shape, axis)


def where_equal(left, right):
    return jnp.where(left == right, 1.0, 0.0)


def dot(left, right, contract=((1,), (0,))):
    return lax.dot_general(left, right, (contract, ((), ())), preferred_element_type=jnp.float32)


def phase_rows(width):
    row, column = iota((width, width), 0), iota((width, width), 1)
    span = width // PHASES
    return where_equal(column, PHASES * (row % span) + row // span).astype(jnp.bfloat16)


def back_matrix(m_dec):
    size = GROUP * GROUP
    pick = where_equal(iota((size, GROUP), 0) % GROUP, iota((size, GROUP), 1)).astype(jnp.bfloat16)
    place = where_equal(iota((GROUP, size), 0), iota((GROUP, size), 1) // GROUP).astype(jnp.bfloat16)
    wide = dot(dot(pick, m_dec, ((1,), (1,))).astype(jnp.bfloat16), place)
    return (wide * where_equal(iota((size, size), 0) // GROUP, iota((size, size), 1) % GROUP)).astype(jnp.bfloat16)


def forward_matrix(m_dec):
    size = GROUP * GROUP
    pick = where_equal(iota((size, GROUP), 0) // GROUP, iota((size, GROUP), 1)).astype(jnp.bfloat16)
    place = where_equal(iota((GROUP, size), 0), iota((GROUP, size), 1) % GROUP).astype(jnp.bfloat16)
    wide = dot(dot(pick, m_dec).astype(jnp.bfloat16), place)
    return (wide * where_equal(iota((size, size), 0) % GROUP, iota((size, size), 1) // GROUP)).astype(jnp.bfloat16)


def swap_rows(size_a, size_b):
    size = size_a * size_b
    row, column = iota((size, size), 0), iota((size, size), 1)
    return where_equal((row % size_a) * size_b + row // size_a, column).astype(jnp.bfloat16)


def accumulate(facet_ref, tile_ref, beam_ref, table, dec_back, ra_out, total, group):
    dec_rows = total.shape[1]
    patches = dot(dec_back[group * GROUP * dec_rows : (group + 1) * GROUP * dec_rows], ra_out[...])
    for i in range(GROUP):
        p = group * GROUP + i
        patch = patches[i * dec_rows : (i + 1) * dec_rows]
        patch_grad = (table[beam_ref[p]].astype(jnp.float32) * patch).astype(jnp.bfloat16).astype(jnp.float32)
        tile = 2 * facet_ref[p] + tile_ref[p]
        total[tile] = total[tile] + patch_grad


def run_steps(groups, steps):
    for turn in range(groups + 2*len(steps) - 2):
        for behind, step in reversed(list(enumerate(steps))):
            if 0 <= turn - 2*behind < groups:
                step(turn - 2*behind)


def served_facet(me, index, side):
    chip = (me >> 1) ^ ((index & ~1) + ((me & 1) ^ side))
    return 2 * chip + (index & 1)


def write_sums(total, me_ref, outs, channel):
    tiles, dec_rows, width = total.shape
    from_left = iota((dec_rows, width), 1) % SPAN >= SPAN // 2
    paired = me_ref is not None

    def one_facet(index, carry):
        for side, out_ref in enumerate(outs):
            facet = served_facet(me_ref[0], index, side) if paired else index
            own = 2 * facet
            left, right = lax.rem(own + tiles - 1, tiles), lax.rem(own + 2, tiles)
            out_ref[index, 0, channel] = total[own].astype(out_ref.dtype)
            out_ref[index, 1, channel] = total[own + 1].astype(out_ref.dtype)
            out_ref[index, 2, channel] = jnp.where(from_left, total[left], total[right]).astype(out_ref.dtype)
        return carry

    lax.fori_loop(0, outs[0].shape[0], one_facet, 0, unroll=4)


def vis_copy(vis_ref, held, arrived, channel):
    return pltpu.make_async_copy(vis_ref.at[channel], held.at[channel], arrived.at[channel])


def wait_and_start_next(vis_ref, held, arrived, channel):
    vis_copy(vis_ref, held, arrived, channel).wait()

    @pl.when(channel + 1 < held.shape[0])
    def _():
        vis_copy(vis_ref, held, arrived, channel + 1).start()


def group_data(held, channel, group, columns):
    data = held[channel, :, group * GROUP : (group + 1) * GROUP, columns]
    return data.reshape(-1, data.shape[-1])


def column_blocks(samples):
    return [slice(k, k + COLUMNS) for k in range(0, samples, COLUMNS)]


def first_gradient_kernel(paired, facet_ref, tile_ref, beam_ref, *refs):
    me_ref, refs = (refs[0], refs[1:]) if paired else (None, refs)
    vis_ref, *small_refs = refs[:4]
    outs, refs = refs[4 : 5 + paired], refs[5 + paired :]
    table, back, forward, ra_out, ra_in, total, dec_back, swap, order, beams, m_ra, m_dec, held, arrived, came = refs
    channels, dec_rows, owned, samples = held.shape
    width = m_ra.shape[0]
    beam_count = beams.shape[2]
    size = GROUP * dec_rows
    copies = [
        pltpu.make_async_copy(source, target, came.at[index])
        for index, (source, target) in enumerate(zip(small_refs, (beams, m_ra, m_dec)))
    ]
    for copy in reversed(copies):
        copy.start()
    vis_copy(vis_ref, held, arrived, 0).start()
    order[...] = phase_rows(width)
    swap[...] = swap_rows(dec_rows, beam_count)
    for copy in copies:
        copy.wait()
    back[...] = back_matrix(m_dec[...])
    forward[...] = forward_matrix(m_dec[...])
    ra_out[...] = dot(m_ra[...], order[...], ((0,), (1,))).astype(jnp.bfloat16)
    ra_in[...] = dot(order[...], m_ra[...]).astype(jnp.bfloat16)
    for channel in range(channels):
        swapped = dot(swap[...], beams[channel].reshape(dec_rows * beam_count, width)).astype(jnp.bfloat16)
        ordered = dot(swapped, order[...], ((1,), (1,))).astype(jnp.bfloat16)
        table[channel] = ordered.reshape(beam_count, dec_rows, width)

    def one_channel(channel, carry):
        total[...] = jnp.zeros_like(total)
        wait_and_start_next(vis_ref, held, arrived, channel)

        def go_back(group):
            rows = slice(group * size, (group + 1) * size)
            for columns in column_blocks(samples):
                data = group_data(held, channel, group, columns)
                dec_back[rows, columns] = dot(back[...], data).astype(jnp.bfloat16)

        gather = functools.partial(
            accumulate, facet_ref, tile_ref, beam_ref, table.at[channel], dec_back, ra_out, total
        )
        run_steps(owned // GROUP, [go_back, gather])
        write_sums(total, me_ref, outs, channel)
        return carry

    lax.fori_loop(0, channels, one_channel, 0)


def second_gradient_kernel(paired, facet_ref, tile_ref, beam_ref, *refs):
    me_ref, refs = (refs[0], refs[1:]) if paired else (None, refs)
    vis_ref, table, back, forward, ra_out, ra_in, tiles_ref, *refs = refs
    outs, refs = refs[: 1 + paired], refs[1 + paired :]
    total, rows_k, held, arrived = refs
    channels, dec_rows, owned, samples = held.shape
    size = GROUP * dec_rows
    vis_copy(vis_ref, held, arrived, 0).start()

    def one_channel(channel, carry):
        total[...] = jnp.zeros_like(total)

        def go_in(group):
            weighted = []
            for p in range(group * GROUP, (group + 1) * GROUP):
                facet = facet_ref[p] ^ me_ref[0] if paired else facet_ref[p]
                tile = tiles_ref[(2 * facet + tile_ref[p]) * channels + channel].astype(jnp.float32)
                weighted.append((table[channel, beam_ref[p]].astype(jnp.float32) * tile).astype(jnp.bfloat16))
            weighted = jnp.concatenate(weighted, axis=0)
            for columns in column_blocks(samples):
                along = dot(weighted, ra_in[:, columns]).astype(jnp.bfloat16)
                rows_k[group * size : (group + 1) * size, columns] = along

        def go_forward(group):
            if group == 0:
                wait_and_start_next(vis_ref, held, arrived, channel)
            rows = slice(group * size, (group + 1) * size)
            for columns in column_blocks(samples):
                predicted = dot(forward[...], rows_k[rows, columns])
                data = group_data(held, channel, group, columns).astype(jnp.float32)
                rows_k[rows, columns] = (predicted - data).astype(jnp.bfloat16)

        def go_back(group):
            rows = slice(group * size, (group + 1) * size)
            for columns in column_blocks(samples):
                rows_k[rows, columns] = dot(back[...], rows_k[rows, columns]).astype(jnp.bfloat16)

        gather = functools.partial(
            accumulate, facet_ref, tile_ref, beam_ref, table.at[channel], rows_k, ra_out, total
        )
        run_steps(owned // GROUP, [go_in, go_forward, go_back, gather])
        write_sums(total, me_ref, outs, channel)
        return carry

    lax.fori_loop(0, channels, one_channel, 0)


def gradient_call(scalars, vis, operands, facets, paired, second):
    channels, dec_rows, owned, samples = vis.shape
    width = LANES
    size = GROUP * dec_rows
    bf16 = jnp.bfloat16
    vmem, hbm = pl.BlockSpec(memory_space=pltpu.VMEM), pl.BlockSpec(memory_space=pltpu.HBM)
    kept, sum_type = (facets // 2, jnp.float32) if paired else (facets, bf16)
    out_shapes = [jax.ShapeDtypeStruct((kept, SLOTS, channels, dec_rows, width), sum_type)] * (1 + paired)
    scratch = [
        pltpu.VMEM((2 * facets, dec_rows, width), jnp.float32),
        pltpu.VMEM((owned * dec_rows, samples), bf16),
    ]
    if second:
        in_specs = [hbm] + [vmem] * len(operands)
    else:
        in_specs = [hbm] * (1 + len(operands))
        beam_count = operands[0].shape[2]
        shared = [(channels, beam_count, dec_rows, width), (size, size), (size, size), (samples, width), (width, samples)]
        out_shapes += [jax.ShapeDtypeStruct(shape, bf16) for shape in shared]
        scratch += [pltpu.VMEM((size, size), bf16), pltpu.VMEM((width, width), bf16)]
        scratch += [pltpu.VMEM(operand.shape, bf16) for operand in operands]
    scratch += [pltpu.VMEM(vis.shape, bf16), pltpu.SemaphoreType.DMA((channels,))]
    if not second:
        scratch.append(pltpu.SemaphoreType.DMA((len(operands),)))
    work = channels * owned * samples * dec_rows
    return pl.pallas_call(
        functools.partial(second_gradient_kernel if second else first_gradient_kernel, paired),
        out_shape=out_shapes,
        grid_spec=pltpu.PrefetchScalarGridSpec(
            num_scalar_prefetch=len(scalars),
            grid=(),
            in_specs=in_specs,
            out_specs=[vmem] * len(out_shapes),
            scratch_shapes=scratch,
        ),
        compiler_params=pltpu.CompilerParams(vmem_limit_bytes=40 << 20),
        cost_estimate=pl.CostEstimate(
            flops=(4 if second else 2) * 256 * work, bytes_accessed=2 * work, transcendentals=0
        ),
        name="second_gradient" if second else "first_gradient",
    )(*scalars, vis, *operands)


def shrink(values, bound):
    return values - jnp.clip(values, -bound, bound)


def combine(terms):
    total = None
    for factor, value in terms:
        if factor == 0.0:
            continue
        term = value * jnp.float32(factor)
        total = term if total is None else total + term
    return total


def dec_analysis(rows, low, high):
    count = len(rows)
    half = count // 2
    lows = [combine([(low[j], rows[(2 * k + j) % count]) for j in range(8)]) for k in range(half)]
    highs = [combine([(high[j], rows[(2 * k + j) % count]) for j in range(8)]) for k in range(half)]
    return lows + highs


def dec_synthesis(rows, low, high):
    count = len(rows)
    half = count // 2
    gathered = [[] for _ in range(count)]
    for k in range(half):
        for j in range(8):
            gathered[(2 * k + j) % count].append((low[j], rows[k]))
            gathered[(2 * k + j) % count].append((high[j], rows[half + k]))
    return [combine(terms) for terms in gathered]


def prox_kernel(second, parts, *refs):
    part_refs, (thresholds_ref, step_ref, *refs) = refs[:parts], refs[parts:]
    first_ref, out_ref, summed, columns, natural, tops = refs
    rows = part_refs[0].shape[1]
    dec_rows = first_ref.shape[1]
    channels = step_ref.shape[0]
    half = 4
    shape = (8, LANES)
    upper = iota(shape, 0) >= half
    channel = iota(shape, 0) % half
    lane = iota(shape, 1)
    block = lane // SPAN

    total = part_refs[0][0].astype(jnp.float32)
    for part_ref in part_refs[1:]:
        total = total + part_ref[0].astype(jnp.float32)
    for index in range(1, part_refs[0].shape[0]):
        total = total + part_refs[0][index].astype(jnp.float32)
    summed[:rows] = total
    summed[rows:] = total[rows - channels * dec_rows :]

    def spread(scalars):
        value = jnp.full(shape, scalars[channels - 1], jnp.float32)
        for c in range(channels - 1):
            value = jnp.where(channel == c, scalars[c], value)
        return value

    step = spread([step_ref[c] for c in range(channels)])
    roll = lambda value, shift: pltpu.roll(value, shift % LANES, 1)
    swap = lambda value: pltpu.roll(value, half, 0)
    halves = lambda low, high: jnp.where(upper, high, low)

    for d in range(dec_rows):
        own = summed[pl.ds(d, 8, stride=dec_rows), :]
        edge = summed[pl.ds(8 * dec_rows + d, 8, stride=dec_rows), :]
        other = swap(own)
        own_32, own_64 = roll(own, -32), roll(own, -64)
        other_up, other_64 = roll(other, 32), roll(other, -64)
        edge_32, edge_64, edge_96 = roll(edge, 32), roll(edge, 64), roll(edge, 96)
        evens = jnp.where(
            block == 0,
            halves(own, other_64),
            jnp.where(
                block == 1,
                halves(other_up, own_32),
                jnp.where(block == 2, halves(edge_64, edge), halves(edge_96, edge_32)),
            ),
        )
        odds = jnp.where(
            block == 0,
            halves(own_32, other_up),
            jnp.where(
                block == 1,
                halves(other, own_64),
                jnp.where(block == 2, halves(edge_32, edge_96), halves(edge_64, edge)),
            ),
        )
        evens, odds = step * evens, step * odds
        if second:
            evens, odds = first_ref[0, d] - evens, first_ref[1, d] - odds
        columns[0, d], columns[1, d] = evens, odds
        for e, value in enumerate((evens, odds)):
            later = roll(value, -1)
            middle = swap(halves(later, value))
            columns[2 + e, d] = middle
            columns[4 + e, d] = later
            columns[6 + e, d] = roll(middle, -1)

    low_pass, high_pass = filter_table(BASES)
    for b in range(BASES):
        low, high = [float(v) for v in low_pass[b]], [float(v) for v in high_pass[b]]
        bound = spread([thresholds_ref[b, c] for c in range(channels)]) * step
        ra_low = [combine([(low[j], columns[j, d]) for j in range(8)]) for d in range(dec_rows)]
        ra_high = [combine([(high[j], columns[j, d]) for j in range(8)]) for d in range(dec_rows)]
        coarse_a = dec_analysis(ra_low, low, high)
        coarse_b = [shrink(v, bound) for v in dec_analysis(ra_high, low, high)]
        smooth, detail = coarse_a[: dec_rows // 2], [shrink(v, bound) for v in coarse_a[dec_rows // 2 :]]
        pair = lambda even, odd: jnp.where(upper, jnp.float32(odd), jnp.float32(even))
        pair_sum = lambda values, factors: sum(pair(*f) * v for f, v in zip(factors, values) if f != (0.0, 0.0))
        fine = []
        for value in smooth:
            moved = [value] + [roll(value, -i) for i in (1, 2, 3)]
            lows = pair_sum(moved, [(low[2 * i], low[2 * i + 1]) for i in range(4)])
            highs = pair_sum(moved, [(high[2 * i], high[2 * i + 1]) for i in range(4)])
            fine.append(halves(lows, highs) + swap(halves(highs, lows)))
        fine = [shrink(v, bound) for v in dec_analysis(fine, low, high)]
        fine = dec_synthesis(fine, low, high)
        smooth = []
        for value in fine:
            moved = [value] + [roll(value, i) for i in (1, 2, 3)]
            evens = pair_sum(moved, [(low[2 * i], high[2 * i]) for i in range(4)])
            odds = pair_sum(moved, [(low[2 * i + 1], high[2 * i + 1]) for i in range(4)])
            smooth.append(halves(evens, odds) + swap(halves(odds, evens)))
        top_low = dec_synthesis(smooth + detail, low, high)
        top_high = dec_synthesis(coarse_b, low, high)
        for d in range(dec_rows):
            tops[b, 0, d], tops[b, 1, d] = top_low[d], top_high[d]

    for d in range(dec_rows):
        images = []
        for e in range(2):
            parts = [
                combine(
                    [(float(low_pass[b, 2 * i + e]), tops[b, 0, d]) for b in range(BASES)]
                    + [(float(high_pass[b, 2 * i + e]), tops[b, 1, d]) for b in range(BASES)]
                )
                for i in range(4)
            ]
            other = swap(parts[1] + roll(parts[3], 1))
            value = parts[0] + roll(parts[2], 1) + halves(roll(other, 1), other)
            images.append(jnp.maximum(value * (1.0 / BASES), 0.0))
        evens, odds = images
        if not second:
            first_ref[0, d], first_ref[1, d] = evens, odds
        even_other, odd_other = swap(evens), swap(odds)
        value = jnp.where(
            block == 0,
            halves(evens, roll(even_other, -32)),
            jnp.where(
                block == 1,
                halves(roll(odds, 32), odd_other),
                jnp.where(
                    block == 2,
                    halves(roll(even_other, 64), roll(evens, 32)),
                    halves(roll(odd_other, 96), roll(odds, 64)),
                ),
            ),
        )
        natural[pl.ds(d, 8, stride=dec_rows), :] = value
    if second:
        order = phase_rows(LANES).astype(jnp.float32)
        image = lax.dot_general(
            natural[...],
            order,
            (((1,), (0,)), ((), ())),
            precision=lax.Precision.HIGHEST,
            preferred_element_type=jnp.float32,
        )
        for tile in range(2):
            for c in range(channels):
                start = (tile * channels + c) * dec_rows
                out_ref[c, :, tile * LANES : (tile + 1) * LANES] = image[start : start + dec_rows]
    else:
        out_ref[...] = natural[...].astype(jnp.bfloat16)


def prox_call(received, thresholds, step_size, dec_rows, first=None):
    second = first is not None
    channels = step_size.shape[0]
    received = [part.reshape(-1, SLOTS * channels * dec_rows, LANES) for part in received]
    vmem = pl.BlockSpec(memory_space=pltpu.VMEM)
    smem = pl.BlockSpec(memory_space=pltpu.SMEM)
    held = jax.ShapeDtypeStruct((2, dec_rows, 8, LANES), jnp.float32)
    if second:
        out_shape = jax.ShapeDtypeStruct((channels, dec_rows, RA_DEV), jnp.float32)
        out_specs = vmem
    else:
        out_shape = (held, jax.ShapeDtypeStruct((2 * channels * dec_rows, LANES), jnp.bfloat16))
        out_specs = (vmem, vmem)
    return pl.pallas_call(
        functools.partial(prox_kernel, second, len(received)),
        out_shape=out_shape,
        in_specs=[vmem] * len(received) + [smem, smem] + ([vmem] if second else []),
        out_specs=out_specs,
        scratch_shapes=[
            pltpu.VMEM((4 * channels * dec_rows, LANES), jnp.float32),
            pltpu.VMEM((8, dec_rows, 8, LANES), jnp.float32),
            pltpu.VMEM((2 * channels * dec_rows, LANES), jnp.float32),
            pltpu.VMEM((BASES, 2, dec_rows, 8, LANES), jnp.float32),
        ],
        compiler_params=pltpu.CompilerParams(vmem_limit_bytes=32 << 20),
        name="second_prox" if second else "first_prox",
    )(*received, thresholds, step_size, *([first] if second else []))


def fold_kernel(me_ref, keep_ref, got_ref, own_ref, *outs):
    here = jnp.where(me_ref[0] & 1 == 0, 1.0, 0.0).astype(jnp.float32)
    for parity in range(2):
        own_ref[parity] = here * (keep_ref[parity] + got_ref[parity])
        for z, out_ref in enumerate(outs):
            index = 2 * z + parity
            out_ref[parity] = (keep_ref[index] + got_ref[index]).astype(out_ref.dtype)


def settle_kernel(me_ref, own_ref, *refs):
    *far, mine_ref, theirs_ref = refs
    first, second = (
        own_ref[parity] + sum(far_ref[parity].astype(jnp.float32) for far_ref in far) for parity in range(2)
    )
    even = me_ref[0] & 1 == 0
    mine_ref[0] = jnp.where(even, first, second)
    theirs_ref[0] = jnp.where(even, second, first)


def join_kernel(*refs):
    *parts, out_ref = refs
    start = 0
    for part_ref in parts:
        out_ref[start : start + part_ref.shape[0]] = part_ref[...]
        start += part_ref.shape[0]


def weave_kernel(rows, *refs):
    *parts, out_ref = refs
    for index in range(parts[0].shape[0] // rows):
        for side, part_ref in enumerate(parts):
            start = (2 * index + side) * rows
            out_ref[start : start + rows] = part_ref[index * rows : (index + 1) * rows]


def small_call(kernel, name, out_shape, *operands, scalars=()):
    vmem, smem = pl.BlockSpec(memory_space=pltpu.VMEM), pl.BlockSpec(memory_space=pltpu.SMEM)
    return pl.pallas_call(
        kernel,
        out_shape=out_shape,
        in_specs=[smem] * len(scalars) + [vmem] * len(operands),
        out_specs=jax.tree.map(lambda _: vmem, out_shape),
        compiler_params=pltpu.CompilerParams(vmem_limit_bytes=16 << 20),
        name=name,
    )(*scalars, *operands)


def join(*parts):
    rows = sum(part.shape[0] for part in parts)
    shape = jax.ShapeDtypeStruct((rows,) + parts[0].shape[1:], parts[0].dtype)
    return small_call(join_kernel, "join", shape, *parts)


def across(value, difference):
    count = lax.axis_size("ra")
    return lax.ppermute(value, "ra", [(source, source ^ difference) for source in range(count)])


def pair_exchange(me, keep, send):
    count = lax.axis_size("ra")
    got = across(send, 1)
    shape = (2,) + keep.shape[1:]
    steps = keep.shape[0] // 2
    kinds = [jnp.float32] + [jnp.bfloat16] * steps
    outs = [jax.ShapeDtypeStruct(shape, kind) for kind in kinds]
    own, *parts = small_call(fold_kernel, "fold", outs, keep, got, scalars=[me])
    far = []
    for z in reversed(range(steps)):
        pairs = [(source, source ^ (4 * z + 2 * (source & 1))) for source in range(count)]
        pairs = [(source, target) for source, target in pairs if source != target]
        far.append(lax.ppermute(parts[z], "ra", pairs))
    outs = [jax.ShapeDtypeStruct((1,) + keep.shape[1:], jnp.float32)] * 2
    mine, theirs = small_call(settle_kernel, "settle", outs, own, *far, scalars=[me])
    return [mine, across(theirs, 1)]


def pair_gather(tiles):
    rows = tiles.shape[0]
    tiles = join(tiles, across(tiles, 2))
    far = [across(tiles, difference) for difference in (12, 8, 4)]
    tiles = join(tiles, *reversed(far))
    shape = jax.ShapeDtypeStruct((2 * tiles.shape[0],) + tiles.shape[1:], tiles.dtype)
    return small_call(functools.partial(weave_kernel, rows), "weave", shape, tiles, across(tiles, 1))


def local(vis, beams, m_ra, m_dec, facet_of, tile_of, beam_of, step_size, thresholds):
    facets = lax.axis_size("ra")
    channels, dec_rows, owned, samples = vis.shape
    width = m_ra.shape[0]
    per_facet = RA_DEV // width
    facet_of = facet_of.reshape(owned)
    held = [vis, beams, m_ra, m_dec, facet_of, tile_of, beam_of]
    held = [pltpu.with_memory_space_constraint(array, pltpu.HBM) for array in held]
    vis, beams, m_ra, m_dec, facet_of, tile_of, beam_of = held
    paired = facets == 16
    if paired:
        base = [lax.axis_index("ra").astype(jnp.int32).reshape(1)]
        exchange, gather = functools.partial(pair_exchange, base[0]), pair_gather
    else:
        base = []
        exchange = lambda sums: [lax.all_to_all(sums, "ra", split_axis=0, concat_axis=0, tiled=True)]
        gather = lambda tiles: lax.all_gather(tiles, "ra", axis=0, tiled=True)

    scalars = [facet_of, tile_of, beam_of] + base
    sent = 1 + paired
    sums = gradient_call(scalars, vis, [beams, m_ra, m_dec], facets, paired, False)
    sums, shared = sums[:sent], sums[sent:]
    first, tiles = prox_call(exchange(*sums), thresholds, step_size, dec_rows)
    tiles = gather(tiles).reshape(facets * per_facet * channels, dec_rows, width)
    sums = gradient_call(scalars, vis, [*shared, tiles], facets, paired, True)
    return prox_call(exchange(*sums), thresholds, step_size, dec_rows, first)


def solution(mesh):
    in_specs = (
        P(None, "strip", "ra", None),
        P(None, "strip", None, None),
        P(),
        P(),
        P(("strip", "ra"), None),
        P(("strip", "ra")),
        P(("strip", "ra")),
        P(),
        P(),
    )
    out_specs = P(None, "strip", "ra")
    return jax.shard_map(local, mesh=mesh, in_specs=in_specs, out_specs=out_specs, check_vma=False)
```

```python
import functools

import jax
import jax.numpy as jnp
import numpy as np
from jax import lax
from jax.experimental import pallas as pl
from jax.experimental.pallas import tpu as pltpu
from jax.sharding import PartitionSpec as P

BASES = 4
RA_DEV = 256
GROUP = 16
PHASES = 4
LANES = 128
SPAN = LANES // PHASES
SLOTS = 3
COLUMNS = 256

daub_coeffs = (
    (0.7071067811865476, 0.7071067811865476),
    (0.48296291314453416, 0.8365163037378079, 0.2241438680420134, -0.12940952255126037),
    (
        0.3326705529500825,
        0.8068915093110924,
        0.4598775021184914,
        -0.1350110200102546,
        -0.0854412738820267,
        0.0352262918857095,
    ),
    (
        0.2303778133088964,
        0.7148465705529155,
        0.6308807679298587,
        -0.0279837694168599,
        -0.1870348117190931,
        0.0308413818355607,
        0.0328830116668852,
        -0.010597401785069,
    ),
)


def filter_table(basis_count):
    low_pass = np.zeros((basis_count, 8))
    for basis_id in range(basis_count):
        coeffs = daub_coeffs[basis_id]
        low_pass[basis_id, : len(coeffs)] = coeffs
    high_pass = np.zeros((basis_count, 8))
    for column in range(8):
        high_pass[:, column] = (-1.0) ** column * low_pass[:, 7 - column]
    return low_pass.astype(np.float32), high_pass.astype(np.float32)


def iota(shape, axis):
    return lax.broadcasted_iota(jnp.int32, shape, axis)


def where_equal(left, right):
    return jnp.where(left == right, 1.0, 0.0)


def dot(left, right, contract=((1,), (0,))):
    return lax.dot_general(left, right, (contract, ((), ())), preferred_element_type=jnp.float32)


def phase_rows(width):
    row, column = iota((width, width), 0), iota((width, width), 1)
    span = width // PHASES
    return where_equal(column, PHASES * (row % span) + row // span).astype(jnp.bfloat16)


def back_matrix(m_dec):
    size = GROUP * GROUP
    pick = where_equal(iota((size, GROUP), 0) % GROUP, iota((size, GROUP), 1)).astype(jnp.bfloat16)
    place = where_equal(iota((GROUP, size), 0), iota((GROUP, size), 1) // GROUP).astype(jnp.bfloat16)
    wide = dot(dot(pick, m_dec, ((1,), (1,))).astype(jnp.bfloat16), place)
    return (wide * where_equal(iota((size, size), 0) // GROUP, iota((size, size), 1) % GROUP)).astype(jnp.bfloat16)


def forward_matrix(m_dec):
    size = GROUP * GROUP
    pick = where_equal(iota((size, GROUP), 0) // GROUP, iota((size, GROUP), 1)).astype(jnp.bfloat16)
    place = where_equal(iota((GROUP, size), 0), iota((GROUP, size), 1) % GROUP).astype(jnp.bfloat16)
    wide = dot(dot(pick, m_dec).astype(jnp.bfloat16), place)
    return (wide * where_equal(iota((size, size), 0) % GROUP, iota((size, size), 1) // GROUP)).astype(jnp.bfloat16)


def swap_rows(size_a, size_b):
    size = size_a * size_b
    row, column = iota((size, size), 0), iota((size, size), 1)
    return where_equal((row % size_a) * size_b + row // size_a, column).astype(jnp.bfloat16)


def accumulate(facet_ref, tile_ref, beam_ref, table, dec_back, ra_out, total, group):
    dec_rows = total.shape[1]
    patches = dot(dec_back[group * GROUP * dec_rows : (group + 1) * GROUP * dec_rows], ra_out[...])
    for i in range(GROUP):
        p = group * GROUP + i
        patch = patches[i * dec_rows : (i + 1) * dec_rows]
        patch_grad = (table[beam_ref[p]].astype(jnp.float32) * patch).astype(jnp.bfloat16).astype(jnp.float32)
        tile = 2 * facet_ref[p] + tile_ref[p]
        total[tile] = total[tile] + patch_grad


def run_steps(groups, steps):
    for turn in range(groups + 2*len(steps) - 2):
        for behind, step in reversed(list(enumerate(steps))):
            if 0 <= turn - 2*behind < groups:
                step(turn - 2*behind)


def served_facet(me, index, side):
    chip = (me >> 1) ^ ((index & ~1) + ((me & 1) ^ side))
    return 2 * chip + (index & 1)


def write_sums(total, me_ref, outs, channel):
    tiles, dec_rows, width = total.shape
    from_left = iota((dec_rows, width), 1) % SPAN >= SPAN // 2
    paired = me_ref is not None

    def one_facet(index, carry):
        for side, out_ref in enumerate(outs):
            facet = served_facet(me_ref[0], index, side) if paired else index
            own = 2 * facet
            left, right = lax.rem(own + tiles - 1, tiles), lax.rem(own + 2, tiles)
            out_ref[index, 0, channel] = total[own].astype(out_ref.dtype)
            out_ref[index, 1, channel] = total[own + 1].astype(out_ref.dtype)
            out_ref[index, 2, channel] = jnp.where(from_left, total[left], total[right]).astype(out_ref.dtype)
        return carry

    lax.fori_loop(0, outs[0].shape[0], one_facet, 0, unroll=4)


def vis_copy(vis_ref, held, arrived, channel):
    return pltpu.make_async_copy(vis_ref.at[channel], held.at[channel], arrived.at[channel])


def wait_and_start_next(vis_ref, held, arrived, channel):
    vis_copy(vis_ref, held, arrived, channel).wait()

    @pl.when(channel + 1 < held.shape[0])
    def _():
        vis_copy(vis_ref, held, arrived, channel + 1).start()


def group_data(held, channel, group, columns):
    data = held[channel, :, group * GROUP : (group + 1) * GROUP, columns]
    return data.reshape(-1, data.shape[-1])


def column_blocks(samples):
    return [slice(k, k + COLUMNS) for k in range(0, samples, COLUMNS)]


def first_gradient_kernel(paired, facet_ref, tile_ref, beam_ref, *refs):
    me_ref, refs = (refs[0], refs[1:]) if paired else (None, refs)
    vis_ref, *small_refs = refs[:4]
    outs, refs = refs[4 : 5 + paired], refs[5 + paired :]
    table, back, forward, ra_out, ra_in, total, dec_back, swap, order, beams, m_ra, m_dec, held, arrived, came = refs
    channels, dec_rows, owned, samples = held.shape
    width = m_ra.shape[0]
    beam_count = beams.shape[2]
    size = GROUP * dec_rows
    copies = [
        pltpu.make_async_copy(source, target, came.at[index])
        for index, (source, target) in enumerate(zip(small_refs, (beams, m_ra, m_dec)))
    ]
    for copy in reversed(copies):
        copy.start()
    vis_copy(vis_ref, held, arrived, 0).start()
    order[...] = phase_rows(width)
    swap[...] = swap_rows(dec_rows, beam_count)
    for copy in copies:
        copy.wait()
    back[...] = back_matrix(m_dec[...])
    forward[...] = forward_matrix(m_dec[...])
    ra_out[...] = dot(m_ra[...], order[...], ((0,), (1,))).astype(jnp.bfloat16)
    ra_in[...] = dot(order[...], m_ra[...]).astype(jnp.bfloat16)
    for channel in range(channels):
        swapped = dot(swap[...], beams[channel].reshape(dec_rows * beam_count, width)).astype(jnp.bfloat16)
        ordered = dot(swapped, order[...], ((1,), (1,))).astype(jnp.bfloat16)
        table[channel] = ordered.reshape(beam_count, dec_rows, width)

    def one_channel(channel, carry):
        total[...] = jnp.zeros_like(total)
        wait_and_start_next(vis_ref, held, arrived, channel)

        def go_back(group):
            rows = slice(group * size, (group + 1) * size)
            for columns in column_blocks(samples):
                data = group_data(held, channel, group, columns)
                dec_back[rows, columns] = dot(back[...], data).astype(jnp.bfloat16)

        gather = functools.partial(
            accumulate, facet_ref, tile_ref, beam_ref, table.at[channel], dec_back, ra_out, total
        )
        run_steps(owned // GROUP, [go_back, gather])
        write_sums(total, me_ref, outs, channel)
        return carry

    lax.fori_loop(0, channels, one_channel, 0)


def second_gradient_kernel(paired, facet_ref, tile_ref, beam_ref, *refs):
    me_ref, refs = (refs[0], refs[1:]) if paired else (None, refs)
    vis_ref, table, back, forward, ra_out, ra_in, tiles_ref, *refs = refs
    outs, refs = refs[: 1 + paired], refs[1 + paired :]
    total, rows_k, held, arrived = refs
    channels, dec_rows, owned, samples = held.shape
    size = GROUP * dec_rows
    vis_copy(vis_ref, held, arrived, 0).start()

    def one_channel(channel, carry):
        total[...] = jnp.zeros_like(total)

        def go_in(group):
            weighted = []
            for p in range(group * GROUP, (group + 1) * GROUP):
                facet = facet_ref[p] ^ me_ref[0] if paired else facet_ref[p]
                tile = tiles_ref[(2 * facet + tile_ref[p]) * channels + channel].astype(jnp.float32)
                weighted.append((table[channel, beam_ref[p]].astype(jnp.float32) * tile).astype(jnp.bfloat16))
            weighted = jnp.concatenate(weighted, axis=0)
            for columns in column_blocks(samples):
                along = dot(weighted, ra_in[:, columns]).astype(jnp.bfloat16)
                rows_k[group * size : (group + 1) * size, columns] = along

        def go_forward(group):
            if group == 0:
                wait_and_start_next(vis_ref, held, arrived, channel)
            rows = slice(group * size, (group + 1) * size)
            for columns in column_blocks(samples):
                predicted = dot(forward[...], rows_k[rows, columns])
                data = group_data(held, channel, group, columns).astype(jnp.float32)
                rows_k[rows, columns] = (predicted - data).astype(jnp.bfloat16)

        def go_back(group):
            rows = slice(group * size, (group + 1) * size)
            for columns in column_blocks(samples):
                rows_k[rows, columns] = dot(back[...], rows_k[rows, columns]).astype(jnp.bfloat16)

        gather = functools.partial(
            accumulate, facet_ref, tile_ref, beam_ref, table.at[channel], rows_k, ra_out, total
        )
        run_steps(owned // GROUP, [go_in, go_forward, go_back, gather])
        write_sums(total, me_ref, outs, channel)
        return carry

    lax.fori_loop(0, channels, one_channel, 0)


def gradient_call(scalars, vis, operands, facets, paired, second):
    channels, dec_rows, owned, samples = vis.shape
    width = LANES
    size = GROUP * dec_rows
    bf16 = jnp.bfloat16
    vmem, hbm = pl.BlockSpec(memory_space=pltpu.VMEM), pl.BlockSpec(memory_space=pltpu.HBM)
    kept, sum_type = (facets // 2, jnp.float32) if paired else (facets, bf16)
    out_shapes = [jax.ShapeDtypeStruct((kept, SLOTS, channels, dec_rows, width), sum_type)] * (1 + paired)
    scratch = [
        pltpu.VMEM((2 * facets, dec_rows, width), jnp.float32),
        pltpu.VMEM((owned * dec_rows, samples), bf16),
    ]
    if second:
        in_specs = [hbm] + [vmem] * len(operands)
    else:
        in_specs = [hbm] * (1 + len(operands))
        beam_count = operands[0].shape[2]
        shared = [(channels, beam_count, dec_rows, width), (size, size), (size, size), (samples, width), (width, samples)]
        out_shapes += [jax.ShapeDtypeStruct(shape, bf16) for shape in shared]
        scratch += [pltpu.VMEM((size, size), bf16), pltpu.VMEM((width, width), bf16)]
        scratch += [pltpu.VMEM(operand.shape, bf16) for operand in operands]
    scratch += [pltpu.VMEM(vis.shape, bf16), pltpu.SemaphoreType.DMA((channels,))]
    if not second:
        scratch.append(pltpu.SemaphoreType.DMA((len(operands),)))
    work = channels * owned * samples * dec_rows
    return pl.pallas_call(
        functools.partial(second_gradient_kernel if second else first_gradient_kernel, paired),
        out_shape=out_shapes,
        grid_spec=pltpu.PrefetchScalarGridSpec(
            num_scalar_prefetch=len(scalars),
            grid=(),
            in_specs=in_specs,
            out_specs=[vmem] * len(out_shapes),
            scratch_shapes=scratch,
        ),
        compiler_params=pltpu.CompilerParams(vmem_limit_bytes=40 << 20),
        cost_estimate=pl.CostEstimate(
            flops=(4 if second else 2) * 256 * work, bytes_accessed=2 * work, transcendentals=0
        ),
        name="second_gradient" if second else "first_gradient",
    )(*scalars, vis, *operands)


def shrink(values, bound):
    return values - jnp.clip(values, -bound, bound)


def combine(terms):
    total = None
    for factor, value in terms:
        if factor == 0.0:
            continue
        term = value * jnp.float32(factor)
        total = term if total is None else total + term
    return total


def dec_analysis(rows, low, high):
    count = len(rows)
    half = count // 2
    lows = [combine([(low[j], rows[(2 * k + j) % count]) for j in range(8)]) for k in range(half)]
    highs = [combine([(high[j], rows[(2 * k + j) % count]) for j in range(8)]) for k in range(half)]
    return lows + highs


def dec_synthesis(rows, low, high):
    count = len(rows)
    half = count // 2
    gathered = [[] for _ in range(count)]
    for k in range(half):
        for j in range(8):
            gathered[(2 * k + j) % count].append((low[j], rows[k]))
            gathered[(2 * k + j) % count].append((high[j], rows[half + k]))
    return [combine(terms) for terms in gathered]


def prox_kernel(second, parts, *refs):
    part_refs, (thresholds_ref, step_ref, *refs) = refs[:parts], refs[parts:]
    first_ref, out_ref, summed, columns, natural, tops = refs
    rows = part_refs[0].shape[1]
    dec_rows = first_ref.shape[1]
    channels = step_ref.shape[0]
    half = 4
    shape = (8, LANES)
    upper = iota(shape, 0) >= half
    channel = iota(shape, 0) % half
    lane = iota(shape, 1)
    block = lane // SPAN

    total = part_refs[0][0].astype(jnp.float32)
    for part_ref in part_refs[1:]:
        total = total + part_ref[0].astype(jnp.float32)
    for index in range(1, part_refs[0].shape[0]):
        total = total + part_refs[0][index].astype(jnp.float32)
    summed[:rows] = total
    summed[rows:] = total[rows - channels * dec_rows :]

    def spread(scalars):
        value = jnp.full(shape, scalars[channels - 1], jnp.float32)
        for c in range(channels - 1):
            value = jnp.where(channel == c, scalars[c], value)
        return value

    step = spread([step_ref[c] for c in range(channels)])
    roll = lambda value, shift: pltpu.roll(value, shift % LANES, 1)
    swap = lambda value: pltpu.roll(value, half, 0)
    halves = lambda low, high: jnp.where(upper, high, low)

    for d in range(dec_rows):
        own = summed[pl.ds(d, 8, stride=dec_rows), :]
        edge = summed[pl.ds(8 * dec_rows + d, 8, stride=dec_rows), :]
        other = swap(own)
        own_32, own_64 = roll(own, -32), roll(own, -64)
        other_up, other_64 = roll(other, 32), roll(other, -64)
        edge_32, edge_64, edge_96 = roll(edge, 32), roll(edge, 64), roll(edge, 96)
        evens = jnp.where(
            block == 0,
            halves(own, other_64),
            jnp.where(
                block == 1,
                halves(other_up, own_32),
                jnp.where(block == 2, halves(edge_64, edge), halves(edge_96, edge_32)),
            ),
        )
        odds = jnp.where(
            block == 0,
            halves(own_32, other_up),
            jnp.where(
                block == 1,
                halves(other, own_64),
                jnp.where(block == 2, halves(edge_32, edge_96), halves(edge_64, edge)),
            ),
        )
        evens, odds = step * evens, step * odds
        if second:
            evens, odds = first_ref[0, d] - evens, first_ref[1, d] - odds
        columns[0, d], columns[1, d] = evens, odds
        for e, value in enumerate((evens, odds)):
            later = roll(value, -1)
            middle = swap(halves(later, value))
            columns[2 + e, d] = middle
            columns[4 + e, d] = later
            columns[6 + e, d] = roll(middle, -1)

    low_pass, high_pass = filter_table(BASES)
    for b in range(BASES):
        low, high = [float(v) for v in low_pass[b]], [float(v) for v in high_pass[b]]
        bound = spread([thresholds_ref[b, c] for c in range(channels)]) * step
        ra_low = [combine([(low[j], columns[j, d]) for j in range(8)]) for d in range(dec_rows)]
        ra_high = [combine([(high[j], columns[j, d]) for j in range(8)]) for d in range(dec_rows)]
        coarse_a = dec_analysis(ra_low, low, high)
        coarse_b = [shrink(v, bound) for v in dec_analysis(ra_high, low, high)]
        smooth, detail = coarse_a[: dec_rows // 2], [shrink(v, bound) for v in coarse_a[dec_rows // 2 :]]
        pair = lambda even, odd: jnp.where(upper, jnp.float32(odd), jnp.float32(even))
        pair_sum = lambda values, factors: sum(pair(*f) * v for f, v in zip(factors, values) if f != (0.0, 0.0))
        fine = []
        for value in smooth:
            moved = [value] + [roll(value, -i) for i in (1, 2, 3)]
            lows = pair_sum(moved, [(low[2 * i], low[2 * i + 1]) for i in range(4)])
            highs = pair_sum(moved, [(high[2 * i], high[2 * i + 1]) for i in range(4)])
            fine.append(halves(lows, highs) + swap(halves(highs, lows)))
        fine = [shrink(v, bound) for v in dec_analysis(fine, low, high)]
        fine = dec_synthesis(fine, low, high)
        smooth = []
        for value in fine:
            moved = [value] + [roll(value, i) for i in (1, 2, 3)]
            evens = pair_sum(moved, [(low[2 * i], high[2 * i]) for i in range(4)])
            odds = pair_sum(moved, [(low[2 * i + 1], high[2 * i + 1]) for i in range(4)])
            smooth.append(halves(evens, odds) + swap(halves(odds, evens)))
        top_low = dec_synthesis(smooth + detail, low, high)
        top_high = dec_synthesis(coarse_b, low, high)
        for d in range(dec_rows):
            tops[b, 0, d], tops[b, 1, d] = top_low[d], top_high[d]

    for d in range(dec_rows):
        images = []
        for e in range(2):
            parts = [
                combine(
                    [(float(low_pass[b, 2 * i + e]), tops[b, 0, d]) for b in range(BASES)]
                    + [(float(high_pass[b, 2 * i + e]), tops[b, 1, d]) for b in range(BASES)]
                )
                for i in range(4)
            ]
            other = swap(parts[1] + roll(parts[3], 1))
            value = parts[0] + roll(parts[2], 1) + halves(roll(other, 1), other)
            images.append(jnp.maximum(value * (1.0 / BASES), 0.0))
        evens, odds = images
        if not second:
            first_ref[0, d], first_ref[1, d] = evens, odds
        even_other, odd_other = swap(evens), swap(odds)
        value = jnp.where(
            block == 0,
            halves(evens, roll(even_other, -32)),
            jnp.where(
                block == 1,
                halves(roll(odds, 32), odd_other),
                jnp.where(
                    block == 2,
                    halves(roll(even_other, 64), roll(evens, 32)),
                    halves(roll(odd_other, 96), roll(odds, 64)),
                ),
            ),
        )
        natural[pl.ds(d, 8, stride=dec_rows), :] = value
    if second:
        order = phase_rows(LANES).astype(jnp.float32)
        image = lax.dot_general(
            natural[...],
            order,
            (((1,), (0,)), ((), ())),
            precision=lax.Precision.HIGHEST,
            preferred_element_type=jnp.float32,
        )
        for tile in range(2):
            for c in range(channels):
                start = (tile * channels + c) * dec_rows
                out_ref[c, :, tile * LANES : (tile + 1) * LANES] = image[start : start + dec_rows]
    else:
        out_ref[...] = natural[...].astype(jnp.bfloat16)


def prox_call(received, thresholds, step_size, dec_rows, first=None):
    second = first is not None
    channels = step_size.shape[0]
    received = [part.reshape(-1, SLOTS * channels * dec_rows, LANES) for part in received]
    vmem = pl.BlockSpec(memory_space=pltpu.VMEM)
    smem = pl.BlockSpec(memory_space=pltpu.SMEM)
    held = jax.ShapeDtypeStruct((2, dec_rows, 8, LANES), jnp.float32)
    if second:
        out_shape = jax.ShapeDtypeStruct((channels, dec_rows, RA_DEV), jnp.float32)
        out_specs = vmem
    else:
        out_shape = (held, jax.ShapeDtypeStruct((2 * channels * dec_rows, LANES), jnp.bfloat16))
        out_specs = (vmem, vmem)
    return pl.pallas_call(
        functools.partial(prox_kernel, second, len(received)),
        out_shape=out_shape,
        in_specs=[vmem] * len(received) + [smem, smem] + ([vmem] if second else []),
        out_specs=out_specs,
        scratch_shapes=[
            pltpu.VMEM((4 * channels * dec_rows, LANES), jnp.float32),
            pltpu.VMEM((8, dec_rows, 8, LANES), jnp.float32),
            pltpu.VMEM((2 * channels * dec_rows, LANES), jnp.float32),
            pltpu.VMEM((BASES, 2, dec_rows, 8, LANES), jnp.float32),
        ],
        compiler_params=pltpu.CompilerParams(vmem_limit_bytes=32 << 20),
        name="second_prox" if second else "first_prox",
    )(*received, thresholds, step_size, *([first] if second else []))


def fold_kernel(me_ref, keep_ref, got_ref, own_ref, *outs):
    here = jnp.where(me_ref[0] & 1 == 0, 1.0, 0.0).astype(jnp.float32)
    for parity in range(2):
        own_ref[parity] = here * (keep_ref[parity] + got_ref[parity])
        for z, out_ref in enumerate(outs):
            index = 2 * z + parity
            out_ref[parity] = (keep_ref[index] + got_ref[index]).astype(out_ref.dtype)


def settle_kernel(me_ref, own_ref, *refs):
    *far, mine_ref, theirs_ref = refs
    first, second = (
        own_ref[parity] + sum(far_ref[parity].astype(jnp.float32) for far_ref in far) for parity in range(2)
    )
    even = me_ref[0] & 1 == 0
    mine_ref[0] = jnp.where(even, first, second)
    theirs_ref[0] = jnp.where(even, second, first)


def join_kernel(*refs):
    *parts, out_ref = refs
    start = 0
    for part_ref in parts:
        out_ref[start : start + part_ref.shape[0]] = part_ref[...]
        start += part_ref.shape[0]


def served_kernel(me_ref, own_ref, *refs):
    *far, out_ref = refs
    even = me_ref[0] & 1 == 0
    rows = own_ref.shape[0]
    nearest = jnp.where(even, own_ref[...].astype(jnp.float32), far[0][...].astype(jnp.float32))
    out_ref[:rows] = nearest.astype(out_ref.dtype)
    for z in range(1, len(far)):
        out_ref[z * rows : (z + 1) * rows] = far[z][...]


def weave_kernel(rows, me_ref, mine_ref, theirs_ref, out_ref):
    core = me_ref[0] & 1
    for index in range(mine_ref.shape[0] // rows):
        z, b = index // 2, index % 2
        block = slice(index * rows, (index + 1) * rows)
        start = pl.multiple_of((4 * z + 2 * core + b) * rows, rows)
        out_ref[pl.ds(start, rows)] = mine_ref[block]
        start = pl.multiple_of((4 * z + 2 * (1 - core) + (1 - b)) * rows, rows)
        out_ref[pl.ds(start, rows)] = theirs_ref[block]


def small_call(kernel, name, out_shape, *operands, scalars=()):
    vmem, smem = pl.BlockSpec(memory_space=pltpu.VMEM), pl.BlockSpec(memory_space=pltpu.SMEM)
    return pl.pallas_call(
        kernel,
        out_shape=out_shape,
        in_specs=[smem] * len(scalars) + [vmem] * len(operands),
        out_specs=jax.tree.map(lambda _: vmem, out_shape),
        compiler_params=pltpu.CompilerParams(vmem_limit_bytes=16 << 20),
        name=name,
    )(*scalars, *operands)


def join(*parts):
    rows = sum(part.shape[0] for part in parts)
    shape = jax.ShapeDtypeStruct((rows,) + parts[0].shape[1:], parts[0].dtype)
    return small_call(join_kernel, "join", shape, *parts)


def across(value, difference):
    count = lax.axis_size("ra")
    return lax.ppermute(value, "ra", [(source, source ^ difference) for source in range(count)])


def to_served(value, z):
    count = lax.axis_size("ra")
    pairs = [(source, source ^ (4 * z + 2 * (source & 1))) for source in range(count)]
    return lax.ppermute(value, "ra", [(source, target) for source, target in pairs if source != target])


def pair_exchange(me, keep, send):
    got = across(send, 1)
    shape = (2,) + keep.shape[1:]
    steps = keep.shape[0] // 2
    kinds = [jnp.float32] + [jnp.bfloat16] * steps
    outs = [jax.ShapeDtypeStruct(shape, kind) for kind in kinds]
    own, *parts = small_call(fold_kernel, "fold", outs, keep, got, scalars=[me])
    far = [to_served(parts[z], z) for z in reversed(range(steps))]
    outs = [jax.ShapeDtypeStruct((1,) + keep.shape[1:], jnp.float32)] * 2
    mine, theirs = small_call(settle_kernel, "settle", outs, own, *far, scalars=[me])
    return [mine, across(theirs, 1)]


def pair_gather(me, tiles):
    rows, width = tiles.shape
    facets = lax.axis_size("ra")
    both = join(tiles, across(tiles, 1))
    far = [to_served(both, z) for z in reversed(range(facets // 4))]
    shape = jax.ShapeDtypeStruct((facets // 2 * rows, width), tiles.dtype)
    mine = small_call(served_kernel, "served", shape, both, *reversed(far), scalars=[me])
    shape = jax.ShapeDtypeStruct((facets * rows, width), tiles.dtype)
    weave = functools.partial(weave_kernel, rows)
    return small_call(weave, "weave", shape, mine, across(mine, 1), scalars=[me])


def local(vis, beams, m_ra, m_dec, facet_of, tile_of, beam_of, step_size, thresholds):
    facets = lax.axis_size("ra")
    channels, dec_rows, owned, samples = vis.shape
    width = m_ra.shape[0]
    per_facet = RA_DEV // width
    facet_of = facet_of.reshape(owned)
    held = [vis, beams, m_ra, m_dec, facet_of, tile_of, beam_of]
    held = [pltpu.with_memory_space_constraint(array, pltpu.HBM) for array in held]
    vis, beams, m_ra, m_dec, facet_of, tile_of, beam_of = held
    paired = facets == 16
    if paired:
        base = [lax.axis_index("ra").astype(jnp.int32).reshape(1)]
        exchange, gather = functools.partial(pair_exchange, base[0]), functools.partial(pair_gather, base[0])
    else:
        base = []
        exchange = lambda sums: [lax.all_to_all(sums, "ra", split_axis=0, concat_axis=0, tiled=True)]
        gather = lambda tiles: lax.all_gather(tiles, "ra", axis=0, tiled=True)

    scalars = [facet_of, tile_of, beam_of] + base
    sent = 1 + paired
    sums = gradient_call(scalars, vis, [beams, m_ra, m_dec], facets, paired, False)
    sums, shared = sums[:sent], sums[sent:]
    first, tiles = prox_call(exchange(*sums), thresholds, step_size, dec_rows)
    tiles = gather(tiles).reshape(facets * per_facet * channels, dec_rows, width)
    sums = gradient_call(scalars, vis, [*shared, tiles], facets, paired, True)
    return prox_call(exchange(*sums), thresholds, step_size, dec_rows, first)


def solution(mesh):
    in_specs = (
        P(None, "strip", "ra", None),
        P(None, "strip", None, None),
        P(),
        P(),
        P(("strip", "ra"), None),
        P(("strip", "ra")),
        P(("strip", "ra")),
        P(),
        P(),
    )
    out_specs = P(None, "strip", "ra")
    return jax.shard_map(local, mesh=mesh, in_specs=in_specs, out_specs=out_specs, check_vma=False)
```

```python
import functools

import jax
import jax.numpy as jnp
import numpy as np
from jax import lax
from jax.experimental import pallas as pl
from jax.experimental.pallas import tpu as pltpu
from jax.sharding import PartitionSpec as P

BASES = 4
RA_DEV = 256
GROUP = 16
PHASES = 4
LANES = 128
SPAN = LANES // PHASES
SLOTS = 3
COLUMNS = 256

daub_coeffs = (
    (0.7071067811865476, 0.7071067811865476),
    (0.48296291314453416, 0.8365163037378079, 0.2241438680420134, -0.12940952255126037),
    (
        0.3326705529500825,
        0.8068915093110924,
        0.4598775021184914,
        -0.1350110200102546,
        -0.0854412738820267,
        0.0352262918857095,
    ),
    (
        0.2303778133088964,
        0.7148465705529155,
        0.6308807679298587,
        -0.0279837694168599,
        -0.1870348117190931,
        0.0308413818355607,
        0.0328830116668852,
        -0.010597401785069,
    ),
)


def filter_table(basis_count):
    low_pass = np.zeros((basis_count, 8))
    for basis_id in range(basis_count):
        coeffs = daub_coeffs[basis_id]
        low_pass[basis_id, : len(coeffs)] = coeffs
    high_pass = np.zeros((basis_count, 8))
    for column in range(8):
        high_pass[:, column] = (-1.0) ** column * low_pass[:, 7 - column]
    return low_pass.astype(np.float32), high_pass.astype(np.float32)


def iota(shape, axis):
    return lax.broadcasted_iota(jnp.int32, shape, axis)


def where_equal(left, right):
    return jnp.where(left == right, 1.0, 0.0)


def dot(left, right, contract=((1,), (0,))):
    return lax.dot_general(left, right, (contract, ((), ())), preferred_element_type=jnp.float32)


def phase_rows(width):
    row, column = iota((width, width), 0), iota((width, width), 1)
    span = width // PHASES
    return where_equal(column, PHASES * (row % span) + row // span).astype(jnp.bfloat16)


def back_matrix(m_dec):
    size = GROUP * GROUP
    pick = where_equal(iota((size, GROUP), 0) % GROUP, iota((size, GROUP), 1)).astype(jnp.bfloat16)
    place = where_equal(iota((GROUP, size), 0), iota((GROUP, size), 1) // GROUP).astype(jnp.bfloat16)
    wide = dot(dot(pick, m_dec, ((1,), (1,))).astype(jnp.bfloat16), place)
    return (wide * where_equal(iota((size, size), 0) // GROUP, iota((size, size), 1) % GROUP)).astype(jnp.bfloat16)


def forward_matrix(m_dec):
    size = GROUP * GROUP
    pick = where_equal(iota((size, GROUP), 0) // GROUP, iota((size, GROUP), 1)).astype(jnp.bfloat16)
    place = where_equal(iota((GROUP, size), 0), iota((GROUP, size), 1) % GROUP).astype(jnp.bfloat16)
    wide = dot(dot(pick, m_dec).astype(jnp.bfloat16), place)
    return (wide * where_equal(iota((size, size), 0) % GROUP, iota((size, size), 1) // GROUP)).astype(jnp.bfloat16)


def swap_rows(size_a, size_b):
    size = size_a * size_b
    row, column = iota((size, size), 0), iota((size, size), 1)
    return where_equal((row % size_a) * size_b + row // size_a, column).astype(jnp.bfloat16)


def accumulate(facet_ref, tile_ref, beam_ref, table, dec_back, ra_out, total, group):
    dec_rows = total.shape[1]
    patches = dot(dec_back[group * GROUP * dec_rows : (group + 1) * GROUP * dec_rows], ra_out[...])
    for i in range(GROUP):
        p = group * GROUP + i
        patch = patches[i * dec_rows : (i + 1) * dec_rows]
        patch_grad = (table[beam_ref[p]].astype(jnp.float32) * patch).astype(jnp.bfloat16).astype(jnp.float32)
        tile = 2 * facet_ref[p] + tile_ref[p]
        total[tile] = total[tile] + patch_grad


def run_steps(groups, steps):
    apart = 3 if len(steps) == 2 else 2
    for turn in range(groups + apart * (len(steps) - 1)):
        for behind, step in reversed(list(enumerate(steps))):
            if 0 <= turn - apart * behind < groups:
                step(turn - apart * behind)


def served_facet(me, index, side):
    chip = (me >> 1) ^ ((index & ~1) + ((me & 1) ^ side))
    return 2 * chip + (index & 1)


def write_sums(total, me_ref, outs, channel):
    tiles, dec_rows, width = total.shape
    from_left = iota((dec_rows, width), 1) % SPAN >= SPAN // 2
    paired = me_ref is not None

    def one_facet(index, carry):
        for side, out_ref in enumerate(outs):
            facet = served_facet(me_ref[0], index, side) if paired else index
            own = 2 * facet
            left, right = lax.rem(own + tiles - 1, tiles), lax.rem(own + 2, tiles)
            out_ref[index, 0, channel] = total[own].astype(out_ref.dtype)
            out_ref[index, 1, channel] = total[own + 1].astype(out_ref.dtype)
            out_ref[index, 2, channel] = jnp.where(from_left, total[left], total[right]).astype(out_ref.dtype)
        return carry

    lax.fori_loop(0, outs[0].shape[0], one_facet, 0, unroll=8)


def vis_copy(vis_ref, held, arrived, channel):
    return pltpu.make_async_copy(vis_ref.at[channel], held.at[channel], arrived.at[channel])


def wait_and_start_next(vis_ref, held, arrived, channel):
    vis_copy(vis_ref, held, arrived, channel).wait()

    @pl.when(channel + 1 < held.shape[0])
    def _():
        vis_copy(vis_ref, held, arrived, channel + 1).start()


def group_data(held, channel, group, columns):
    data = held[channel, :, group * GROUP : (group + 1) * GROUP, columns]
    return data.reshape(-1, data.shape[-1])


def column_blocks(samples):
    return [slice(k, k + COLUMNS) for k in range(0, samples, COLUMNS)]


def first_gradient_kernel(paired, facet_ref, tile_ref, beam_ref, *refs):
    me_ref, refs = (refs[0], refs[1:]) if paired else (None, refs)
    vis_ref, *small_refs = refs[:4]
    outs, refs = refs[4 : 5 + paired], refs[5 + paired :]
    table, back, forward, ra_out, ra_in, total, dec_back, swap, order, beams, m_ra, m_dec, held, arrived, came = refs
    channels, dec_rows, owned, samples = held.shape
    width = m_ra.shape[0]
    beam_count = beams.shape[2]
    size = GROUP * dec_rows
    copies = [
        pltpu.make_async_copy(source, target, came.at[index])
        for index, (source, target) in enumerate(zip(small_refs, (beams, m_ra, m_dec)))
    ]
    for copy in reversed(copies):
        copy.start()
    vis_copy(vis_ref, held, arrived, 0).start()
    order[...] = phase_rows(width)
    swap[...] = swap_rows(dec_rows, beam_count)
    for copy in copies:
        copy.wait()
    back[...] = back_matrix(m_dec[...])
    forward[...] = forward_matrix(m_dec[...])
    ra_out[...] = dot(m_ra[...], order[...], ((0,), (1,))).astype(jnp.bfloat16)
    ra_in[...] = dot(order[...], m_ra[...]).astype(jnp.bfloat16)
    for channel in range(channels):
        swapped = dot(swap[...], beams[channel].reshape(dec_rows * beam_count, width)).astype(jnp.bfloat16)
        ordered = dot(swapped, order[...], ((1,), (1,))).astype(jnp.bfloat16)
        table[channel] = ordered.reshape(beam_count, dec_rows, width)

    def one_channel(channel, carry):
        total[...] = jnp.zeros_like(total)
        wait_and_start_next(vis_ref, held, arrived, channel)

        def go_back(group):
            rows = slice(group * size, (group + 1) * size)
            for columns in column_blocks(samples):
                data = group_data(held, channel, group, columns)
                dec_back[rows, columns] = dot(back[...], data).astype(jnp.bfloat16)

        gather = functools.partial(
            accumulate, facet_ref, tile_ref, beam_ref, table.at[channel], dec_back, ra_out, total
        )
        run_steps(owned // GROUP, [go_back, gather])
        write_sums(total, me_ref, outs, channel)
        return carry

    lax.fori_loop(0, channels, one_channel, 0)


def second_gradient_kernel(paired, facet_ref, tile_ref, beam_ref, *refs):
    me_ref, refs = (refs[0], refs[1:]) if paired else (None, refs)
    vis_ref, table, back, forward, ra_out, ra_in, tiles_ref, *refs = refs
    outs, refs = refs[: 1 + paired], refs[1 + paired :]
    total, rows_k, held, arrived = refs
    channels, dec_rows, owned, samples = held.shape
    size = GROUP * dec_rows
    vis_copy(vis_ref, held, arrived, 0).start()

    def one_channel(channel, carry):
        total[...] = jnp.zeros_like(total)

        def go_in(group):
            weighted = []
            for p in range(group * GROUP, (group + 1) * GROUP):
                facet = facet_ref[p] ^ me_ref[0] if paired else facet_ref[p]
                tile = tiles_ref[(2 * facet + tile_ref[p]) * channels + channel].astype(jnp.float32)
                weighted.append((table[channel, beam_ref[p]].astype(jnp.float32) * tile).astype(jnp.bfloat16))
            weighted = jnp.concatenate(weighted, axis=0)
            for columns in column_blocks(samples):
                along = dot(weighted, ra_in[:, columns]).astype(jnp.bfloat16)
                rows_k[group * size : (group + 1) * size, columns] = along

        def go_forward(group):
            if group == 0:
                wait_and_start_next(vis_ref, held, arrived, channel)
            rows = slice(group * size, (group + 1) * size)
            for columns in column_blocks(samples):
                predicted = dot(forward[...], rows_k[rows, columns])
                data = group_data(held, channel, group, columns).astype(jnp.float32)
                rows_k[rows, columns] = (predicted - data).astype(jnp.bfloat16)

        def go_back(group):
            rows = slice(group * size, (group + 1) * size)
            for columns in column_blocks(samples):
                rows_k[rows, columns] = dot(back[...], rows_k[rows, columns]).astype(jnp.bfloat16)

        gather = functools.partial(
            accumulate, facet_ref, tile_ref, beam_ref, table.at[channel], rows_k, ra_out, total
        )
        run_steps(owned // GROUP, [go_in, go_forward, go_back, gather])
        write_sums(total, me_ref, outs, channel)
        return carry

    lax.fori_loop(0, channels, one_channel, 0)


def gradient_call(scalars, vis, operands, facets, paired, second):
    channels, dec_rows, owned, samples = vis.shape
    width = LANES
    size = GROUP * dec_rows
    bf16 = jnp.bfloat16
    vmem, hbm = pl.BlockSpec(memory_space=pltpu.VMEM), pl.BlockSpec(memory_space=pltpu.HBM)
    kept, sum_type = (facets // 2, jnp.float32) if paired else (facets, bf16)
    out_shapes = [jax.ShapeDtypeStruct((kept, SLOTS, channels, dec_rows, width), sum_type)] * (1 + paired)
    scratch = [
        pltpu.VMEM((2 * facets, dec_rows, width), jnp.float32),
        pltpu.VMEM((owned * dec_rows, samples), bf16),
    ]
    if second:
        in_specs = [hbm] + [vmem] * len(operands)
    else:
        in_specs = [hbm] * (1 + len(operands))
        beam_count = operands[0].shape[2]
        shared = [(channels, beam_count, dec_rows, width), (size, size), (size, size), (samples, width), (width, samples)]
        out_shapes += [jax.ShapeDtypeStruct(shape, bf16) for shape in shared]
        scratch += [pltpu.VMEM((size, size), bf16), pltpu.VMEM((width, width), bf16)]
        scratch += [pltpu.VMEM(operand.shape, bf16) for operand in operands]
    scratch += [pltpu.VMEM(vis.shape, bf16), pltpu.SemaphoreType.DMA((channels,))]
    if not second:
        scratch.append(pltpu.SemaphoreType.DMA((len(operands),)))
    work = channels * owned * samples * dec_rows
    return pl.pallas_call(
        functools.partial(second_gradient_kernel if second else first_gradient_kernel, paired),
        out_shape=out_shapes,
        grid_spec=pltpu.PrefetchScalarGridSpec(
            num_scalar_prefetch=len(scalars),
            grid=(),
            in_specs=in_specs,
            out_specs=[vmem] * len(out_shapes),
            scratch_shapes=scratch,
        ),
        compiler_params=pltpu.CompilerParams(vmem_limit_bytes=40 << 20),
        cost_estimate=pl.CostEstimate(
            flops=(4 if second else 2) * 256 * work, bytes_accessed=2 * work, transcendentals=0
        ),
        name="second_gradient" if second else "first_gradient",
    )(*scalars, vis, *operands)


def shrink(values, bound):
    return values - jnp.clip(values, -bound, bound)


def combine(terms):
    total = None
    for factor, value in terms:
        if factor == 0.0:
            continue
        term = value * jnp.float32(factor)
        total = term if total is None else total + term
    return total


def dec_analysis(rows, low, high):
    count = len(rows)
    half = count // 2
    lows = [combine([(low[j], rows[(2 * k + j) % count]) for j in range(8)]) for k in range(half)]
    highs = [combine([(high[j], rows[(2 * k + j) % count]) for j in range(8)]) for k in range(half)]
    return lows + highs


def dec_synthesis(rows, low, high):
    count = len(rows)
    half = count // 2
    gathered = [[] for _ in range(count)]
    for k in range(half):
        for j in range(8):
            gathered[(2 * k + j) % count].append((low[j], rows[k]))
            gathered[(2 * k + j) % count].append((high[j], rows[half + k]))
    return [combine(terms) for terms in gathered]


def prox_kernel(second, parts, *refs):
    part_refs, (thresholds_ref, step_ref, *refs) = refs[:parts], refs[parts:]
    first_ref, out_ref, summed, columns, natural, tops = refs
    rows = part_refs[0].shape[1]
    dec_rows = first_ref.shape[1]
    channels = step_ref.shape[0]
    half = 4
    shape = (8, LANES)
    upper = iota(shape, 0) >= half
    channel = iota(shape, 0) % half
    lane = iota(shape, 1)
    block = lane // SPAN

    total = part_refs[0][0].astype(jnp.float32)
    for part_ref in part_refs[1:]:
        total = total + part_ref[0].astype(jnp.float32)
    for index in range(1, part_refs[0].shape[0]):
        total = total + part_refs[0][index].astype(jnp.float32)
    summed[:rows] = total
    summed[rows:] = total[rows - channels * dec_rows :]

    def spread(scalars):
        value = jnp.full(shape, scalars[channels - 1], jnp.float32)
        for c in range(channels - 1):
            value = jnp.where(channel == c, scalars[c], value)
        return value

    step = spread([step_ref[c] for c in range(channels)])
    roll = lambda value, shift: pltpu.roll(value, shift % LANES, 1)
    swap = lambda value: pltpu.roll(value, half, 0)
    halves = lambda low, high: jnp.where(upper, high, low)

    for d in range(dec_rows):
        own = summed[pl.ds(d, 8, stride=dec_rows), :]
        edge = summed[pl.ds(8 * dec_rows + d, 8, stride=dec_rows), :]
        other = swap(own)
        own_32, own_64 = roll(own, -32), roll(own, -64)
        other_up, other_64 = roll(other, 32), roll(other, -64)
        edge_32, edge_64, edge_96 = roll(edge, 32), roll(edge, 64), roll(edge, 96)
        evens = jnp.where(
            block == 0,
            halves(own, other_64),
            jnp.where(
                block == 1,
                halves(other_up, own_32),
                jnp.where(block == 2, halves(edge_64, edge), halves(edge_96, edge_32)),
            ),
        )
        odds = jnp.where(
            block == 0,
            halves(own_32, other_up),
            jnp.where(
                block == 1,
                halves(other, own_64),
                jnp.where(block == 2, halves(edge_32, edge_96), halves(edge_64, edge)),
            ),
        )
        evens, odds = step * evens, step * odds
        if second:
            evens, odds = first_ref[0, d] - evens, first_ref[1, d] - odds
        columns[0, d], columns[1, d] = evens, odds
        for e, value in enumerate((evens, odds)):
            later = roll(value, -1)
            middle = swap(halves(later, value))
            columns[2 + e, d] = middle
            columns[4 + e, d] = later
            columns[6 + e, d] = roll(middle, -1)

    low_pass, high_pass = filter_table(BASES)
    for b in range(BASES):
        low, high = [float(v) for v in low_pass[b]], [float(v) for v in high_pass[b]]
        bound = spread([thresholds_ref[b, c] for c in range(channels)]) * step
        ra_low = [combine([(low[j], columns[j, d]) for j in range(8)]) for d in range(dec_rows)]
        ra_high = [combine([(high[j], columns[j, d]) for j in range(8)]) for d in range(dec_rows)]
        coarse_a = dec_analysis(ra_low, low, high)
        coarse_b = [shrink(v, bound) for v in dec_analysis(ra_high, low, high)]
        smooth, detail = coarse_a[: dec_rows // 2], [shrink(v, bound) for v in coarse_a[dec_rows // 2 :]]
        pair = lambda even, odd: jnp.where(upper, jnp.float32(odd), jnp.float32(even))
        pair_sum = lambda values, factors: sum(pair(*f) * v for f, v in zip(factors, values) if f != (0.0, 0.0))
        fine = []
        for value in smooth:
            moved = [value] + [roll(value, -i) for i in (1, 2, 3)]
            lows = pair_sum(moved, [(low[2 * i], low[2 * i + 1]) for i in range(4)])
            highs = pair_sum(moved, [(high[2 * i], high[2 * i + 1]) for i in range(4)])
            fine.append(halves(lows, highs) + swap(halves(highs, lows)))
        fine = [shrink(v, bound) for v in dec_analysis(fine, low, high)]
        fine = dec_synthesis(fine, low, high)
        smooth = []
        for value in fine:
            moved = [value] + [roll(value, i) for i in (1, 2, 3)]
            evens = pair_sum(moved, [(low[2 * i], high[2 * i]) for i in range(4)])
            odds = pair_sum(moved, [(low[2 * i + 1], high[2 * i + 1]) for i in range(4)])
            smooth.append(halves(evens, odds) + swap(halves(odds, evens)))
        top_low = dec_synthesis(smooth + detail, low, high)
        top_high = dec_synthesis(coarse_b, low, high)
        for d in range(dec_rows):
            tops[b, 0, d], tops[b, 1, d] = top_low[d], top_high[d]

    for d in range(dec_rows):
        images = []
        for e in range(2):
            parts = [
                combine(
                    [(float(low_pass[b, 2 * i + e]), tops[b, 0, d]) for b in range(BASES)]
                    + [(float(high_pass[b, 2 * i + e]), tops[b, 1, d]) for b in range(BASES)]
                )
                for i in range(4)
            ]
            other = swap(parts[1] + roll(parts[3], 1))
            value = parts[0] + roll(parts[2], 1) + halves(roll(other, 1), other)
            images.append(jnp.maximum(value * (1.0 / BASES), 0.0))
        evens, odds = images
        if not second:
            first_ref[0, d], first_ref[1, d] = evens, odds
        even_other, odd_other = swap(evens), swap(odds)
        value = jnp.where(
            block == 0,
            halves(evens, roll(even_other, -32)),
            jnp.where(
                block == 1,
                halves(roll(odds, 32), odd_other),
                jnp.where(
                    block == 2,
                    halves(roll(even_other, 64), roll(evens, 32)),
                    halves(roll(odd_other, 96), roll(odds, 64)),
                ),
            ),
        )
        natural[pl.ds(d, 8, stride=dec_rows), :] = value
    if second:
        order = phase_rows(LANES).astype(jnp.float32)
        image = lax.dot_general(
            natural[...],
            order,
            (((1,), (0,)), ((), ())),
            precision=lax.Precision.HIGHEST,
            preferred_element_type=jnp.float32,
        )
        for tile in range(2):
            for c in range(channels):
                start = (tile * channels + c) * dec_rows
                out_ref[c, :, tile * LANES : (tile + 1) * LANES] = image[start : start + dec_rows]
    else:
        out_ref[...] = natural[...].astype(jnp.bfloat16)


def prox_call(received, thresholds, step_size, dec_rows, first=None):
    second = first is not None
    channels = step_size.shape[0]
    received = [part.reshape(-1, SLOTS * channels * dec_rows, LANES) for part in received]
    vmem = pl.BlockSpec(memory_space=pltpu.VMEM)
    smem = pl.BlockSpec(memory_space=pltpu.SMEM)
    held = jax.ShapeDtypeStruct((2, dec_rows, 8, LANES), jnp.float32)
    if second:
        out_shape = jax.ShapeDtypeStruct((channels, dec_rows, RA_DEV), jnp.float32)
        out_specs = vmem
    else:
        out_shape = (held, jax.ShapeDtypeStruct((2 * channels * dec_rows, LANES), jnp.bfloat16))
        out_specs = (vmem, vmem)
    return pl.pallas_call(
        functools.partial(prox_kernel, second, len(received)),
        out_shape=out_shape,
        in_specs=[vmem] * len(received) + [smem, smem] + ([vmem] if second else []),
        out_specs=out_specs,
        scratch_shapes=[
            pltpu.VMEM((4 * channels * dec_rows, LANES), jnp.float32),
            pltpu.VMEM((8, dec_rows, 8, LANES), jnp.float32),
            pltpu.VMEM((2 * channels * dec_rows, LANES), jnp.float32),
            pltpu.VMEM((BASES, 2, dec_rows, 8, LANES), jnp.float32),
        ],
        compiler_params=pltpu.CompilerParams(vmem_limit_bytes=32 << 20),
        name="second_prox" if second else "first_prox",
    )(*received, thresholds, step_size, *([first] if second else []))


def fold_kernel(me_ref, keep_ref, got_ref, own_ref, *outs):
    here = jnp.where(me_ref[0] & 1 == 0, 1.0, 0.0).astype(jnp.float32)
    for parity in range(2):
        own_ref[parity] = here * (keep_ref[parity] + got_ref[parity])
        for z, out_ref in enumerate(outs):
            index = 2 * z + parity
            out_ref[parity] = (keep_ref[index] + got_ref[index]).astype(out_ref.dtype)


def settle_kernel(me_ref, own_ref, *refs):
    *far, mine_ref, theirs_ref = refs
    first, second = (
        own_ref[parity] + sum(far_ref[parity].astype(jnp.float32) for far_ref in far) for parity in range(2)
    )
    even = me_ref[0] & 1 == 0
    mine_ref[0] = jnp.where(even, first, second)
    theirs_ref[0] = jnp.where(even, second, first)


def join_kernel(*refs):
    *parts, out_ref = refs
    start = 0
    for part_ref in parts:
        out_ref[start : start + part_ref.shape[0]] = part_ref[...]
        start += part_ref.shape[0]


def served_kernel(me_ref, own_ref, *refs):
    *far, out_ref = refs
    even = me_ref[0] & 1 == 0
    rows = own_ref.shape[0]
    nearest = jnp.where(even, own_ref[...].astype(jnp.float32), far[0][...].astype(jnp.float32))
    out_ref[:rows] = nearest.astype(out_ref.dtype)
    for z in range(1, len(far)):
        out_ref[z * rows : (z + 1) * rows] = far[z][...]


def weave_kernel(rows, me_ref, mine_ref, theirs_ref, out_ref):
    core = me_ref[0] & 1
    for index in range(mine_ref.shape[0] // rows):
        z, b = index // 2, index % 2
        block = slice(index * rows, (index + 1) * rows)
        start = pl.multiple_of((4 * z + 2 * core + b) * rows, rows)
        out_ref[pl.ds(start, rows)] = mine_ref[block]
        start = pl.multiple_of((4 * z + 2 * (1 - core) + (1 - b)) * rows, rows)
        out_ref[pl.ds(start, rows)] = theirs_ref[block]


def small_call(kernel, name, out_shape, *operands, scalars=()):
    vmem, smem = pl.BlockSpec(memory_space=pltpu.VMEM), pl.BlockSpec(memory_space=pltpu.SMEM)
    return pl.pallas_call(
        kernel,
        out_shape=out_shape,
        in_specs=[smem] * len(scalars) + [vmem] * len(operands),
        out_specs=jax.tree.map(lambda _: vmem, out_shape),
        compiler_params=pltpu.CompilerParams(vmem_limit_bytes=16 << 20),
        name=name,
    )(*scalars, *operands)


def join(*parts):
    rows = sum(part.shape[0] for part in parts)
    shape = jax.ShapeDtypeStruct((rows,) + parts[0].shape[1:], parts[0].dtype)
    return small_call(join_kernel, "join", shape, *parts)


def across(value, difference):
    count = lax.axis_size("ra")
    return lax.ppermute(value, "ra", [(source, source ^ difference) for source in range(count)])


def to_served(value, z):
    count = lax.axis_size("ra")
    pairs = [(source, source ^ (4 * z + 2 * (source & 1))) for source in range(count)]
    return lax.ppermute(value, "ra", [(source, target) for source, target in pairs if source != target])


def pair_exchange(me, keep, send):
    got = across(send, 1)
    shape = (2,) + keep.shape[1:]
    steps = keep.shape[0] // 2
    kinds = [jnp.float32] + [jnp.bfloat16] * steps
    outs = [jax.ShapeDtypeStruct(shape, kind) for kind in kinds]
    own, *parts = small_call(fold_kernel, "fold", outs, keep, got, scalars=[me])
    far = [to_served(parts[z], z) for z in reversed(range(steps))]
    outs = [jax.ShapeDtypeStruct((1,) + keep.shape[1:], jnp.float32)] * 2
    mine, theirs = small_call(settle_kernel, "settle", outs, own, *far, scalars=[me])
    return [mine, across(theirs, 1)]


def pair_gather(me, tiles):
    rows, width = tiles.shape
    facets = lax.axis_size("ra")
    both = join(tiles, across(tiles, 1))
    far = [to_served(both, z) for z in reversed(range(facets // 4))]
    shape = jax.ShapeDtypeStruct((facets // 2 * rows, width), tiles.dtype)
    mine = small_call(served_kernel, "served", shape, both, *reversed(far), scalars=[me])
    shape = jax.ShapeDtypeStruct((facets * rows, width), tiles.dtype)
    weave = functools.partial(weave_kernel, rows)
    return small_call(weave, "weave", shape, mine, across(mine, 1), scalars=[me])


def local(vis, beams, m_ra, m_dec, facet_of, tile_of, beam_of, step_size, thresholds):
    facets = lax.axis_size("ra")
    channels, dec_rows, owned, samples = vis.shape
    width = m_ra.shape[0]
    per_facet = RA_DEV // width
    facet_of = facet_of.reshape(owned)
    held = [vis, beams, m_ra, m_dec, facet_of, tile_of, beam_of]
    held = [pltpu.with_memory_space_constraint(array, pltpu.HBM) for array in held]
    vis, beams, m_ra, m_dec, facet_of, tile_of, beam_of = held
    paired = facets == 16
    if paired:
        base = [lax.axis_index("ra").astype(jnp.int32).reshape(1)]
        exchange, gather = functools.partial(pair_exchange, base[0]), functools.partial(pair_gather, base[0])
    else:
        base = []
        exchange = lambda sums: [lax.all_to_all(sums, "ra", split_axis=0, concat_axis=0, tiled=True)]
        gather = lambda tiles: lax.all_gather(tiles, "ra", axis=0, tiled=True)

    scalars = [facet_of, tile_of, beam_of] + base
    sent = 1 + paired
    sums = gradient_call(scalars, vis, [beams, m_ra, m_dec], facets, paired, False)
    sums, shared = sums[:sent], sums[sent:]
    first, tiles = prox_call(exchange(*sums), thresholds, step_size, dec_rows)
    tiles = gather(tiles).reshape(facets * per_facet * channels, dec_rows, width)
    sums = gradient_call(scalars, vis, [*shared, tiles], facets, paired, True)
    return prox_call(exchange(*sums), thresholds, step_size, dec_rows, first)


def solution(mesh):
    in_specs = (
        P(None, "strip", "ra", None),
        P(None, "strip", None, None),
        P(),
        P(),
        P(("strip", "ra"), None),
        P(("strip", "ra")),
        P(("strip", "ra")),
        P(),
        P(),
    )
    out_specs = P(None, "strip", "ra")
    return jax.shard_map(local, mesh=mesh, in_specs=in_specs, out_specs=out_specs, check_vma=False)
```
